256 devices in a mesh: segment: 2 (over y_lo), tm: 8 (over z), rows: 16 (over y_hi, x, core).
Axes of the slice: x: 4, y: 4 (y_hi: 2, y_lo: 2; y = y_hi * 2 + y_lo), z: 8, core: 2. Of those that a mesh axis runs over, the one named last changes fastest.
Arguments:
- input_clip: bfloat16 [16, 32, 128, 128], P('tm', 'rows'), may hold values from -6 to 6
- cotangent: bfloat16 [16, 32, 128, 128], P('tm', 'rows'), may hold values from -0.046875 to 0.046875
- kernel_in: bfloat16 [2, 3456, 256], P('segment'), may hold values from -0.109375 to 0.109375
- kernel_out: bfloat16 [2, 6912, 128], P('segment'), may hold values from -0.078125 to 0.078125
Outputs:
- sections: bfloat16 [2, 16, 32, 128, 128], P('segment', 'tm', 'rows')
- grad_in: float32 [2, 884736], P('segment', ('tm', 'rows'))
- grad_out: float32 [2, 884736], P('segment', ('tm', 'rows'))
The draws below stay inside these ranges and needn't reach their ends.
All inputs are finite; a program needn't handle non-finite values.
Results may differ from the reference program's by a relative error of at most 0.007.
Values may be sent and summed in bfloat16 or wider, within the bound.
A program may use at most 128 MiB of HBM per device.

```python
import jax
import jax.numpy as jnp
from jax import lax

CH = 128
HID = 256
WID = 128
FRAMES = 16
HEIGHT = 32


def steps_of(rng, dims, split, low, largest):
    def one(axis_at, blocks):
        heights = jax.random.uniform(jax.random.fold_in(jax.random.fold_in(rng, 6), axis_at), (blocks,), jnp.float32, low / len(split), largest / len(split))
        return jnp.repeat(jnp.exp(heights), dims[axis_at] // blocks).reshape((-1,) + (1,) * (len(dims) - axis_at - 1))

    loudness = one(*split[0])
    for cut in split[1:]:
        loudness = loudness * one(*cut)
    return loudness


def centred(own_key, dims, scale, limit, cuts=(), held_as=jnp.bfloat16):
    gain = steps_of(own_key, dims, cuts, -0.22, 0.18) if cuts else 1.0
    array = jax.random.normal(own_key, dims, jnp.float32) * scale * gain
    return jnp.minimum(jnp.maximum(array, -limit), limit).astype(held_as)


def setup_inputs(seed: int = 0) -> dict:
    seeds = jax.random.split(jax.random.key(seed), 5)
    input_clip = centred(seeds[0], (FRAMES, HEIGHT, WID, CH), 1.0, 6.0, ((0, 8), (1, 16)))
    cotangent = centred(seeds[1], (FRAMES, HEIGHT, WID, CH), (2.0 / (FRAMES * HEIGHT * WID) ** 0.5), 0.046875, ((0, 8), (1, 16)))
    kernel_in = centred(seeds[2], (2, 27 * CH, HID), (27 * CH) ** -0.5, 0.109375, ((0, 2),))
    kernel_out = centred(seeds[3], (2, 27 * HID, CH), (27 * HID) ** -0.5, 0.078125, ((0, 2),))
    return {"input_clip": input_clip, "cotangent": cotangent, "kernel_in": kernel_in, "kernel_out": kernel_out}


def causal_conv(volume, kernel):
    frames, height, width, channels = volume.shape
    padded = jnp.pad(volume, ((2, 0), (1, 1), (1, 1), (0, 0)))
    blocks = kernel.reshape(27, channels, -1)
    summed = jnp.zeros((frames * height * width, blocks.shape[2]), jnp.float32)
    for depth in range(3):
        for row_step in range(3):
            for col_step in range(3):
                window = padded[depth:depth + frames, row_step:row_step + height, col_step:col_step + width]
                summed = summed + jnp.dot(window.reshape(-1, channels), blocks[9 * depth + 3 * row_step + col_step], preferred_element_type=jnp.float32)
    return summed.reshape(frames, height, width, -1)

def conv_transpose(volume, kernel):
    frames, height, width, channels = volume.shape
    padded = jnp.pad(volume, ((0, 2), (1, 1), (1, 1), (0, 0)))
    blocks = kernel.reshape(27, -1, channels)
    summed = jnp.zeros((frames * height * width, blocks.shape[1]), jnp.float32)
    for depth in range(3):
        for row_step in range(3):
            for col_step in range(3):
                window = padded[2 - depth:2 - depth + frames, 2 - row_step:2 - row_step + height, 2 - col_step:2 - col_step + width]
                summed = summed + jnp.dot(window.reshape(-1, channels), blocks[9 * depth + 3 * row_step + col_step].T, preferred_element_type=jnp.float32)
    return summed.reshape(frames, height, width, -1)

def weight_grad(volume, upstream):
    frames, height, width, channels = volume.shape
    padded = jnp.pad(volume, ((2, 0), (1, 1), (1, 1), (0, 0)))
    flat_up = upstream.reshape(frames * height * width, -1)
    pieces = []
    for depth in range(3):
        for row_step in range(3):
            for col_step in range(3):
                window = padded[depth:depth + frames, row_step:row_step + height, col_step:col_step + width]
                pieces.append(lax.dot_general(window.reshape(-1, channels), flat_up, (((0,), (0,)), ((), ())), preferred_element_type=jnp.float32))
    return jnp.stack(pieces).reshape(-1)

def section(volume, kernel_a, kernel_b):
    hidden = causal_conv(volume, kernel_a)
    active = jax.nn.silu(hidden).astype(jnp.bfloat16)
    result = (volume.astype(jnp.float32) + causal_conv(active, kernel_b)).astype(jnp.bfloat16)
    return (result, hidden, active)

def gate_grad(upstream, hidden):
    sigmoid_h = jax.nn.sigmoid(hidden)
    return (upstream * sigmoid_h * (1.0 + hidden * (1.0 - sigmoid_h))).astype(jnp.bfloat16)

def reference(input_clip, cotangent, kernel_in, kernel_out):
    enc_out, enc_hidden, enc_active = section(input_clip, kernel_in[0], kernel_out[0])
    dec_out, dec_hidden, dec_active = section(enc_out, kernel_in[1], kernel_out[1])
    dec_gated = gate_grad(conv_transpose(cotangent, kernel_out[1]), dec_hidden)
    passed = (cotangent.astype(jnp.float32) + conv_transpose(dec_gated, kernel_in[1])).astype(jnp.bfloat16)
    enc_gated = gate_grad(conv_transpose(passed, kernel_out[0]), enc_hidden)
    grad_in = jnp.stack([weight_grad(input_clip, enc_gated), weight_grad(enc_out, dec_gated)])
    grad_out = jnp.stack([weight_grad(enc_active, passed), weight_grad(dec_active, cotangent)])
    return (jnp.stack([enc_out, dec_out]), grad_in, grad_out)
```

```python
from functools import partial

import jax
import jax.numpy as jnp
from jax import lax
from jax.experimental import pallas as pl
from jax.experimental.pallas import tpu as pltpu
from jax.sharding import PartitionSpec as P


def padded_2(cells, sides, width):
    for axis, dim in sides:
        count = lax.axis_size(axis)
        ends = count - 1
        head = lax.slice_in_dim(cells, 0, width, axis=dim)
        tail = lax.slice_in_dim(cells, cells.shape[dim] - width, cells.shape[dim], axis=dim)
        cells = jnp.concatenate(
            [
                lax.ppermute(tail, axis, [(i, (i + 1) % count) for i in range(ends)]),
                cells,
                lax.ppermute(head, axis, [((i + 1) % count, i) for i in range(ends)]),
            ],
            axis=dim,
        )
    return cells


def passed_along(block, axis, distance):
    devices = range(lax.axis_size(axis))
    route = [(i - distance, i) for i in devices if i - distance in devices]
    return lax.ppermute(block, axis, route)


def swapped(block, axis, apart):
    count = lax.axis_size(axis)
    route = []
    for low in range(count):
        high = low | 1 << apart
        if high != low and high < count:
            route += [(low, high), (high, low)]
    return lax.ppermute(block, axis, route)


def extend_rims(longer):
    widened = padded_2(longer, (("rows", 1),), 1)
    extended = jnp.pad(widened, ((0, 0), (0, 0), (1, 1), (0, 0)))
    return extended


def past_padded(volume):
    before = passed_along(volume, "tm", 1)
    return extend_rims(jnp.concatenate([before, volume], axis=0))


def future_padded(volume):
    after = passed_along(volume, "tm", -1)
    return extend_rims(jnp.concatenate([volume, after], axis=0))


def tap_matrix(padded, shape, reverse):
    frames, height, width = (shape[0], shape[1], shape[2])
    columns = []
    for depth in range(3):
        for row_step in range(3):
            for col_step in range(3):
                if reverse:
                    lead, mid, tail = (2 - depth, 2 - row_step, 2 - col_step)
                else:
                    lead, mid, tail = (depth, row_step, col_step)
                columns.append(
                    padded[lead : lead + frames, mid : mid + height, tail : tail + width, :]
                )
    stacked = jnp.concatenate(columns, axis=3)
    return stacked.reshape(frames * height * width, -1)


def flipped(kernel, inputs):
    return kernel.reshape(27, inputs, -1).transpose(0, 2, 1).reshape(-1, inputs)


def gate_grad(upstream, hidden):
    sigmoid_h = jax.nn.sigmoid(hidden)
    return (upstream * sigmoid_h * (1.0 + hidden * (1.0 - sigmoid_h))).astype(jnp.bfloat16)


def masked_dot(flag, taps, kernel):
    return lax.cond(
        flag,
        lambda: jnp.dot(taps, kernel, preferred_element_type=jnp.float32),
        lambda: jnp.zeros((taps.shape[0], kernel.shape[1]), jnp.float32),
    )


def forward(volume, kernel_a, kernel_b, product):
    shape = volume.shape
    first_taps = tap_matrix(past_padded(volume), shape, False)
    hidden = product(first_taps, kernel_a)
    active = jax.nn.silu(hidden).astype(jnp.bfloat16).reshape(shape[0], shape[1], shape[2], -1)
    second_taps = tap_matrix(past_padded(active), shape, False)
    branch = product(second_taps, kernel_b)
    result = (
        (volume.reshape(-1, shape[3]).astype(jnp.float32) + branch)
        .astype(jnp.bfloat16)
        .reshape(shape)
    )
    return (result, first_taps, hidden, active, second_taps)


def contract(taps, upstream):
    return lax.dot_general(
        taps, upstream, (((0,), (0,)), ((), ())), preferred_element_type=jnp.float32
    ).reshape(-1)


def across(volume):
    return swapped(volume, "segment", 0)


MESH_ID = pl.DeviceIdType.MESH
CORES, XS, YS, ZS = 2, 4, 2, 8
CHUNK = 112


def reduce_scatter_kernel(
    b_ref, in_ref, out_ref, got_core, half, got_x, mine, quarter, got_z, last, got_y,
    send_core, recv_core, send_x, recv_x, send_z, recv_z, send_y, recv_y,
):
    row = lax.axis_index("rows")
    tm = lax.axis_index("tm")
    core = lax.rem(row, 2)
    at_x = lax.rem(row // 2, 4)
    at_y = row // 8

    def row_of(y, x, c):
        return y * 8 + x * 2 + c

    def x_at(offset):
        return lax.rem(at_x + offset, XS)

    def z_at(offset):
        return lax.rem(tm + offset, ZS)

    sibling = {"rows": row_of(at_y, at_x, 1 - core)}
    across_y = {"rows": row_of(1 - at_y, at_x, core)}
    barrier = pltpu.get_barrier_semaphore()
    partners = [sibling, across_y]
    partners += [{"rows": row_of(at_y, x_at(o), core)} for o in range(1, XS)]
    partners += [{"tm": z_at(p)} for p in range(1, ZS)]
    for partner in partners:
        pl.semaphore_signal(barrier, inc=1, device_id=partner, device_id_type=MESH_ID)
    pl.semaphore_wait(barrier, len(partners))

    order = (2, 1, 3, 0)
    core_copies = {}
    for o in order:
        copy = pltpu.make_async_remote_copy(
            src_ref=b_ref.at[:, :, x_at(o), 1 - core],
            dst_ref=got_core.at[o],
            send_sem=send_core.at[o],
            recv_sem=recv_core.at[o],
            device_id=sibling,
            device_id_type=MESH_ID,
        )
        copy.start()
        core_copies[o] = copy
    x_copies = []
    for o in order:
        core_copies[o].wait_recv()
        x = x_at(o)

        def add_core(z, carry, o=o, x=x):
            total = b_ref[z, :, x, core].astype(jnp.float32) + got_core[o, z].astype(jnp.float32)
            if o == 0:
                mine[z] = total
            else:
                half[o, z] = total.astype(jnp.bfloat16)
            return carry

        lax.fori_loop(0, ZS, add_core, 0)
        if o:
            copy = pltpu.make_async_remote_copy(
                src_ref=half.at[o],
                dst_ref=got_x.at[o],
                send_sem=send_x.at[o],
                recv_sem=recv_x.at[o],
                device_id={"rows": row_of(at_y, x, core)},
                device_id_type=MESH_ID,
            )
            copy.start()
            x_copies.append(copy)
    for copy in x_copies:
        copy.wait_recv()
    z_copies = []
    for p in (4, 3, 5, 2, 6, 1, 7, 0):
        z = z_at(p)
        total = mine[z]
        for o in range(1, XS):
            total = total + got_x[o, z].astype(jnp.float32)
        if p == 0:
            mine[z] = total
        else:
            quarter[p] = total.astype(jnp.bfloat16)
            copy = pltpu.make_async_remote_copy(
                src_ref=quarter.at[p],
                dst_ref=got_z.at[p],
                send_sem=send_z.at[p],
                recv_sem=recv_z.at[p],
                device_id={"tm": z},
                device_id_type=MESH_ID,
            )
            copy.start()
            z_copies.append(copy)
    for copy in z_copies:
        copy.wait_recv()
    for side in range(YS):
        total = mine[tm, side]
        for p in range(1, ZS):
            total = total + got_z[p, side].astype(jnp.float32)
        mine[tm, side] = total
    last[...] = mine[tm, 1 - at_y].astype(jnp.bfloat16)
    copy = pltpu.make_async_remote_copy(
        src_ref=last,
        dst_ref=got_y,
        send_sem=send_y,
        recv_sem=recv_y,
        device_id=across_y,
        device_id_type=MESH_ID,
    )
    copy.start()
    copy.wait_recv()
    total = mine[tm, at_y] + got_y[...].astype(jnp.float32)
    in_ref[:, 0:128] = total[0:27]
    in_ref[:, 128:256] = total[27:54]
    out_ref[...] = total[54:108]
    for copy in [core_copies[o] for o in order] + x_copies + z_copies + [copy]:
        copy.wait_send()


def reduce_scatter(blocks):
    whole = pl.BlockSpec(memory_space=pltpu.VMEM)
    tile = (CHUNK, 128)
    dma = pltpu.SemaphoreType.DMA
    return pl.pallas_call(
        reduce_scatter_kernel,
        out_shape=(
            jax.ShapeDtypeStruct((27, 256), jnp.float32),
            jax.ShapeDtypeStruct((54, 128), jnp.float32),
        ),
        in_specs=[whole],
        out_specs=(whole, whole),
        scratch_shapes=[
            pltpu.VMEM((XS, ZS, YS) + tile, jnp.bfloat16),
            pltpu.VMEM((XS, ZS, YS) + tile, jnp.bfloat16),
            pltpu.VMEM((XS, ZS, YS) + tile, jnp.bfloat16),
            pltpu.VMEM((ZS, YS) + tile, jnp.float32),
            pltpu.VMEM((ZS, YS) + tile, jnp.bfloat16),
            pltpu.VMEM((ZS, YS) + tile, jnp.bfloat16),
            pltpu.VMEM(tile, jnp.bfloat16),
            pltpu.VMEM(tile, jnp.bfloat16),
            dma((XS,)), dma((XS,)), dma((XS,)), dma((XS,)), dma((ZS,)), dma((ZS,)), dma, dma,
        ],
        compiler_params=pltpu.CompilerParams(
            collective_id=0, has_side_effects=True, vmem_limit_bytes=40 << 20
        ),
    )(blocks)


def chunked(in_term, out_term):
    ins = in_term.reshape(128, 27, 2, 128).transpose(0, 2, 1, 3).reshape(128, 54, 128)
    outs = out_term.reshape(128, 54, 128)
    both = jnp.concatenate([ins, outs], axis=1).astype(jnp.bfloat16)
    padded = jnp.pad(both, ((0, 0), (0, CHUNK - 108), (0, 0)))
    return padded.reshape(ZS, YS, XS, CORES, CHUNK, 128)


def relay_plan(input_clip, cotangent, kernel_in, kernel_out):
    kernel_a = kernel_in[0]
    kernel_b = kernel_out[0]
    shape = input_clip.shape
    channels = shape[3]
    hidden_width = kernel_a.shape[1]
    on_encoder = lax.axis_index("segment") == 0
    on_decoder = jnp.logical_not(on_encoder)
    enc_dot = partial(masked_dot, on_encoder)
    dec_dot = partial(masked_dot, on_decoder)
    enc_result, enc_first, enc_hidden, enc_active, enc_second = forward(
        input_clip, kernel_a, kernel_b, enc_dot
    )
    linked = across(enc_result)
    dec_result, dec_first, dec_hidden, dec_active, dec_second = forward(
        linked, kernel_a, kernel_b, dec_dot
    )
    sections = jnp.where(on_encoder, enc_result, dec_result)
    role_hidden = jnp.where(on_encoder, enc_hidden, dec_hidden)
    back_out = flipped(kernel_b, hidden_width)
    back_in = flipped(kernel_a, channels)
    upstream = dec_dot(tap_matrix(future_padded(cotangent), shape, True), back_out)
    gated = gate_grad(upstream, dec_hidden).reshape(shape[0], shape[1], shape[2], -1)
    inner = dec_dot(tap_matrix(future_padded(gated), shape, True), back_in)
    passed = (
        (cotangent.reshape(-1, channels).astype(jnp.float32) + inner)
        .astype(jnp.bfloat16)
        .reshape(shape)
    )
    returned = across(passed)
    role_grad = jnp.where(on_encoder, returned, cotangent)
    enc_upstream = enc_dot(tap_matrix(future_padded(returned), shape, True), back_out)
    role_upstream = jnp.where(on_encoder, enc_upstream, upstream)
    role_gated = gate_grad(role_upstream, role_hidden)
    first_role = jnp.where(on_encoder, enc_first, dec_first)
    second_role = jnp.where(on_encoder, enc_second, dec_second)
    out_term = contract(second_role, role_grad.reshape(-1, channels))
    in_term = contract(first_role, role_gated)
    in_sum, out_sum = reduce_scatter(chunked(in_term, out_term))
    return (sections[None], in_sum.reshape(1, -1), out_sum.reshape(1, -1))


def on_device(input_clip, cotangent, kernel_in, kernel_out):
    outputs = relay_plan(input_clip, cotangent, kernel_in, kernel_out)
    return outputs


def solution(mesh):
    in_specs = (
        P("tm", "rows", None, None),
        P("tm", "rows", None, None),
        P("segment", None, None),
        P("segment", None, None),
    )
    out_specs = (
        P("segment", "tm", "rows", None, None),
        P("segment", ("tm", "rows")),
        P("segment", ("tm", "rows")),
    )
    return jax.shard_map(
        on_device, mesh=mesh, in_specs=in_specs, out_specs=out_specs, check_vma=False
    )
```

```python
from functools import partial

import jax
import jax.numpy as jnp
from jax import lax
from jax.experimental import pallas as pl
from jax.experimental.pallas import tpu as pltpu
from jax.sharding import PartitionSpec as P

MESH_ID = pl.DeviceIdType.MESH
CORES, XS, YS, ZS = 2, 4, 2, 8
CHUNK = 112


def reduce_scatter_kernel(
    b_ref, in_ref, out_ref, got_core, half, got_x, mine, quarter, got_z, last, got_y,
    send_core, recv_core, send_x, recv_x, send_z, recv_z, send_y, recv_y,
):
    row = lax.axis_index("rows")
    tm = lax.axis_index("tm")
    core = lax.rem(row, 2)
    at_x = lax.rem(row // 2, 4)
    at_y = row // 8

    def row_of(y, x, c):
        return y * 8 + x * 2 + c

    def x_at(offset):
        return lax.rem(at_x + offset, XS)

    def z_at(offset):
        return lax.rem(tm + offset, ZS)

    sibling = {"rows": row_of(at_y, at_x, 1 - core)}
    across_y = {"rows": row_of(1 - at_y, at_x, core)}
    barrier = pltpu.get_barrier_semaphore()
    partners = [sibling, across_y]
    partners += [{"rows": row_of(at_y, x_at(o), core)} for o in range(1, XS)]
    partners += [{"tm": z_at(p)} for p in range(1, ZS)]
    for partner in partners:
        pl.semaphore_signal(barrier, inc=1, device_id=partner, device_id_type=MESH_ID)
    pl.semaphore_wait(barrier, len(partners))

    order = (2, 1, 3, 0)
    core_copies = {}
    for o in order:
        copy = pltpu.make_async_remote_copy(
            src_ref=b_ref.at[:, :, x_at(o), 1 - core],
            dst_ref=got_core.at[o],
            send_sem=send_core.at[o],
            recv_sem=recv_core.at[o],
            device_id=sibling,
            device_id_type=MESH_ID,
        )
        copy.start()
        core_copies[o] = copy
    x_copies = []
    for o in order:
        core_copies[o].wait_recv()
        x = x_at(o)

        def add_core(z, carry, o=o, x=x):
            total = b_ref[z, :, x, core].astype(jnp.float32) + got_core[o, z].astype(jnp.float32)
            if o == 0:
                mine[z] = total
            else:
                half[o, z] = total.astype(jnp.bfloat16)
            return carry

        lax.fori_loop(0, ZS, add_core, 0)
        if o:
            copy = pltpu.make_async_remote_copy(
                src_ref=half.at[o],
                dst_ref=got_x.at[o],
                send_sem=send_x.at[o],
                recv_sem=recv_x.at[o],
                device_id={"rows": row_of(at_y, x, core)},
                device_id_type=MESH_ID,
            )
            copy.start()
            x_copies.append(copy)
    for copy in x_copies:
        copy.wait_recv()
    z_copies = []
    for p in (4, 3, 5, 2, 6, 1, 7, 0):
        z = z_at(p)
        total = mine[z]
        for o in range(1, XS):
            total = total + got_x[o, z].astype(jnp.float32)
        if p == 0:
            mine[z] = total
        else:
            quarter[p] = total.astype(jnp.bfloat16)
            copy = pltpu.make_async_remote_copy(
                src_ref=quarter.at[p],
                dst_ref=got_z.at[p],
                send_sem=send_z.at[p],
                recv_sem=recv_z.at[p],
                device_id={"tm": z},
                device_id_type=MESH_ID,
            )
            copy.start()
            z_copies.append(copy)
    for copy in z_copies:
        copy.wait_recv()
    for side in range(YS):
        total = mine[tm, side]
        for p in range(1, ZS):
            total = total + got_z[p, side].astype(jnp.float32)
        mine[tm, side] = total
    last[...] = mine[tm, 1 - at_y].astype(jnp.bfloat16)
    copy = pltpu.make_async_remote_copy(
        src_ref=last,
        dst_ref=got_y,
        send_sem=send_y,
        recv_sem=recv_y,
        device_id=across_y,
        device_id_type=MESH_ID,
    )
    copy.start()
    copy.wait_recv()
    total = mine[tm, at_y] + got_y[...].astype(jnp.float32)
    in_ref[:, 0:128] = total[0:27]
    in_ref[:, 128:256] = total[27:54]
    out_ref[...] = total[54:108]
    for copy in [core_copies[o] for o in order] + x_copies + z_copies + [copy]:
        copy.wait_send()


def reduce_scatter(blocks):
    whole = pl.BlockSpec(memory_space=pltpu.VMEM)
    tile = (CHUNK, 128)
    dma = pltpu.SemaphoreType.DMA
    return pl.pallas_call(
        reduce_scatter_kernel,
        out_shape=(
            jax.ShapeDtypeStruct((27, 256), jnp.float32),
            jax.ShapeDtypeStruct((54, 128), jnp.float32),
        ),
        in_specs=[whole],
        out_specs=(whole, whole),
        scratch_shapes=[
            pltpu.VMEM((XS, ZS, YS) + tile, jnp.bfloat16),
            pltpu.VMEM((XS, ZS, YS) + tile, jnp.bfloat16),
            pltpu.VMEM((XS, ZS, YS) + tile, jnp.bfloat16),
            pltpu.VMEM((ZS, YS) + tile, jnp.float32),
            pltpu.VMEM((ZS, YS) + tile, jnp.bfloat16),
            pltpu.VMEM((ZS, YS) + tile, jnp.bfloat16),
            pltpu.VMEM(tile, jnp.bfloat16),
            pltpu.VMEM(tile, jnp.bfloat16),
            dma((XS,)), dma((XS,)), dma((XS,)), dma((XS,)), dma((ZS,)), dma((ZS,)), dma, dma,
        ],
        compiler_params=pltpu.CompilerParams(
            collective_id=0, has_side_effects=True, vmem_limit_bytes=40 << 20
        ),
    )(blocks)


def shifted(line, by):
    rows = lax.broadcasted_iota(jnp.int32, line.shape, 0)
    if by == 1:
        return jnp.where(rows == 0, 0.0, pltpu.roll(line, 1, 0))
    return jnp.where(rows == 127, 0.0, pltpu.roll(line, 127, 0))


def joined(low, mid, high, reverse):
    if reverse:
        return shifted(low, -1) + mid + shifted(high, 1)
    return shifted(low, 1) + mid + shifted(high, -1)


class Link:
    def __init__(self, src, dst, sems, index, device, sends, receives):
        self.parts = (src, dst, sems[0].at[index], sems[1].at[index], device)
        self.sends = sends
        self.receives = receives

    def copy(self):
        src, dst, send_sem, recv_sem, device = self.parts
        return pltpu.make_async_remote_copy(
            src_ref=src, dst_ref=dst, send_sem=send_sem, recv_sem=recv_sem,
            device_id=device, device_id_type=MESH_ID,
        )

    def start(self):
        @pl.when(self.sends)
        def _():
            self.copy().start()

    def wait_recv(self):
        @pl.when(self.receives)
        def _():
            self.copy().wait_recv()

    def wait_send(self):
        @pl.when(self.sends)
        def _():
            self.copy().wait_send()


def front_kernel(
    tms, rows_count, x_ref, g_ref, kin_ref, kout_ref, sect_ref, b_ref,
    back_ref, xp, gp, icx, icg, acc, hid, dgrad, act, gate, window, inner,
    sent_f, got_f, sum_f, got_zf, sent_b, got_b, sum_b, got_zb,
    wide_e, wide_a, fin, fout,
    s_xp, r_xp, s_gp, r_gp, s_sf, r_sf, s_sb, r_sb, s_seg, r_seg,
):
    seg = lax.axis_index("segment")
    tm = lax.axis_index("tm")
    row = lax.axis_index("rows")
    encodes = seg == 0
    decodes = seg == 1
    up, down = row + 1 < rows_count, row > 0
    later, earlier = tm + 1 < tms, tm > 0
    row_up = {"rows": lax.rem(row + 1, rows_count)}
    row_down = {"rows": lax.rem(row + rows_count - 1, rows_count)}
    tm_later = {"tm": lax.rem(tm + 1, tms)}
    tm_earlier = {"tm": lax.rem(tm + tms - 1, tms)}
    other = {"segment": 1 - seg}
    both = jnp.logical_and

    xp[...] = jnp.zeros_like(xp)
    gp[...] = jnp.zeros_like(gp)
    got_f[...] = jnp.zeros_like(got_f)
    got_zf[...] = jnp.zeros_like(got_zf)
    got_b[...] = jnp.zeros_like(got_b)
    got_zb[...] = jnp.zeros_like(got_zb)

    @pl.when(encodes)
    def _():
        xp[2:4, 1:3] = x_ref[...]

    @pl.when(decodes)
    def _():
        gp[0:2, 1:3] = g_ref[...]

    barrier = pltpu.get_barrier_semaphore()
    for partner in (row_up, row_down, tm_later, tm_earlier, other):
        pl.semaphore_signal(barrier, inc=1, device_id=partner, device_id_type=MESH_ID)
    pl.semaphore_wait(barrier, 5)

    def gather(buf, own, far, sems, to, sends, receives, arrivals):
        edge_up = Link(buf.at[own, 2], buf.at[own, 0], sems, 0, row_up, up, down)
        edge_down = Link(buf.at[own, 1], buf.at[own, 3], sems, 1, row_down, down, up)
        time_hi = Link(buf.at[own, 2], buf.at[far, 2], sems, 2, to, sends, receives)
        time_lo = Link(buf.at[own, 1], buf.at[far, 1], sems, 3, to, sends, receives)
        far_up = Link(
            buf.at[far, 2], buf.at[far, 0], sems, 4, row_up, both(up, receives), both(down, receives)
        )
        far_down = Link(
            buf.at[far, 1], buf.at[far, 3], sems, 5, row_down, both(down, receives), both(up, receives)
        )
        arrivals[0]()
        time_hi.start()
        edge_up.start()
        arrivals[1]()
        time_lo.start()
        edge_down.start()
        time_hi.wait_recv()
        far_up.start()
        time_lo.wait_recv()
        far_down.start()
        for link in (edge_up, edge_down, far_up, far_down):
            link.wait_recv()
        return [edge_up, edge_down, time_hi, time_lo, far_up, far_down]

    def columns(buf, dest, reverse):
        for t in range(3):
            for i in range(3):
                a, b = (2 - t, 2 - i) if reverse else (t, i)
                for f in range(2):
                    for r in range(2):
                        dest[pl.ds((2 * f + r) * 128, 128), pl.ds((3 * t + i) * 128, 128)] = buf[a + f, b + r]

    def hidden():
        for j in range(3):
            acc[j] = jnp.dot(
                icx[...], kin_ref[:, j].reshape(1152, 256), preferred_element_type=jnp.float32
            )

        def line(n, carry):
            at = pl.ds(pl.multiple_of(n * 128, 128), 128)
            value = joined(acc[0, at], acc[1, at], acc[2, at], False)
            hid[at] = value
            act[at] = (value / (1.0 + jnp.exp(-value))).astype(jnp.bfloat16)
            return carry

        lax.fori_loop(0, 4, line, 0)

    def upstream():
        for j in range(3):
            weights = jnp.concatenate([kout_ref[n, j] for n in range(9)], axis=1)
            acc[j] = lax.dot_general(
                icg[...], weights, (((1,), (1,)), ((), ())), preferred_element_type=jnp.float32
            )

        def line(n, carry):
            at = pl.ds(pl.multiple_of(n * 128, 128), 128)
            dgrad[at] = joined(acc[0, at], acc[1, at], acc[2, at], True)
            return carry

        lax.fori_loop(0, 4, line, 0)

    def gating():
        def line(n, carry):
            at = pl.ds(pl.multiple_of(n * 128, 128), 128)
            value = hid[at]
            sigmoid = 1.0 / (1.0 + jnp.exp(-value))
            gate[at] = (dgrad[at] * sigmoid * (1.0 + value * (1.0 - sigmoid))).astype(jnp.bfloat16)
            return carry

        lax.fori_loop(0, 4, line, 0)

    def scatter(source, reverse, sent, got, total, got_time, sems, to, sends, receives):
        seen = set()
        for t in range(3):
            for i in range(3):
                n = 3 * t + i
                if reverse:
                    product = lax.dot_general(
                        source[...], kin_ref[n].reshape(384, 256), (((1,), (1,)), ((), ())),
                        preferred_element_type=jnp.float32,
                    )
                    a, b = t, i
                else:
                    weights = jnp.concatenate([kout_ref[n, j] for j in range(3)], axis=1)
                    product = jnp.dot(source[...], weights, preferred_element_type=jnp.float32)
                    a, b = 2 - t, 2 - i
                for f in range(2):
                    for r in range(2):
                        piece = product[(2 * f + r) * 128 : (2 * f + r + 1) * 128]
                        where = (a + f, b + r)
                        if where in seen:
                            window[where] += piece
                        else:
                            window[where] = piece
                        seen.add(where)
        own, far = (2, 0) if reverse else (0, 2)

        def value(f, r):
            return joined(
                window[f, r, :, 0:128], window[f, r, :, 128:256], window[f, r, :, 256:384], reverse
            )

        links = []
        for start in (far, own):
            for f in range(2):
                sent[start + f, 0] = value(start + f, 0).astype(jnp.bfloat16)
                sent[start + f, 1] = value(start + f, 3).astype(jnp.bfloat16)
            crossing = sends if start == far else True
            span = pl.ds(start, 2)
            base = 0 if start == far else 2
            to_up = Link(
                sent.at[span, 1], got.at[span, 0], sems, base, row_up, both(up, crossing), both(down, crossing)
            )
            to_down = Link(
                sent.at[span, 0], got.at[span, 1], sems, base + 1, row_down, both(down, crossing), both(up, crossing)
            )
            to_up.start()
            to_down.start()
            links += [to_up, to_down]
        for f in range(2):
            for r in range(2):
                inner[f, r] = value(own + f, r + 1)
        links[0].wait_recv()
        links[1].wait_recv()
        for f in range(2):
            for r in range(2):
                total[f, r] = (value(far + f, r + 1) + got[far + f, r].astype(jnp.float32)).astype(jnp.bfloat16)
        in_time = Link(total, got_time, sems, 4, to, sends, receives)
        in_time.start()
        links[2].wait_recv()
        links[3].wait_recv()
        in_time.wait_recv()
        for f in range(2):
            for r in range(2):
                inner[f, r] += got[own + f, r].astype(jnp.float32) + got_time[f, r].astype(jnp.float32)
        return links + [in_time]

    own_x, far_x = pl.ds(2, 2), pl.ds(0, 2)
    own_g, far_g = pl.ds(0, 2), pl.ds(2, 2)
    seg_sems = (s_seg, r_seg)
    x_hi = Link(sect_ref.at[:, 1], xp.at[own_x, 2], seg_sems, 0, other, encodes, decodes)
    x_lo = Link(sect_ref.at[:, 0], xp.at[own_x, 1], seg_sems, 1, other, encodes, decodes)
    g_hi = Link(back_ref.at[:, 1], gp.at[own_g, 2], seg_sems, 2, other, decodes, encodes)
    g_lo = Link(back_ref.at[:, 0], gp.at[own_g, 1], seg_sems, 3, other, decodes, encodes)

    def gather_g(arrivals):
        links = gather(gp, own_g, far_g, (s_gp, r_gp), tm_earlier, earlier, later, arrivals)
        columns(gp, icg, True)
        upstream()
        for link in links:
            link.wait_send()

    @pl.when(decodes)
    def _():
        gather_g((lambda: None, lambda: None))

    links = gather(
        xp, own_x, far_x, (s_xp, r_xp), tm_later, later, earlier, (x_hi.wait_recv, x_lo.wait_recv)
    )
    columns(xp, icx, False)
    hidden()

    @pl.when(decodes)
    def _():
        gating()
        back_links = scatter(
            gate, True, sent_b, got_b, sum_b, got_zb, (s_sb, r_sb), tm_earlier, earlier, later
        )
        for r, link in ((1, g_hi), (0, g_lo)):
            for f in range(2):
                back_ref[f, r] = (gp[f, r + 1].astype(jnp.float32) + inner[f, r]).astype(jnp.bfloat16)
            link.start()
        for link in back_links:
            link.wait_send()

    links += scatter(
        act, False, sent_f, got_f, sum_f, got_zf, (s_sf, r_sf), tm_later, later, earlier
    )
    for r, link in ((1, x_hi), (0, x_lo)):
        for f in range(2):
            sect_ref[f, r] = (xp[f + 2, r + 1].astype(jnp.float32) + inner[f, r]).astype(jnp.bfloat16)
        link.start()

    @pl.when(encodes)
    def _():
        gather_g((g_hi.wait_recv, g_lo.wait_recv))
        gating()

    def widen(n, carry):
        at = pl.ds(pl.multiple_of(n * 128, 128), 128)
        for source, dest, by in ((gate, wide_e, -1), (act, wide_a, 1)):
            line = source[at].astype(jnp.float32)
            dest[at, 0:256] = shifted(line, by).astype(jnp.bfloat16)
            dest[at, 256:512] = source[at]
            dest[at, 512:768] = shifted(line, -by).astype(jnp.bfloat16)
        return carry

    lax.fori_loop(0, 4, widen, 0)
    over_cells = (((0,), (0,)), ((), ()))
    for t in range(3):
        span = pl.ds(t * 384, 384)
        product = lax.dot_general(
            icx[:, span], wide_e[...], over_cells, preferred_element_type=jnp.float32
        )
        for i in range(3):
            for j in range(3):
                fin[pl.ds((9 * t + 3 * i + j) * 128, 128)] = product[
                    i * 128 : (i + 1) * 128, j * 256 : (j + 1) * 256
                ]
        product = lax.dot_general(
            wide_a[...], icg[:, span], over_cells, preferred_element_type=jnp.float32
        )
        for i in range(3):
            for j in range(3):
                fout[pl.ds((9 * t + 3 * i + j) * 256, 256)] = product[
                    j * 256 : (j + 1) * 256, i * 128 : (i + 1) * 128
                ]

    def pack(z, carry):
        ins = fin[pl.ds(pl.multiple_of(z * 432, 432), 432)]
        outs = fout[pl.ds(pl.multiple_of(z * 864, 864), 864)]
        pad = jnp.zeros((CHUNK - 108, 128), jnp.float32)
        for k in range(16):
            part = ins[27 * k : 27 * k + 27]
            block = jnp.concatenate([part[:, :128], part[:, 128:], outs[54 * k : 54 * k + 54], pad], axis=0)
            b_ref[z, k // 8, k // 2 % 4, k % 2] = block.astype(jnp.bfloat16)
        return carry

    lax.fori_loop(0, ZS, pack, 0)
    for link in links + [x_hi, x_lo, g_hi, g_lo]:
        link.wait_send()


def front(tms, rows_count, clip, cotangent, kernel_in, kernel_out):
    whole = pl.BlockSpec(memory_space=pltpu.VMEM)
    dma = pltpu.SemaphoreType.DMA
    bf16, f32 = jnp.bfloat16, jnp.float32
    vmem = pltpu.VMEM
    tile = (128, 128)
    return pl.pallas_call(
        partial(front_kernel, tms, rows_count),
        out_shape=(
            jax.ShapeDtypeStruct((2, 2) + tile, bf16),
            jax.ShapeDtypeStruct((ZS, YS, XS, CORES, CHUNK, 128), bf16),
        ),
        in_specs=[whole] * 4,
        out_specs=(whole, whole),
        scratch_shapes=[
            vmem((2, 2) + tile, bf16),
            vmem((4, 4) + tile, bf16),
            vmem((4, 4) + tile, bf16),
            vmem((512, 1152), bf16),
            vmem((512, 1152), bf16),
            vmem((3, 512, 256), f32),
            vmem((512, 256), f32),
            vmem((512, 256), f32),
            vmem((512, 256), bf16),
            vmem((512, 256), bf16),
            vmem((4, 4, 128, 384), f32),
            vmem((2, 2) + tile, f32),
        ]
        + [vmem((4, 2) + tile, bf16), vmem((4, 2) + tile, bf16), vmem((2, 2) + tile, bf16), vmem((2, 2) + tile, bf16)] * 2
        + [
            vmem((512, 768), bf16),
            vmem((512, 768), bf16),
            vmem((3456, 256), f32),
            vmem((6912, 128), f32),
            dma((6,)), dma((6,)), dma((6,)), dma((6,)), dma((5,)), dma((5,)), dma((5,)), dma((5,)), dma((4,)), dma((4,)),
        ],
        compiler_params=pltpu.CompilerParams(
            collective_id=1, has_side_effects=True, vmem_limit_bytes=56 << 20
        ),
    )(clip, cotangent, kernel_in, kernel_out)


def on_device(tms, rows_count, input_clip, cotangent, kernel_in, kernel_out):
    sections, blocks = front(
        tms, rows_count, input_clip, cotangent,
        kernel_in.reshape(9, 3, 128, 256), kernel_out.reshape(9, 3, 256, 128),
    )
    in_sum, out_sum = reduce_scatter(blocks)
    return (sections[None], in_sum.reshape(1, -1), out_sum.reshape(1, -1))


def solution(mesh):
    in_specs = (
        P("tm", "rows", None, None),
        P("tm", "rows", None, None),
        P("segment", None, None),
        P("segment", None, None),
    )
    out_specs = (
        P("segment", "tm", "rows", None, None),
        P("segment", ("tm", "rows")),
        P("segment", ("tm", "rows")),
    )
    return jax.shard_map(
        partial(on_device, mesh.shape["tm"], mesh.shape["rows"]),
        mesh=mesh, in_specs=in_specs, out_specs=out_specs, check_vma=False,
    )
```

```python
from functools import partial

import jax
import jax.numpy as jnp
from jax import lax
from jax.experimental import pallas as pl
from jax.experimental.pallas import tpu as pltpu
from jax.sharding import PartitionSpec as P

MESH_ID = pl.DeviceIdType.MESH
CORES, XS, YS, ZS = 2, 4, 2, 8
CHUNK = 112


TOP = 64


def shifted(line, by):
    rows = lax.broadcasted_iota(jnp.int32, line.shape, 0)
    if by == 1:
        return jnp.where(rows == 0, 0.0, pltpu.roll(line, 1, 0))
    return jnp.where(rows == 127, 0.0, pltpu.roll(line, 127, 0))


def joined(low, mid, high, reverse):
    if reverse:
        return shifted(low, -1) + mid + shifted(high, 1)
    return shifted(low, 1) + mid + shifted(high, -1)


class Link:
    def __init__(self, src, dst, sems, index, device, sends, receives):
        self.parts = (src, dst, sems[0].at[index], sems[1].at[index], device)
        self.sends = sends
        self.receives = receives

    def copy(self):
        src, dst, send_sem, recv_sem, device = self.parts
        return pltpu.make_async_remote_copy(
            src_ref=src, dst_ref=dst, send_sem=send_sem, recv_sem=recv_sem,
            device_id=device, device_id_type=MESH_ID,
        )

    def start(self):
        @pl.when(self.sends)
        def _():
            self.copy().start()

    def wait_recv(self):
        @pl.when(self.receives)
        def _():
            self.copy().wait_recv()

    def wait_send(self):
        @pl.when(self.sends)
        def _():
            self.copy().wait_send()


def front_kernel(
    tms, rows_count, x_ref, g_ref, kin_hbm, kout_hbm, sect_ref, in_ref, out_ref,
    kin_ref, kout_ref, s_load, back_ref, xp, gp, icx, icg, acc, hid, dgrad, act, gate, window, inner,
    sent_f, got_f, sum_f, got_zf, sent_b, got_b, sum_b, got_zb,
    wide_e, wide_a, fin, fout,
    s_xp, r_xp, s_gp, r_gp, s_sf, r_sf, s_sb, r_sb, s_seg, r_seg,
    *reduce_refs,
):
    seg = lax.axis_index("segment")
    tm = lax.axis_index("tm")
    row = lax.axis_index("rows")
    encodes = seg == 0
    decodes = seg == 1
    up, down = row + 1 < rows_count, row > 0
    later, earlier = tm + 1 < tms, tm > 0
    row_up = {"rows": lax.rem(row + 1, rows_count)}
    row_down = {"rows": lax.rem(row + rows_count - 1, rows_count)}
    tm_later = {"tm": lax.rem(tm + 1, tms)}
    tm_earlier = {"tm": lax.rem(tm + tms - 1, tms)}
    other = {"segment": 1 - seg}
    both = jnp.logical_and
    core, at_x, at_y = lax.rem(row, 2), lax.rem(row // 2, XS), row // 8

    def x_at(offset):
        return lax.rem(at_x + offset, XS)

    sibling = {"rows": at_y * 8 + at_x * 2 + 1 - core}
    across_y = {"rows": (1 - at_y) * 8 + at_x * 2 + core}
    across_x = [{"rows": at_y * 8 + x_at(o) * 2 + core} for o in range(1, XS)]
    in_time = [{"tm": lax.rem(tm + p, ZS)} for p in range(1, ZS)]
    load_in = pltpu.make_async_copy(kin_hbm, kin_ref, s_load.at[0])
    load_out = pltpu.make_async_copy(kout_hbm, kout_ref, s_load.at[1])
    load_in.start()
    load_out.start()

    xp[...] = jnp.zeros_like(xp)
    gp[...] = jnp.zeros_like(gp)
    got_f[...] = jnp.zeros_like(got_f)
    got_zf[...] = jnp.zeros_like(got_zf)
    got_b[...] = jnp.zeros_like(got_b)
    got_zb[...] = jnp.zeros_like(got_zb)

    @pl.when(encodes)
    def _():
        xp[2:4, 1:3] = x_ref[...]

    @pl.when(decodes)
    def _():
        gp[0:2, 1:3] = g_ref[...]

    barrier = pltpu.get_barrier_semaphore()
    partners = [row_up, row_down, other, sibling, across_y] + across_x + in_time
    for partner in partners:
        pl.semaphore_signal(barrier, inc=1, device_id=partner, device_id_type=MESH_ID)
    pl.semaphore_wait(barrier, len(partners))

    def gather(buf, own, far, sems, to, sends, receives, arrivals):
        edge_up = Link(buf.at[own, 2], buf.at[own, 0], sems, 0, row_up, up, down)
        edge_down = Link(buf.at[own, 1], buf.at[own, 3], sems, 1, row_down, down, up)
        time_hi = Link(buf.at[own, 2], buf.at[far, 2], sems, 2, to, sends, receives)
        time_lo = Link(buf.at[own, 1], buf.at[far, 1], sems, 3, to, sends, receives)
        far_up = Link(
            buf.at[far, 2], buf.at[far, 0], sems, 4, row_up, both(up, receives), both(down, receives)
        )
        far_down = Link(
            buf.at[far, 1], buf.at[far, 3], sems, 5, row_down, both(down, receives), both(up, receives)
        )
        arrivals[0]()
        time_hi.start()
        edge_up.start()
        arrivals[1]()
        time_lo.start()
        edge_down.start()
        time_hi.wait_recv()
        far_up.start()
        time_lo.wait_recv()
        far_down.start()
        for link in (edge_up, edge_down, far_up, far_down):
            link.wait_recv()
        return [edge_up, edge_down, time_hi, time_lo, far_up, far_down]

    def columns(buf, dest, reverse):
        for t in range(3):
            for i in range(3):
                a, b = (2 - t, 2 - i) if reverse else (t, i)
                for f in range(2):
                    for r in range(2):
                        dest[pl.ds((2 * f + r) * 128, 128), pl.ds((3 * t + i) * 128, 128)] = buf[a + f, b + r]

    def hidden():
        for j in range(3):
            acc[j] = jnp.dot(
                icx[...], kin_ref[:, j].reshape(1152, 256), preferred_element_type=jnp.float32
            )

        def line(n, carry):
            at = pl.ds(pl.multiple_of(n * 128, 128), 128)
            value = joined(acc[0, at], acc[1, at], acc[2, at], False)
            hid[at] = value
            act[at] = (value / (1.0 + jnp.exp(-value))).astype(jnp.bfloat16)
            return carry

        lax.fori_loop(0, 4, line, 0)

    def upstream():
        for j in range(3):
            weights = jnp.concatenate([kout_ref[n, j] for n in range(9)], axis=1)
            acc[j] = lax.dot_general(
                icg[...], weights, (((1,), (1,)), ((), ())), preferred_element_type=jnp.float32
            )

        def line(n, carry):
            at = pl.ds(pl.multiple_of(n * 128, 128), 128)
            dgrad[at] = joined(acc[0, at], acc[1, at], acc[2, at], True)
            return carry

        lax.fori_loop(0, 4, line, 0)

    def gating():
        def line(n, carry):
            at = pl.ds(pl.multiple_of(n * 128, 128), 128)
            value = hid[at]
            sigmoid = 1.0 / (1.0 + jnp.exp(-value))
            gate[at] = (dgrad[at] * sigmoid * (1.0 + value * (1.0 - sigmoid))).astype(jnp.bfloat16)
            return carry

        lax.fori_loop(0, 4, line, 0)

    def scatter(source, reverse, sent, got, total, got_time, sems, to, sends, receives):
        seen = set()
        for t in range(3):
            for i in range(3):
                n = 3 * t + i
                if reverse:
                    product = lax.dot_general(
                        source[...], kin_ref[n].reshape(384, 256), (((1,), (1,)), ((), ())),
                        preferred_element_type=jnp.float32,
                    )
                    a, b = t, i
                else:
                    weights = jnp.concatenate([kout_ref[n, j] for j in range(3)], axis=1)
                    product = jnp.dot(source[...], weights, preferred_element_type=jnp.float32)
                    a, b = 2 - t, 2 - i
                for f in range(2):
                    for r in range(2):
                        piece = product[(2 * f + r) * 128 : (2 * f + r + 1) * 128]
                        where = (a + f, b + r)
                        if where in seen:
                            window[where] += piece
                        else:
                            window[where] = piece
                        seen.add(where)
        own, far = (2, 0) if reverse else (0, 2)

        def value(f, r):
            return joined(
                window[f, r, :, 0:128], window[f, r, :, 128:256], window[f, r, :, 256:384], reverse
            )

        links = []
        for start in (far, own):
            for f in range(2):
                sent[start + f, 0] = value(start + f, 0).astype(jnp.bfloat16)
                sent[start + f, 1] = value(start + f, 3).astype(jnp.bfloat16)
            crossing = sends if start == far else True
            span = pl.ds(start, 2)
            base = 0 if start == far else 2
            to_up = Link(
                sent.at[span, 1], got.at[span, 0], sems, base, row_up, both(up, crossing), both(down, crossing)
            )
            to_down = Link(
                sent.at[span, 0], got.at[span, 1], sems, base + 1, row_down, both(down, crossing), both(up, crossing)
            )
            to_up.start()
            to_down.start()
            links += [to_up, to_down]
        for f in range(2):
            for r in range(2):
                inner[f, r] = value(own + f, r + 1)
        links[0].wait_recv()
        links[1].wait_recv()
        for f in range(2):
            for r in range(2):
                total[f, r] = (value(far + f, r + 1) + got[far + f, r].astype(jnp.float32)).astype(jnp.bfloat16)
        ahead = Link(total, got_time, sems, 4, to, sends, receives)
        ahead.start()
        links[2].wait_recv()
        links[3].wait_recv()
        ahead.wait_recv()
        for f in range(2):
            for r in range(2):
                inner[f, r] += got[own + f, r].astype(jnp.float32) + got_time[f, r].astype(jnp.float32)
        return links + [ahead]

    own_x, far_x = pl.ds(2, 2), pl.ds(0, 2)
    own_g, far_g = pl.ds(0, 2), pl.ds(2, 2)
    seg_sems = (s_seg, r_seg)
    x_hi = Link(sect_ref.at[:, 1], xp.at[own_x, 2], seg_sems, 0, other, encodes, decodes)
    x_lo = Link(sect_ref.at[:, 0], xp.at[own_x, 1], seg_sems, 1, other, encodes, decodes)
    g_hi = Link(back_ref.at[:, 1], gp.at[own_g, 2], seg_sems, 2, other, decodes, encodes)
    g_lo = Link(back_ref.at[:, 0], gp.at[own_g, 1], seg_sems, 3, other, decodes, encodes)

    def gather_g(arrivals):
        links = gather(gp, own_g, far_g, (s_gp, r_gp), tm_earlier, earlier, later, arrivals)
        columns(gp, icg, True)
        upstream()
        for link in links:
            link.wait_send()

    load_in.wait()
    load_out.wait()

    @pl.when(decodes)
    def _():
        gather_g((lambda: None, lambda: None))

    links = gather(
        xp, own_x, far_x, (s_xp, r_xp), tm_later, later, earlier, (x_hi.wait_recv, x_lo.wait_recv)
    )
    columns(xp, icx, False)
    hidden()

    @pl.when(decodes)
    def _():
        gating()
        back_links = scatter(
            gate, True, sent_b, got_b, sum_b, got_zb, (s_sb, r_sb), tm_earlier, earlier, later
        )
        for r, link in ((1, g_hi), (0, g_lo)):
            for f in range(2):
                back_ref[f, r] = (gp[f, r + 1].astype(jnp.float32) + inner[f, r]).astype(jnp.bfloat16)
            link.start()
        for link in back_links:
            link.wait_send()

    links += scatter(
        act, False, sent_f, got_f, sum_f, got_zf, (s_sf, r_sf), tm_later, later, earlier
    )
    for r, link in ((1, x_hi), (0, x_lo)):
        for f in range(2):
            sect_ref[f, r] = (xp[f + 2, r + 1].astype(jnp.float32) + inner[f, r]).astype(jnp.bfloat16)
        link.start()

    @pl.when(encodes)
    def _():
        gather_g((g_hi.wait_recv, g_lo.wait_recv))
        gating()

    def widen(n, carry):
        at = pl.ds(pl.multiple_of(n * 128, 128), 128)
        for source, dest, by in ((gate, wide_e, -1), (act, wide_a, 1)):
            line = source[at].astype(jnp.float32)
            dest[at, 0:256] = shifted(line, by).astype(jnp.bfloat16)
            dest[at, 256:512] = source[at]
            dest[at, 512:768] = shifted(line, -by).astype(jnp.bfloat16)
        return carry

    lax.fori_loop(0, 4, widen, 0)
    over_cells = (((0,), (0,)), ((), ()))
    for t in range(3):
        span = pl.ds(t * 384, 384)
        product = lax.dot_general(
            icx[:, span], wide_e[...], over_cells, preferred_element_type=jnp.float32
        )
        for i in range(3):
            for j in range(3):
                fin[pl.ds((9 * t + 3 * i + j) * 128, 128)] = product[
                    i * 128 : (i + 1) * 128, j * 256 : (j + 1) * 256
                ]
        product = lax.dot_general(
            wide_a[...], icg[:, span], over_cells, preferred_element_type=jnp.float32
        )
        for i in range(3):
            for j in range(3):
                fout[pl.ds((9 * t + 3 * i + j) * 256, 256)] = product[
                    j * 256 : (j + 1) * 256, i * 128 : (i + 1) * 128
                ]

    reduce_scatter(
        fin, fout, in_ref, out_ref, tm, core, at_y, x_at, sibling, across_y, *reduce_refs
    )
    for link in links + [x_hi, x_lo, g_hi, g_lo]:
        link.wait_send()


def reduce_scatter(
    fin, fout, in_ref, out_ref, tm, core, at_y, x_at, sibling, across_y,
    blocks, got_core, half_a, got_a, half_c, got_c, next_a, got_a2, next_c, got_c2,
    own_a, own_c, last, got_z,
    s_core, r_core, s_a, r_a, s_c, r_c, s_a2, r_a2, s_c2, r_c2, s_z, r_z,
):
    f32, bf16 = jnp.float32, jnp.bfloat16

    def send(src, dst, send_sem, recv_sem, device):
        copy = pltpu.make_async_remote_copy(
            src_ref=src, dst_ref=dst, send_sem=send_sem, recv_sem=recv_sem,
            device_id=device, device_id_type=MESH_ID,
        )
        copy.start()
        return copy

    def x_device(o):
        return {"rows": at_y * 8 + x_at(o) * 2 + core}

    def core_copy(q):
        return pltpu.make_async_remote_copy(
            src_ref=blocks.at[q, :, :, 1 - core], dst_ref=got_core.at[q],
            send_sem=s_core.at[q], recv_sem=r_core.at[q],
            device_id=sibling, device_id_type=MESH_ID,
        )

    def pack(q, carry):
        odd = lax.rem(q, 2)
        offset = 4 + (1 - odd) * (q // 2) - odd * ((q + 1) // 2)
        z = lax.rem(tm + offset, ZS)
        ins = fin[pl.ds(pl.multiple_of(z * 432, 16), 432)]
        outs = fout[pl.ds(pl.multiple_of(z * 864, 16), 864)]
        pad = jnp.zeros((CHUNK - 108, 128), f32)
        for k in range(16):
            part = ins[27 * k : 27 * k + 27]
            block = jnp.concatenate([part[:, :128], part[:, 128:], outs[54 * k : 54 * k + 54], pad], axis=0)
            blocks[q, k // 8, k // 2 % 4, k % 2] = block.astype(bf16)
        core_copy(q).start()
        return carry

    lax.fori_loop(0, ZS, pack, 0)
    copies = []
    firsts = []
    for h in range(2):

        def add_core(n, carry, h=h):
            q = 4 * h + n
            core_copy(q).wait_recv()
            for o in range(XS):
                for y in range(YS):
                    x = x_at(o)
                    side = lax.rem(at_y + y, 2)
                    total = blocks[q, side, x, core].astype(f32) + got_core[q, side, x].astype(f32)
                    half_a[h, o, n, y] = total[0:TOP].astype(bf16)
                    half_c[h, y, n, o] = total[TOP:CHUNK].astype(bf16)
            return carry

        lax.fori_loop(0, 4, add_core, 0)
        sent = []
        for o in (2, 1, 3):
            sent.append(send(half_a.at[h, o], got_a.at[h, o], s_a.at[h, o], r_a.at[h, o], x_device(o)))
        sent.append(send(half_c.at[h, 1], got_c.at[h], s_c.at[h], r_c.at[h], across_y))
        firsts.append(sent)
        copies += sent
    seconds = []
    for h in range(2):
        for copy in firsts[h]:
            copy.wait_recv()

        def add_first(n, carry, h=h):
            for y in range(YS):
                total = half_a[h, 0, n, y].astype(f32)
                for o in range(1, XS):
                    total = total + got_a[h, o, n, y].astype(f32)
                if y == 0:
                    own_a[h, n] = total
                else:
                    next_a[h, n] = total.astype(bf16)
            for o in range(XS):
                total = half_c[h, 0, n, o].astype(f32) + got_c[h, n, o].astype(f32)
                if o == 0:
                    own_c[h, n] = total
                else:
                    next_c[h, o, n] = total.astype(bf16)
            return carry

        lax.fori_loop(0, 4, add_first, 0)
        sent = [send(next_a.at[h], got_a2.at[h], s_a2.at[h], r_a2.at[h], across_y)]
        for o in (2, 1, 3):
            sent.append(send(next_c.at[h, o], got_c2.at[h, o], s_c2.at[h, o], r_c2.at[h, o], x_device(o)))
        seconds.append(sent)
        copies += sent
    thirds = []
    total = None
    for h in range(2):
        for copy in seconds[h]:
            copy.wait_recv()
        for n in range(4):
            q = 4 * h + n
            top = own_a[h, n] + got_a2[h, n].astype(f32)
            low = own_c[h, n]
            for o in range(1, XS):
                low = low + got_c2[h, o, n].astype(f32)
            total = jnp.concatenate([top, low], axis=0)
            if q < ZS - 1:
                offset = 4 + q // 2 if q % 2 == 0 else 4 - (q + 1) // 2
                last[q] = total.astype(bf16)
                thirds.append(
                    send(last.at[q], got_z.at[q], s_z.at[q], r_z.at[q], {"tm": lax.rem(tm + offset, ZS)})
                )
    for q, copy in enumerate(thirds):
        copy.wait_recv()
        total = total + got_z[q].astype(f32)
    in_ref[:, 0:128] = total[0:27]
    in_ref[:, 128:256] = total[27:54]
    out_ref[...] = total[54:108]
    for copy in copies + thirds:
        copy.wait_send()

    def drain(q, carry):
        core_copy(q).wait_send()
        return carry

    lax.fori_loop(0, ZS, drain, 0)


def front(tms, rows_count, clip, cotangent, kernel_in, kernel_out):
    whole = pl.BlockSpec(memory_space=pltpu.VMEM)
    dma = pltpu.SemaphoreType.DMA
    bf16, f32 = jnp.bfloat16, jnp.float32
    vmem = pltpu.VMEM
    tile = (128, 128)
    return pl.pallas_call(
        partial(front_kernel, tms, rows_count),
        out_shape=(
            jax.ShapeDtypeStruct((2, 2) + tile, bf16),
            jax.ShapeDtypeStruct((27, 256), f32),
            jax.ShapeDtypeStruct((54, 128), f32),
        ),
        in_specs=[whole, whole, pl.BlockSpec(memory_space=pl.ANY), pl.BlockSpec(memory_space=pl.ANY)],
        out_specs=(whole, whole, whole),
        scratch_shapes=[
            vmem((9, 3, 128, 256), bf16),
            vmem((9, 3, 256, 128), bf16),
            dma((2,)),
            vmem((2, 2) + tile, bf16),
            vmem((4, 4) + tile, bf16),
            vmem((4, 4) + tile, bf16),
            vmem((512, 1152), bf16),
            vmem((512, 1152), bf16),
            vmem((3, 512, 256), f32),
            vmem((512, 256), f32),
            vmem((512, 256), f32),
            vmem((512, 256), bf16),
            vmem((512, 256), bf16),
            vmem((4, 4, 128, 384), f32),
            vmem((2, 2) + tile, f32),
        ]
        + [vmem((4, 2) + tile, bf16), vmem((4, 2) + tile, bf16), vmem((2, 2) + tile, bf16), vmem((2, 2) + tile, bf16)] * 2
        + [
            vmem((512, 768), bf16),
            vmem((512, 768), bf16),
            vmem((3456, 256), f32),
            vmem((6912, 128), f32),
            dma((6,)), dma((6,)), dma((6,)), dma((6,)), dma((5,)), dma((5,)), dma((5,)), dma((5,)), dma((4,)), dma((4,)),
            vmem((ZS, YS, XS, CORES, CHUNK, 128), bf16),
            vmem((ZS, YS, XS, CHUNK, 128), bf16),
            vmem((2, XS, 4, YS, TOP, 128), bf16),
            vmem((2, XS, 4, YS, TOP, 128), bf16),
            vmem((2, YS, 4, XS, CHUNK - TOP, 128), bf16),
            vmem((2, 4, XS, CHUNK - TOP, 128), bf16),
            vmem((2, 4, TOP, 128), bf16),
            vmem((2, 4, TOP, 128), bf16),
            vmem((2, XS, 4, CHUNK - TOP, 128), bf16),
            vmem((2, XS, 4, CHUNK - TOP, 128), bf16),
            vmem((2, 4, TOP, 128), f32),
            vmem((2, 4, CHUNK - TOP, 128), f32),
            vmem((ZS, CHUNK, 128), bf16),
            vmem((ZS, CHUNK, 128), bf16),
            dma((ZS,)), dma((ZS,)), dma((2, XS)), dma((2, XS)), dma((2,)), dma((2,)),
            dma((2,)), dma((2,)), dma((2, XS)), dma((2, XS)), dma((ZS,)), dma((ZS,)),
        ],
        compiler_params=pltpu.CompilerParams(
            collective_id=1, has_side_effects=True, vmem_limit_bytes=56 << 20
        ),
    )(clip, cotangent, kernel_in, kernel_out)


def on_device(tms, rows_count, input_clip, cotangent, kernel_in, kernel_out):
    sections, in_sum, out_sum = front(
        tms, rows_count, input_clip, cotangent,
        kernel_in.reshape(9, 3, 128, 256), kernel_out.reshape(9, 3, 256, 128),
    )
    return (sections[None], in_sum.reshape(1, -1), out_sum.reshape(1, -1))


def solution(mesh):
    in_specs = (
        P("tm", "rows", None, None),
        P("tm", "rows", None, None),
        P("segment", None, None),
        P("segment", None, None),
    )
    out_specs = (
        P("segment", "tm", "rows", None, None),
        P("segment", ("tm", "rows")),
        P("segment", ("tm", "rows")),
    )
    return jax.shard_map(
        partial(on_device, mesh.shape["tm"], mesh.shape["rows"]),
        mesh=mesh, in_specs=in_specs, out_specs=out_specs, check_vma=False,
    )
```

```python
from functools import partial

import jax
import jax.numpy as jnp
from jax import lax
from jax.experimental import pallas as pl
from jax.experimental.pallas import tpu as pltpu
from jax.sharding import PartitionSpec as P

MESH_ID = pl.DeviceIdType.MESH
CORES, XS, YS, ZS = 2, 4, 2, 8
CHUNK = 112


TOP = 64
EARLY, LATE = (6, 7, 8, 1, 4), (0, 2, 3, 5)
PLACES = EARLY + LATE


def shifted(line, by):
    rows = lax.broadcasted_iota(jnp.int32, line.shape, 0)
    if by == 1:
        return jnp.where(rows == 0, 0.0, pltpu.roll(line, 1, 0))
    return jnp.where(rows == 127, 0.0, pltpu.roll(line, 127, 0))


def joined(low, mid, high, reverse):
    if reverse:
        return shifted(low, -1) + mid + shifted(high, 1)
    return shifted(low, 1) + mid + shifted(high, -1)


class Link:
    def __init__(self, src, dst, sems, index, device, sends, receives):
        self.parts = (src, dst, sems[0].at[index], sems[1].at[index], device)
        self.sends = sends
        self.receives = receives

    def copy(self):
        src, dst, send_sem, recv_sem, device = self.parts
        return pltpu.make_async_remote_copy(
            src_ref=src, dst_ref=dst, send_sem=send_sem, recv_sem=recv_sem,
            device_id=device, device_id_type=MESH_ID,
        )

    def start(self):
        @pl.when(self.sends)
        def _():
            self.copy().start()

    def wait_recv(self):
        @pl.when(self.receives)
        def _():
            self.copy().wait_recv()

    def wait_send(self):
        @pl.when(self.sends)
        def _():
            self.copy().wait_send()


def front_kernel(
    tms, rows_count, x_ref, g_ref, kin_hbm, kout_hbm, sect_ref, in_ref, out_ref,
    kin_ref, kout_ref, s_load, back_ref, xp, gp, icx, icg, acc, hid, dgrad, act, gate, window, inner,
    sent_f, got_f, sum_f, got_zf, sent_b, got_b, sum_b, got_zb,
    wide_e, wide_a, fin, fout,
    s_xp, r_xp, s_gp, r_gp, s_sf, r_sf, s_sb, r_sb, s_seg, r_seg,
    *reduce_refs,
):
    seg = lax.axis_index("segment")
    tm = lax.axis_index("tm")
    row = lax.axis_index("rows")
    encodes = seg == 0
    decodes = seg == 1
    later, earlier = tm + 1 < tms, tm > 0
    tm_later = {"tm": lax.rem(tm + 1, tms)}
    tm_earlier = {"tm": lax.rem(tm + tms - 1, tms)}
    other = {"segment": 1 - seg}
    both = jnp.logical_and
    core, at_x, at_y = lax.rem(row, 2), lax.rem(row // 2, XS), row // (XS * CORES)

    step = 2 * core - 1
    crosses = both(row + step >= 0, row + step < rows_count)
    across = {"rows": lax.rem(row + step + rows_count, rows_count)}

    def x_at(offset):
        return lax.rem(at_x + offset, XS)

    sibling = {"rows": at_y * (XS * CORES) + at_x * 2 + 1 - core}
    across_y = {"rows": (1 - at_y) * (XS * CORES) + at_x * 2 + core}
    across_x = [{"rows": at_y * (XS * CORES) + x_at(o) * 2 + core} for o in range(1, XS)]
    in_time = [{"tm": lax.rem(tm + p, ZS)} for p in range(1, ZS)]
    load_in = pltpu.make_async_copy(kin_hbm, kin_ref, s_load.at[0])
    load_out = pltpu.make_async_copy(kout_hbm, kout_ref, s_load.at[1])
    load_in.start()
    load_out.start()

    xp[...] = jnp.zeros_like(xp)
    gp[...] = jnp.zeros_like(gp)
    got_f[...] = jnp.zeros_like(got_f)
    got_zf[...] = jnp.zeros_like(got_zf)
    got_b[...] = jnp.zeros_like(got_b)
    got_zb[...] = jnp.zeros_like(got_zb)

    @pl.when(encodes)
    def _():
        xp[2:4, 1:3] = x_ref[...]

    @pl.when(decodes)
    def _():
        gp[0:2, 1:3] = g_ref[...]

    barrier = pltpu.get_barrier_semaphore()
    partners = [across, other, sibling, across_y] + across_x + in_time
    for partner in partners:
        pl.semaphore_signal(barrier, inc=1, device_id=partner, device_id_type=MESH_ID)
    pl.semaphore_wait(barrier, len(partners))

    inner_rows = (1 + core, 2 - core)
    row_devices = (across, sibling)
    edge_slots = (3 * (1 - core), 3 * core)
    outer_rows = (3 * core, 3 * (1 - core))
    row_exists = (crosses, True)

    def gather(buf, own, far, sems, to, sends, receives, arrivals, order, early):
        edges, times, fars = [], [], []
        for k in range(2):
            device, slot = row_devices[k], edge_slots[k]
            edges.append(
                Link(buf.at[own, inner_rows[k]], buf.at[own, slot], sems, k, device, row_exists[k], row_exists[k])
            )
            times.append(
                Link(buf.at[own, inner_rows[k]], buf.at[far, inner_rows[k]], sems, 2 + k, to, sends, receives)
            )
            crossing = both(row_exists[k], receives)
            fars.append(
                Link(buf.at[far, inner_rows[k]], buf.at[far, slot], sems, 4 + k, device, crossing, crossing)
            )
        for k in order:
            arrivals[k]()
            times[k].start()
            edges[k].start()
        for k in order:
            times[k].wait_recv()
            fars[k].start()
        for link in edges:
            link.wait_recv()
        early()
        for link in fars:
            link.wait_recv()
        return edges + times + fars

    def columns(buf, dest, reverse, taps):
        for n in taps:
            t, i = n // 3, n % 3
            a, b = (2 - t, 2 - i) if reverse else (t, i)
            for f in range(2):
                for r in range(2):
                    dest[pl.ds((2 * f + r) * 128, 128), pl.ds(PLACES.index(n) * 128, 128)] = buf[a + f, b + r]

    def conv_part(taps, source, weights_of, contract, add):
        span = pl.ds(PLACES.index(taps[0]) * 128, len(taps) * 128)
        for j in range(3):
            product = lax.dot_general(
                source[:, span], weights_of(taps, j), (((1,), (contract,)), ((), ())),
                preferred_element_type=jnp.float32,
            )
            acc[j] = acc[j] + product if add else product

    def hidden_part(taps, add):
        columns(xp, icx, False, taps)
        conv_part(
            taps, icx, lambda ns, j: jnp.concatenate([kin_ref[n, j] for n in ns], axis=0), 0, add
        )

    def upstream_part(taps, add):
        columns(gp, icg, True, taps)
        conv_part(
            taps, icg, lambda ns, j: jnp.concatenate([kout_ref[n, j] for n in ns], axis=1), 1, add
        )

    def activate():
        def line(n, carry):
            at = pl.ds(pl.multiple_of(n * 128, 128), 128)
            value = joined(acc[0, at], acc[1, at], acc[2, at], False)
            hid[at] = value
            act[at] = (value / (1.0 + jnp.exp(-value))).astype(jnp.bfloat16)
            return carry

        lax.fori_loop(0, 4, line, 0)

    def keep_upstream():
        def line(n, carry):
            at = pl.ds(pl.multiple_of(n * 128, 128), 128)
            dgrad[at] = joined(acc[0, at], acc[1, at], acc[2, at], True)
            return carry

        lax.fori_loop(0, 4, line, 0)

    def gating():
        def line(n, carry):
            at = pl.ds(pl.multiple_of(n * 128, 128), 128)
            value = hid[at]
            sigmoid = 1.0 / (1.0 + jnp.exp(-value))
            gate[at] = (dgrad[at] * sigmoid * (1.0 + value * (1.0 - sigmoid))).astype(jnp.bfloat16)
            return carry

        lax.fori_loop(0, 4, line, 0)

    def scatter(source, reverse, sent, got, total, got_time, sems, to, sends, receives, finish):
        seen = set()
        own, far = (2, 0) if reverse else (0, 2)

        def products(t):
            for i in range(3):
                n = 3 * t + i
                if reverse:
                    product = lax.dot_general(
                        source[...], kin_ref[n].reshape(384, 256), (((1,), (1,)), ((), ())),
                        preferred_element_type=jnp.float32,
                    )
                    a, b = t, i
                else:
                    weights = jnp.concatenate([kout_ref[n, j] for j in range(3)], axis=1)
                    product = jnp.dot(source[...], weights, preferred_element_type=jnp.float32)
                    a, b = 2 - t, 2 - i
                for f in range(2):
                    for r in range(2):
                        piece = product[(2 * f + r) * 128 : (2 * f + r + 1) * 128]
                        where = (a + f, b + r)
                        if where in seen:
                            window[where] += piece
                        else:
                            window[where] = piece
                        seen.add(where)

        def value(f, r):
            return joined(
                window[f, r, :, 0:128], window[f, r, :, 128:256], window[f, r, :, 256:384], reverse
            )

        def send_edges(start, base, exists):
            links = []
            for k in range(2):
                for f in range(2):
                    sent[k, start + f] = value(start + f, outer_rows[k]).astype(jnp.bfloat16)
                span = pl.ds(start, 2)
                goes = both(row_exists[k], exists)
                link = Link(sent.at[k, span], got.at[k, span], sems, base + k, row_devices[k], goes, goes)
                link.start()
                links.append(link)
            return links

        products(0)
        products(1)
        far_links = send_edges(far, 0, sends)
        products(2)
        own_links = send_edges(own, 2, True)
        time_links = []
        for k in (1, 0):
            far_links[k].wait_recv()
            for f in range(2):
                total[k, f] = (
                    value(far + f, inner_rows[k]) + got[k, far + f].astype(jnp.float32)
                ).astype(jnp.bfloat16)
            link = Link(total.at[k], got_time.at[k], sems, 4 + k, to, sends, receives)
            link.start()
            time_links.append(link)
        for k, link in zip((1, 0), time_links):
            for f in range(2):
                inner[k, f] = value(own + f, inner_rows[k])
            own_links[k].wait_recv()
            link.wait_recv()
            finish(
                k,
                [
                    inner[k, f] + got[k, own + f].astype(jnp.float32) + got_time[k, f].astype(jnp.float32)
                    for f in range(2)
                ],
            )
        return far_links + own_links + time_links

    own_x, far_x = pl.ds(2, 2), pl.ds(0, 2)
    own_g, far_g = pl.ds(0, 2), pl.ds(2, 2)
    seg_sems = (s_seg, r_seg)
    x_links, g_links = [], []
    for k in range(2):
        place = inner_rows[k]
        x_links.append(
            Link(sect_ref.at[:, place - 1], xp.at[own_x, place], seg_sems, k, other, encodes, decodes)
        )
        g_links.append(
            Link(back_ref.at[:, place - 1], gp.at[own_g, place], seg_sems, 2 + k, other, decodes, encodes)
        )

    def gather_g(arrivals, order):
        links = gather(
            gp, own_g, far_g, (s_gp, r_gp), tm_earlier, earlier, later, arrivals, order,
            lambda: upstream_part(EARLY, False),
        )
        upstream_part(LATE, True)
        keep_upstream()
        for link in links:
            link.wait_send()

    def gather_x(arrivals, order):
        links = gather(
            xp, own_x, far_x, (s_xp, r_xp), tm_later, later, earlier, arrivals, order,
            lambda: hidden_part(EARLY, False),
        )
        hidden_part(LATE, True)
        activate()
        for link in links:
            link.wait_send()

    def finish_x(k, sums):
        place = inner_rows[k]
        for f in range(2):
            sect_ref[f, place - 1] = (xp[f + 2, place].astype(jnp.float32) + sums[f]).astype(jnp.bfloat16)
        x_links[k].start()

    def finish_g(k, sums):
        place = inner_rows[k]
        for f in range(2):
            back_ref[f, place - 1] = (gp[f, place].astype(jnp.float32) + sums[f]).astype(jnp.bfloat16)
        g_links[k].start()

    at_once = (lambda: None, lambda: None)
    load_in.wait()
    load_out.wait()

    @pl.when(encodes)
    def _():
        gather_x(at_once, (0, 1))

    @pl.when(decodes)
    def _():
        gather_g(at_once, (0, 1))
        gather_x([link.wait_recv for link in x_links], (1, 0))
        gating()
        back_links = scatter(
            gate, True, sent_b, got_b, sum_b, got_zb, (s_sb, r_sb), tm_earlier, earlier, later, finish_g
        )
        for link in back_links:
            link.wait_send()

    links = scatter(
        act, False, sent_f, got_f, sum_f, got_zf, (s_sf, r_sf), tm_later, later, earlier, finish_x
    )

    @pl.when(encodes)
    def _():
        gather_g([link.wait_recv for link in g_links], (1, 0))
        gating()

    def widen(n, carry):
        at = pl.ds(pl.multiple_of(n * 128, 128), 128)
        for source, dest, by in ((gate, wide_e, -1), (act, wide_a, 1)):
            line = source[at].astype(jnp.float32)
            dest[at, 0:256] = shifted(line, by).astype(jnp.bfloat16)
            dest[at, 256:512] = source[at]
            dest[at, 512:768] = shifted(line, -by).astype(jnp.bfloat16)
        return carry

    lax.fori_loop(0, 4, widen, 0)
    over_cells = (((0,), (0,)), ((), ()))
    for t in range(3):
        span = pl.ds(t * 384, 384)
        product = lax.dot_general(
            icx[:, span], wide_e[...], over_cells, preferred_element_type=jnp.float32
        )
        for i in range(3):
            for j in range(3):
                fin[pl.ds((3 * PLACES[3 * t + i] + j) * 128, 128)] = product[
                    i * 128 : (i + 1) * 128, j * 256 : (j + 1) * 256
                ]
        product = lax.dot_general(
            wide_a[...], icg[:, span], over_cells, preferred_element_type=jnp.float32
        )
        for i in range(3):
            for j in range(3):
                fout[pl.ds((3 * PLACES[3 * t + i] + j) * 256, 256)] = product[
                    j * 256 : (j + 1) * 256, i * 128 : (i + 1) * 128
                ]

    reduce_scatter(
        fin, fout, in_ref, out_ref, tm, core, at_y, x_at, sibling, across_y, *reduce_refs
    )
    for link in links + x_links + g_links:
        link.wait_send()


def reduce_scatter(
    fin, fout, in_ref, out_ref, tm, core, at_y, x_at, sibling, across_y,
    blocks, got_core, half_a, got_a, half_c, got_c, next_a, got_a2, next_c, got_c2,
    own_a, own_c, last, got_z,
    s_core, r_core, s_a, r_a, s_c, r_c, s_a2, r_a2, s_c2, r_c2, s_z, r_z,
):
    f32, bf16 = jnp.float32, jnp.bfloat16

    def send(src, dst, send_sem, recv_sem, device):
        copy = pltpu.make_async_remote_copy(
            src_ref=src, dst_ref=dst, send_sem=send_sem, recv_sem=recv_sem,
            device_id=device, device_id_type=MESH_ID,
        )
        copy.start()
        return copy

    def x_device(o):
        return {"rows": at_y * (XS * CORES) + x_at(o) * 2 + core}

    def core_copy(q):
        return pltpu.make_async_remote_copy(
            src_ref=blocks.at[q, :, :, 1 - core], dst_ref=got_core.at[q],
            send_sem=s_core.at[q], recv_sem=r_core.at[q],
            device_id=sibling, device_id_type=MESH_ID,
        )

    def pack(q, carry):
        odd = lax.rem(q, 2)
        offset = 4 + (1 - odd) * (q // 2) - odd * ((q + 1) // 2)
        z = lax.rem(tm + offset, ZS)
        ins = fin[pl.ds(pl.multiple_of(z * 432, 16), 432)]
        outs = fout[pl.ds(pl.multiple_of(z * 864, 16), 864)]
        pad = jnp.zeros((CHUNK - 108, 128), f32)
        for k in range(16):
            part = ins[27 * k : 27 * k + 27]
            block = jnp.concatenate([part[:, :128], part[:, 128:], outs[54 * k : 54 * k + 54], pad], axis=0)
            blocks[q, k // 8, k // 2 % 4, k % 2] = block.astype(bf16)
        core_copy(q).start()
        return carry

    lax.fori_loop(0, ZS, pack, 0)
    copies = []
    firsts = []
    for h in range(2):

        def add_core(n, carry, h=h):
            q = 4 * h + n
            core_copy(q).wait_recv()
            for o in range(XS):
                for y in range(YS):
                    x = x_at(o)
                    side = lax.rem(at_y + y, 2)
                    total = blocks[q, side, x, core].astype(f32) + got_core[q, side, x].astype(f32)
                    half_a[h, o, n, y] = total[0:TOP].astype(bf16)
                    half_c[h, y, n, o] = total[TOP:CHUNK].astype(bf16)
            return carry

        lax.fori_loop(0, 4, add_core, 0)
        sent = []
        for o in (2, 1, 3):
            sent.append(send(half_a.at[h, o], got_a.at[h, o], s_a.at[h, o], r_a.at[h, o], x_device(o)))
        sent.append(send(half_c.at[h, 1], got_c.at[h], s_c.at[h], r_c.at[h], across_y))
        firsts.append(sent)
        copies += sent
    seconds = []
    for h in range(2):
        for copy in firsts[h]:
            copy.wait_recv()

        def add_first(n, carry, h=h):
            for y in range(YS):
                total = half_a[h, 0, n, y].astype(f32)
                for o in range(1, XS):
                    total = total + got_a[h, o, n, y].astype(f32)
                if y == 0:
                    own_a[h, n] = total
                else:
                    next_a[h, n] = total.astype(bf16)
            for o in range(XS):
                total = half_c[h, 0, n, o].astype(f32) + got_c[h, n, o].astype(f32)
                if o == 0:
                    own_c[h, n] = total
                else:
                    next_c[h, o, n] = total.astype(bf16)
            return carry

        lax.fori_loop(0, 4, add_first, 0)
        sent = [send(next_a.at[h], got_a2.at[h], s_a2.at[h], r_a2.at[h], across_y)]
        for o in (2, 1, 3):
            sent.append(send(next_c.at[h, o], got_c2.at[h, o], s_c2.at[h, o], r_c2.at[h, o], x_device(o)))
        seconds.append(sent)
        copies += sent
    thirds = []
    total = None
    for h in range(2):
        for copy in seconds[h]:
            copy.wait_recv()
        for n in range(4):
            q = 4 * h + n
            top = own_a[h, n] + got_a2[h, n].astype(f32)
            low = own_c[h, n]
            for o in range(1, XS):
                low = low + got_c2[h, o, n].astype(f32)
            total = jnp.concatenate([top, low], axis=0)
            if q < ZS - 1:
                offset = 4 + q // 2 if q % 2 == 0 else 4 - (q + 1) // 2
                last[q] = total.astype(bf16)
                thirds.append(
                    send(last.at[q], got_z.at[q], s_z.at[q], r_z.at[q], {"tm": lax.rem(tm + offset, ZS)})
                )
    for q, copy in enumerate(thirds):
        copy.wait_recv()
        total = total + got_z[q].astype(f32)
    in_ref[:, 0:128] = total[0:27]
    in_ref[:, 128:256] = total[27:54]
    out_ref[...] = total[54:108]
    for copy in copies + thirds:
        copy.wait_send()

    def drain(q, carry):
        core_copy(q).wait_send()
        return carry

    lax.fori_loop(0, ZS, drain, 0)


def front(tms, rows_count, clip, cotangent, kernel_in, kernel_out):
    whole = pl.BlockSpec(memory_space=pltpu.VMEM)
    dma = pltpu.SemaphoreType.DMA
    bf16, f32 = jnp.bfloat16, jnp.float32
    vmem = pltpu.VMEM
    tile = (128, 128)
    return pl.pallas_call(
        partial(front_kernel, tms, rows_count),
        out_shape=(
            jax.ShapeDtypeStruct((2, 2) + tile, bf16),
            jax.ShapeDtypeStruct((27, 256), f32),
            jax.ShapeDtypeStruct((54, 128), f32),
        ),
        in_specs=[whole, whole, pl.BlockSpec(memory_space=pl.ANY), pl.BlockSpec(memory_space=pl.ANY)],
        out_specs=(whole, whole, whole),
        scratch_shapes=[
            vmem((9, 3, 128, 256), bf16),
            vmem((9, 3, 256, 128), bf16),
            dma((2,)),
            vmem((2, 2) + tile, bf16),
            vmem((4, 4) + tile, bf16),
            vmem((4, 4) + tile, bf16),
            vmem((512, 1152), bf16),
            vmem((512, 1152), bf16),
            vmem((3, 512, 256), f32),
            vmem((512, 256), f32),
            vmem((512, 256), f32),
            vmem((512, 256), bf16),
            vmem((512, 256), bf16),
            vmem((4, 4, 128, 384), f32),
            vmem((2, 2) + tile, f32),
        ]
        + [vmem((2, 4) + tile, bf16), vmem((2, 4) + tile, bf16), vmem((2, 2) + tile, bf16), vmem((2, 2) + tile, bf16)] * 2
        + [
            vmem((512, 768), bf16),
            vmem((512, 768), bf16),
            vmem((3456, 256), f32),
            vmem((6912, 128), f32),
            dma((6,)), dma((6,)), dma((6,)), dma((6,)), dma((6,)), dma((6,)), dma((6,)), dma((6,)), dma((4,)), dma((4,)),
            vmem((ZS, YS, XS, CORES, CHUNK, 128), bf16),
            vmem((ZS, YS, XS, CHUNK, 128), bf16),
            vmem((2, XS, 4, YS, TOP, 128), bf16),
            vmem((2, XS, 4, YS, TOP, 128), bf16),
            vmem((2, YS, 4, XS, CHUNK - TOP, 128), bf16),
            vmem((2, 4, XS, CHUNK - TOP, 128), bf16),
            vmem((2, 4, TOP, 128), bf16),
            vmem((2, 4, TOP, 128), bf16),
            vmem((2, XS, 4, CHUNK - TOP, 128), bf16),
            vmem((2, XS, 4, CHUNK - TOP, 128), bf16),
            vmem((2, 4, TOP, 128), f32),
            vmem((2, 4, CHUNK - TOP, 128), f32),
            vmem((ZS, CHUNK, 128), bf16),
            vmem((ZS, CHUNK, 128), bf16),
            dma((ZS,)), dma((ZS,)), dma((2, XS)), dma((2, XS)), dma((2,)), dma((2,)),
            dma((2,)), dma((2,)), dma((2, XS)), dma((2, XS)), dma((ZS,)), dma((ZS,)),
        ],
        compiler_params=pltpu.CompilerParams(
            collective_id=1, has_side_effects=True, vmem_limit_bytes=56 << 20
        ),
    )(clip, cotangent, kernel_in, kernel_out)


def hand_over_kernel(sect_ref, in_ref, out_ref, sect_out, in_out, out_out):
    sect_out[...] = sect_ref[...]
    for k in range(27):
        in_out[:, pl.ds(256 * k, 256)] = in_ref[pl.ds(k, 1)]
    for k in range(54):
        out_out[:, pl.ds(128 * k, 128)] = out_ref[pl.ds(k, 1)]


def hand_over(sections, in_sum, out_sum):
    whole = pl.BlockSpec(memory_space=pltpu.VMEM)
    return pl.pallas_call(
        hand_over_kernel,
        out_shape=(
            jax.ShapeDtypeStruct(sections.shape, sections.dtype),
            jax.ShapeDtypeStruct((1, 6912), jnp.float32),
            jax.ShapeDtypeStruct((1, 6912), jnp.float32),
        ),
        in_specs=[whole] * 3,
        out_specs=(whole,) * 3,
    )(sections, in_sum, out_sum)


def on_device(tms, rows_count, input_clip, cotangent, kernel_in, kernel_out):
    sections, in_sum, out_sum = front(
        tms, rows_count, input_clip, cotangent,
        kernel_in.reshape(9, 3, 128, 256), kernel_out.reshape(9, 3, 256, 128),
    )
    sections, in_sum, out_sum = hand_over(sections, in_sum, out_sum)
    return (sections[None], in_sum, out_sum)


def solution(mesh):
    in_specs = (
        P("tm", "rows", None, None),
        P("tm", "rows", None, None),
        P("segment", None, None),
        P("segment", None, None),
    )
    out_specs = (
        P("segment", "tm", "rows", None, None),
        P("segment", ("tm", "rows")),
        P("segment", ("tm", "rows")),
    )
    return jax.shard_map(
        partial(on_device, mesh.shape["tm"], mesh.shape["rows"]),
        mesh=mesh, in_specs=in_specs, out_specs=out_specs, check_vma=False,
    )
```

```python
from functools import partial

import jax
import jax.numpy as jnp
from jax import lax
from jax.experimental import pallas as pl
from jax.experimental.pallas import tpu as pltpu
from jax.sharding import PartitionSpec as P

MESH_ID = pl.DeviceIdType.MESH
CORES, XS, YS, ZS = 2, 4, 2, 8
CHUNK = 112


TOP = 64
EARLY, LATE = (6, 7, 8, 1, 4), (0, 2, 3, 5)
PLACES = EARLY + LATE


def shifted(line, by):
    rows = lax.broadcasted_iota(jnp.int32, line.shape, 0)
    if by == 1:
        return jnp.where(rows == 0, 0.0, pltpu.roll(line, 1, 0))
    return jnp.where(rows == 127, 0.0, pltpu.roll(line, 127, 0))


def joined(low, mid, high, reverse):
    if reverse:
        return shifted(low, -1) + mid + shifted(high, 1)
    return shifted(low, 1) + mid + shifted(high, -1)


class Link:
    def __init__(self, src, dst, sems, index, device, sends, receives):
        self.parts = (src, dst, sems[0].at[index], sems[1].at[index], device)
        self.sends = sends
        self.receives = receives

    def copy(self):
        src, dst, send_sem, recv_sem, device = self.parts
        return pltpu.make_async_remote_copy(
            src_ref=src, dst_ref=dst, send_sem=send_sem, recv_sem=recv_sem,
            device_id=device, device_id_type=MESH_ID,
        )

    def start(self):
        @pl.when(self.sends)
        def _():
            self.copy().start()

    def wait_recv(self):
        @pl.when(self.receives)
        def _():
            self.copy().wait_recv()

    def wait_send(self):
        @pl.when(self.sends)
        def _():
            self.copy().wait_send()


def front_kernel(
    tms, rows_count, x_ref, g_ref, kin_hbm, kout_hbm, sect_ref, in_ref, out_ref,
    kin_ref, kout_ref, s_load, back_ref, xp, gp, icx, icg, acc, hid, dgrad, act, gate, window, inner,
    sent_f, got_f, sum_f, got_zf, sent_b, got_b, sum_b, got_zb,
    wide_e, wide_a, act_t, icx_t, fin, fout,
    s_xp, r_xp, s_gp, r_gp, s_sf, r_sf, s_sb, r_sb, s_seg, r_seg,
    *reduce_refs,
):
    seg = lax.axis_index("segment")
    tm = lax.axis_index("tm")
    row = lax.axis_index("rows")
    encodes = seg == 0
    decodes = seg == 1
    later, earlier = tm + 1 < tms, tm > 0
    tm_later = {"tm": lax.rem(tm + 1, tms)}
    tm_earlier = {"tm": lax.rem(tm + tms - 1, tms)}
    other = {"segment": 1 - seg}
    other_next = {"segment": 1 - seg, "tm": lax.rem(tm + tms + 1 - 2 * seg, tms)}
    both = jnp.logical_and
    core, at_x, at_y = lax.rem(row, 2), lax.rem(row // 2, XS), row // (XS * CORES)

    step = 2 * core - 1
    crosses = both(row + step >= 0, row + step < rows_count)
    across = {"rows": lax.rem(row + step + rows_count, rows_count)}

    def x_at(offset):
        return lax.rem(at_x + offset, XS)

    sibling = {"rows": at_y * (XS * CORES) + at_x * 2 + 1 - core}
    across_y = {"rows": (1 - at_y) * (XS * CORES) + at_x * 2 + core}
    across_x = [{"rows": at_y * (XS * CORES) + x_at(o) * 2 + core} for o in range(1, XS)]
    in_time = [{"tm": lax.rem(tm + p, ZS)} for p in range(1, ZS)]
    load_in = pltpu.make_async_copy(kin_hbm, kin_ref, s_load.at[0])
    load_out = pltpu.make_async_copy(kout_hbm, kout_ref, s_load.at[1])
    load_in.start()
    load_out.start()

    xp[...] = jnp.zeros_like(xp)
    gp[...] = jnp.zeros_like(gp)
    got_f[...] = jnp.zeros_like(got_f)
    got_zf[...] = jnp.zeros_like(got_zf)
    got_b[...] = jnp.zeros_like(got_b)
    got_zb[...] = jnp.zeros_like(got_zb)

    @pl.when(encodes)
    def _():
        xp[2:4, 1:3] = x_ref[...]

    @pl.when(decodes)
    def _():
        gp[0:2, 1:3] = g_ref[...]

    barrier = pltpu.get_barrier_semaphore()
    partners = [across, other, other_next, sibling, across_y] + across_x + in_time
    for partner in partners:
        pl.semaphore_signal(barrier, inc=1, device_id=partner, device_id_type=MESH_ID)
    pl.semaphore_wait(barrier, len(partners))

    inner_rows = (1 + core, 2 - core)
    row_devices = (across, sibling)
    edge_slots = (3 * (1 - core), 3 * core)
    outer_rows = (3 * core, 3 * (1 - core))
    row_exists = (crosses, True)

    def gather(buf, own, far, sems, to, sends, receives, arrivals, order, early, direct=None):
        edges, times, fars = [], [], []
        for k in range(2):
            device, slot = row_devices[k], edge_slots[k]
            edges.append(
                Link(buf.at[own, inner_rows[k]], buf.at[own, slot], sems, k, device, row_exists[k], row_exists[k])
            )
            times.append(
                Link(buf.at[own, inner_rows[k]], buf.at[far, inner_rows[k]], sems, 2 + k, to, sends, receives)
            )
            crossing = both(row_exists[k], receives)
            fars.append(
                Link(buf.at[far, inner_rows[k]], buf.at[far, slot], sems, 4 + k, device, crossing, crossing)
            )
        for k in order:
            if direct:
                arrivals[k]()
                edges[k].start()
                direct[k].wait_recv()
                fars[k].start()
            else:
                times[k].start()
                edges[k].start()
        if not direct:
            for k in order:
                times[k].wait_recv()
                fars[k].start()
        for link in edges:
            link.wait_recv()
        early()
        for link in fars:
            link.wait_recv()
        return edges + fars + ([] if direct else times)

    def columns(buf, dest, reverse, taps):
        for n in taps:
            t, i = n // 3, n % 3
            a, b = (2 - t, 2 - i) if reverse else (t, i)
            for f in range(2):
                for r in range(2):
                    dest[pl.ds((2 * f + r) * 128, 128), pl.ds(PLACES.index(n) * 128, 128)] = buf[a + f, b + r]

    def conv_part(taps, source, weights_of, contract, add):
        span = pl.ds(PLACES.index(taps[0]) * 128, len(taps) * 128)
        for j in range(3):
            product = lax.dot_general(
                source[:, span], weights_of(taps, j), (((1,), (contract,)), ((), ())),
                preferred_element_type=jnp.float32,
            )
            acc[j] = acc[j] + product if add else product

    def hidden_part(taps, add):
        columns(xp, icx, False, taps)
        conv_part(
            taps, icx, lambda ns, j: jnp.concatenate([kin_ref[n, j] for n in ns], axis=0), 0, add
        )

    def upstream_part(taps, add):
        columns(gp, icg, True, taps)
        conv_part(
            taps, icg, lambda ns, j: jnp.concatenate([kout_ref[n, j] for n in ns], axis=1), 1, add
        )

    def activate():
        def line(n, carry):
            at = pl.ds(pl.multiple_of(n * 128, 128), 128)
            value = joined(acc[0, at], acc[1, at], acc[2, at], False)
            hid[at] = value
            act[at] = (value / (1.0 + jnp.exp(-value))).astype(jnp.bfloat16)
            return carry

        lax.fori_loop(0, 4, line, 0)

    def keep_upstream():
        def line(n, carry):
            at = pl.ds(pl.multiple_of(n * 128, 128), 128)
            dgrad[at] = joined(acc[0, at], acc[1, at], acc[2, at], True)
            return carry

        lax.fori_loop(0, 4, line, 0)

    def gating():
        def line(n, carry):
            at = pl.ds(pl.multiple_of(n * 128, 128), 128)
            value = hid[at]
            sigmoid = 1.0 / (1.0 + jnp.exp(-value))
            gate[at] = (dgrad[at] * sigmoid * (1.0 + value * (1.0 - sigmoid))).astype(jnp.bfloat16)
            return carry

        lax.fori_loop(0, 4, line, 0)

    def scatter(source, reverse, sent, got, total, got_time, sems, to, sends, receives, finish):
        seen = set()
        own, far = (2, 0) if reverse else (0, 2)

        def products(t):
            for i in range(3):
                n = 3 * t + i
                if reverse:
                    product = lax.dot_general(
                        source[...], kin_ref[n].reshape(384, 256), (((1,), (1,)), ((), ())),
                        preferred_element_type=jnp.float32,
                    )
                    a, b = t, i
                else:
                    weights = jnp.concatenate([kout_ref[n, j] for j in range(3)], axis=1)
                    product = jnp.dot(source[...], weights, preferred_element_type=jnp.float32)
                    a, b = 2 - t, 2 - i
                for f in range(2):
                    for r in range(2):
                        piece = product[(2 * f + r) * 128 : (2 * f + r + 1) * 128]
                        where = (a + f, b + r)
                        if where in seen:
                            window[where] += piece
                        else:
                            window[where] = piece
                        seen.add(where)

        def value(f, r):
            return joined(
                window[f, r, :, 0:128], window[f, r, :, 128:256], window[f, r, :, 256:384], reverse
            )

        def send_edges(start, base, exists):
            links = []
            for k in range(2):
                for f in range(2):
                    sent[k, start + f] = value(start + f, outer_rows[k]).astype(jnp.bfloat16)
                span = pl.ds(start, 2)
                goes = both(row_exists[k], exists)
                link = Link(sent.at[k, span], got.at[k, span], sems, base + k, row_devices[k], goes, goes)
                link.start()
                links.append(link)
            return links

        products(0)
        products(1)
        far_links = send_edges(far, 0, sends)
        products(2)
        own_links = send_edges(own, 2, True)
        time_links = []
        for k in (1, 0):
            far_links[k].wait_recv()
            for f in range(2):
                total[k, f] = (
                    value(far + f, inner_rows[k]) + got[k, far + f].astype(jnp.float32)
                ).astype(jnp.bfloat16)
            link = Link(total.at[k], got_time.at[k], sems, 4 + k, to, sends, receives)
            link.start()
            time_links.append(link)
        for k, link in zip((1, 0), time_links):
            for f in range(2):
                inner[k, f] = value(own + f, inner_rows[k])
            own_links[k].wait_recv()
            link.wait_recv()
            finish(
                k,
                [
                    inner[k, f] + got[k, own + f].astype(jnp.float32) + got_time[k, f].astype(jnp.float32)
                    for f in range(2)
                ],
            )
        return far_links + own_links + time_links

    own_x, far_x = pl.ds(2, 2), pl.ds(0, 2)
    own_g, far_g = pl.ds(0, 2), pl.ds(2, 2)
    seg_sems = (s_seg, r_seg)
    x_links, g_links, x_next, g_next = [], [], [], []
    for k in range(2):
        place = inner_rows[k]
        x_links.append(
            Link(sect_ref.at[:, place - 1], xp.at[own_x, place], seg_sems, k, other, encodes, decodes)
        )
        g_links.append(
            Link(back_ref.at[:, place - 1], gp.at[own_g, place], seg_sems, 2 + k, other, decodes, encodes)
        )
        x_next.append(
            Link(
                sect_ref.at[:, place - 1], xp.at[far_x, place], seg_sems, 4 + k, other_next,
                both(encodes, later), both(decodes, earlier),
            )
        )
        g_next.append(
            Link(
                back_ref.at[:, place - 1], gp.at[far_g, place], seg_sems, 6 + k, other_next,
                both(decodes, earlier), both(encodes, later),
            )
        )

    def gather_g(arrivals, order, meanwhile, direct=None):
        def early():
            upstream_part(EARLY, False)
            meanwhile()

        links = gather(
            gp, own_g, far_g, (s_gp, r_gp), tm_earlier, earlier, later, arrivals, order, early, direct
        )
        upstream_part(LATE, True)
        keep_upstream()
        for link in links:
            link.wait_send()

    def gather_x(arrivals, order, direct=None):
        links = gather(
            xp, own_x, far_x, (s_xp, r_xp), tm_later, later, earlier, arrivals, order,
            lambda: hidden_part(EARLY, False), direct,
        )
        hidden_part(LATE, True)
        activate()
        for link in links:
            link.wait_send()

    def finish_x(k, sums):
        place = inner_rows[k]
        for f in range(2):
            sect_ref[f, place - 1] = (xp[f + 2, place].astype(jnp.float32) + sums[f]).astype(jnp.bfloat16)
        x_next[k].start()
        x_links[k].start()

    def finish_g(k, sums):
        place = inner_rows[k]
        for f in range(2):
            back_ref[f, place - 1] = (gp[f, place].astype(jnp.float32) + sums[f]).astype(jnp.bfloat16)
        g_next[k].start()
        g_links[k].start()

    def widen(source, dest, by):
        def line(n, carry):
            at = pl.ds(pl.multiple_of(n * 128, 128), 128)
            value = source[at].astype(jnp.float32)
            dest[at, 0:256] = shifted(value, by).astype(jnp.bfloat16)
            dest[at, 256:512] = source[at]
            dest[at, 512:768] = shifted(value, -by).astype(jnp.bfloat16)
            return carry

        lax.fori_loop(0, 4, line, 0)

    def prepare():
        widen(act, wide_a, 1)
        for n in range(6):
            act_t[pl.ds(n * 128, 128)] = wide_a[:, pl.ds(n * 128, 128)].T
        for n in range(9):
            icx_t[pl.ds(n * 128, 128)] = icx[:, pl.ds(n * 128, 128)].T

    def out_grad(taps):
        span = pl.ds(PLACES.index(taps[0]) * 128, len(taps) * 128)
        product = jnp.dot(act_t[...], icg[:, span], preferred_element_type=jnp.float32)
        for at, n in enumerate(taps):
            for j in range(3):
                fout[pl.ds((3 * n + j) * 256, 256)] = product[
                    j * 256 : (j + 1) * 256, at * 128 : (at + 1) * 128
                ]

    def in_grad():
        widen(gate, wide_e, -1)
        for group in range(3):
            product = jnp.dot(
                icx_t[pl.ds(group * 384, 384)], wide_e[...], preferred_element_type=jnp.float32
            )
            for i in range(3):
                for j in range(3):
                    fin[pl.ds((3 * PLACES[3 * group + i] + j) * 128, 128)] = product[
                        i * 128 : (i + 1) * 128, j * 256 : (j + 1) * 256
                    ]

    begin_reduce, end_reduce = reduce_scatter(
        fin, fout, in_ref, out_ref, tm, core, at_y, x_at, sibling, across_y, *reduce_refs
    )
    at_once = (lambda: None, lambda: None)
    load_in.wait()
    load_out.wait()

    @pl.when(encodes)
    def _():
        gather_x(at_once, (0, 1))

    @pl.when(decodes)
    def _():
        gather_g(at_once, (0, 1), lambda: None)
        gather_x([link.wait_recv for link in x_links], (1, 0), x_next)
        gating()
        back_links = scatter(
            gate, True, sent_b, got_b, sum_b, got_zb, (s_sb, r_sb), tm_earlier, earlier, later, finish_g
        )
        for link in back_links:
            link.wait_send()
        prepare()
        out_grad(EARLY)
        out_grad(LATE)
        in_grad()
        begin_reduce()

    links = scatter(
        act, False, sent_f, got_f, sum_f, got_zf, (s_sf, r_sf), tm_later, later, earlier, finish_x
    )

    @pl.when(encodes)
    def _():
        prepare()
        gather_g(
            [link.wait_recv for link in g_links], (1, 0), lambda: out_grad(EARLY), g_next
        )
        gating()
        out_grad(LATE)
        in_grad()
        begin_reduce()

    end_reduce()
    for link in links + x_links + g_links + x_next + g_next:
        link.wait_send()


def reduce_scatter(
    fin, fout, in_ref, out_ref, tm, core, at_y, x_at, sibling, across_y,
    blocks, got_core, half_a, got_a, half_c, got_c, next_a, got_a2, next_c, got_c2,
    own_a, own_c, last, got_z,
    s_core, r_core, s_a, r_a, s_c, r_c, s_a2, r_a2, s_c2, r_c2, s_z, r_z,
):
    f32, bf16 = jnp.float32, jnp.bfloat16

    def made(src, dst, send_sem, recv_sem, device):
        return pltpu.make_async_remote_copy(
            src_ref=src, dst_ref=dst, send_sem=send_sem, recv_sem=recv_sem,
            device_id=device, device_id_type=MESH_ID,
        )

    def x_device(o):
        return {"rows": at_y * (XS * CORES) + x_at(o) * 2 + core}

    def core_copy(q):
        return pltpu.make_async_remote_copy(
            src_ref=blocks.at[q, :, :, 1 - core], dst_ref=got_core.at[q],
            send_sem=s_core.at[q], recv_sem=r_core.at[q],
            device_id=sibling, device_id_type=MESH_ID,
        )

    def pack(q, carry):
        odd = lax.rem(q, 2)
        offset = 4 + (1 - odd) * (q // 2) - odd * ((q + 1) // 2)
        z = lax.rem(tm + offset, ZS)
        ins = fin[pl.ds(pl.multiple_of(z * 432, 16), 432)]
        outs = fout[pl.ds(pl.multiple_of(z * 864, 16), 864)]
        pad = jnp.zeros((CHUNK - 108, 128), f32)
        for k in range(16):
            part = ins[27 * k : 27 * k + 27]
            block = jnp.concatenate([part[:, :128], part[:, 128:], outs[54 * k : 54 * k + 54], pad], axis=0)
            blocks[q, k // 8, k // 2 % 4, k % 2] = block.astype(bf16)
        core_copy(q).start()
        return carry

    def first_copies(h):
        copies = [
            made(half_a.at[h, o], got_a.at[h, o], s_a.at[h, o], r_a.at[h, o], x_device(o)) for o in (2, 1, 3)
        ]
        return copies + [made(half_c.at[h, 1], got_c.at[h], s_c.at[h], r_c.at[h], across_y)]

    def second_copies(h):
        copies = [made(next_a.at[h], got_a2.at[h], s_a2.at[h], r_a2.at[h], across_y)]
        return copies + [
            made(next_c.at[h, o], got_c2.at[h, o], s_c2.at[h, o], r_c2.at[h, o], x_device(o))
            for o in (2, 1, 3)
        ]

    def third_copy(q):
        offset = 4 + q // 2 if q % 2 == 0 else 4 - (q + 1) // 2
        device = {"tm": lax.rem(tm + offset, ZS)}
        return made(last.at[q], got_z.at[q], s_z.at[q], r_z.at[q], device)

    def add_core(q, carry):
        h, n = q // 4, lax.rem(q, 4)
        core_copy(q).wait_recv()
        for o in range(XS):
            for y in range(YS):
                x = x_at(o)
                side = lax.rem(at_y + y, 2)
                total = blocks[q, side, x, core].astype(f32) + got_core[q, side, x].astype(f32)
                half_a[h, o, n, y] = total[0:TOP].astype(bf16)
                half_c[h, y, n, o] = total[TOP:CHUNK].astype(bf16)
        return carry

    def begin():
        lax.fori_loop(0, 6, pack, 0)
        lax.fori_loop(0, 4, add_core, 0)
        for copy in first_copies(0):
            copy.start()
        lax.fori_loop(6, ZS, pack, 0)
        lax.fori_loop(4, ZS, add_core, 0)
        for copy in first_copies(1):
            copy.start()

    def end():
        for h in range(2):
            for copy in first_copies(h):
                copy.wait_recv()

            def add_first(n, carry, h=h):
                for y in range(YS):
                    total = half_a[h, 0, n, y].astype(f32)
                    for o in range(1, XS):
                        total = total + got_a[h, o, n, y].astype(f32)
                    if y == 0:
                        own_a[h, n] = total
                    else:
                        next_a[h, n] = total.astype(bf16)
                for o in range(XS):
                    total = half_c[h, 0, n, o].astype(f32) + got_c[h, n, o].astype(f32)
                    if o == 0:
                        own_c[h, n] = total
                    else:
                        next_c[h, o, n] = total.astype(bf16)
                return carry

            lax.fori_loop(0, 4, add_first, 0)
            for copy in second_copies(h):
                copy.start()
        total = None
        for h in range(2):
            for copy in second_copies(h):
                copy.wait_recv()
            for n in range(4):
                q = 4 * h + n
                top = own_a[h, n] + got_a2[h, n].astype(f32)
                low = own_c[h, n]
                for o in range(1, XS):
                    low = low + got_c2[h, o, n].astype(f32)
                total = jnp.concatenate([top, low], axis=0)
                if q < ZS - 1:
                    last[q] = total.astype(bf16)
                    third_copy(q).start()
        for q in range(ZS - 1):
            third_copy(q).wait_recv()
            total = total + got_z[q].astype(f32)
        in_ref[:, 0:128] = total[0:27]
        in_ref[:, 128:256] = total[27:54]
        out_ref[...] = total[54:108]
        for h in range(2):
            for copy in first_copies(h) + second_copies(h):
                copy.wait_send()
        for q in range(ZS - 1):
            third_copy(q).wait_send()

        def drain(q, carry):
            core_copy(q).wait_send()
            return carry

        lax.fori_loop(0, ZS, drain, 0)

    return begin, end


def front(tms, rows_count, clip, cotangent, kernel_in, kernel_out):
    whole = pl.BlockSpec(memory_space=pltpu.VMEM)
    dma = pltpu.SemaphoreType.DMA
    bf16, f32 = jnp.bfloat16, jnp.float32
    vmem = pltpu.VMEM
    tile = (128, 128)
    return pl.pallas_call(
        partial(front_kernel, tms, rows_count),
        out_shape=(
            jax.ShapeDtypeStruct((2, 2) + tile, bf16),
            jax.ShapeDtypeStruct((27, 256), f32),
            jax.ShapeDtypeStruct((54, 128), f32),
        ),
        in_specs=[whole, whole, pl.BlockSpec(memory_space=pl.ANY), pl.BlockSpec(memory_space=pl.ANY)],
        out_specs=(whole, whole, whole),
        scratch_shapes=[
            vmem((9, 3, 128, 256), bf16),
            vmem((9, 3, 256, 128), bf16),
            dma((2,)),
            vmem((2, 2) + tile, bf16),
            vmem((4, 4) + tile, bf16),
            vmem((4, 4) + tile, bf16),
            vmem((512, 1152), bf16),
            vmem((512, 1152), bf16),
            vmem((3, 512, 256), f32),
            vmem((512, 256), f32),
            vmem((512, 256), f32),
            vmem((512, 256), bf16),
            vmem((512, 256), bf16),
            vmem((4, 4, 128, 384), f32),
            vmem((2, 2) + tile, f32),
        ]
        + [vmem((2, 4) + tile, bf16), vmem((2, 4) + tile, bf16), vmem((2, 2) + tile, bf16), vmem((2, 2) + tile, bf16)] * 2
        + [
            vmem((512, 768), bf16),
            vmem((512, 768), bf16),
            vmem((768, 512), bf16),
            vmem((1152, 512), bf16),
            vmem((3456, 256), f32),
            vmem((6912, 128), f32),
            dma((6,)), dma((6,)), dma((6,)), dma((6,)), dma((6,)), dma((6,)), dma((6,)), dma((6,)), dma((8,)), dma((8,)),
            vmem((ZS, YS, XS, CORES, CHUNK, 128), bf16),
            vmem((ZS, YS, XS, CHUNK, 128), bf16),
            vmem((2, XS, 4, YS, TOP, 128), bf16),
            vmem((2, XS, 4, YS, TOP, 128), bf16),
            vmem((2, YS, 4, XS, CHUNK - TOP, 128), bf16),
            vmem((2, 4, XS, CHUNK - TOP, 128), bf16),
            vmem((2, 4, TOP, 128), bf16),
            vmem((2, 4, TOP, 128), bf16),
            vmem((2, XS, 4, CHUNK - TOP, 128), bf16),
            vmem((2, XS, 4, CHUNK - TOP, 128), bf16),
            vmem((2, 4, TOP, 128), f32),
            vmem((2, 4, CHUNK - TOP, 128), f32),
            vmem((ZS, CHUNK, 128), bf16),
            vmem((ZS, CHUNK, 128), bf16),
            dma((ZS,)), dma((ZS,)), dma((2, XS)), dma((2, XS)), dma((2,)), dma((2,)),
            dma((2,)), dma((2,)), dma((2, XS)), dma((2, XS)), dma((ZS,)), dma((ZS,)),
        ],
        compiler_params=pltpu.CompilerParams(
            collective_id=1, has_side_effects=True, vmem_limit_bytes=56 << 20
        ),
    )(clip, cotangent, kernel_in, kernel_out)


def hand_over_kernel(sect_ref, in_ref, out_ref, sect_out, in_out, out_out):
    sect_out[...] = sect_ref[...]
    for k in range(27):
        in_out[:, pl.ds(256 * k, 256)] = in_ref[pl.ds(k, 1)]
    for k in range(54):
        out_out[:, pl.ds(128 * k, 128)] = out_ref[pl.ds(k, 1)]


def hand_over(sections, in_sum, out_sum):
    whole = pl.BlockSpec(memory_space=pltpu.VMEM)
    return pl.pallas_call(
        hand_over_kernel,
        out_shape=(
            jax.ShapeDtypeStruct(sections.shape, sections.dtype),
            jax.ShapeDtypeStruct((1, 6912), jnp.float32),
            jax.ShapeDtypeStruct((1, 6912), jnp.float32),
        ),
        in_specs=[whole] * 3,
        out_specs=(whole,) * 3,
    )(sections, in_sum, out_sum)


def on_device(tms, rows_count, input_clip, cotangent, kernel_in, kernel_out):
    sections, in_sum, out_sum = front(
        tms, rows_count, input_clip, cotangent,
        kernel_in.reshape(9, 3, 128, 256), kernel_out.reshape(9, 3, 256, 128),
    )
    sections, in_sum, out_sum = hand_over(sections, in_sum, out_sum)
    return (sections[None], in_sum, out_sum)


def solution(mesh):
    in_specs = (
        P("tm", "rows", None, None),
        P("tm", "rows", None, None),
        P("segment", None, None),
        P("segment", None, None),
    )
    out_specs = (
        P("segment", "tm", "rows", None, None),
        P("segment", ("tm", "rows")),
        P("segment", ("tm", "rows")),
    )
    return jax.shard_map(
        partial(on_device, mesh.shape["tm"], mesh.shape["rows"]),
        mesh=mesh, in_specs=in_specs, out_specs=out_specs, check_vma=False,
    )
```

```python
from functools import partial

import jax
import jax.numpy as jnp
from jax import lax
from jax.experimental import pallas as pl
from jax.experimental.pallas import tpu as pltpu
from jax.sharding import PartitionSpec as P

MESH_ID = pl.DeviceIdType.MESH
CORES, XS, YS, ZS = 2, 4, 2, 8
CHUNK = 112


TOP = 48
PIECES = 4
EACH = ZS // PIECES
EARLY, LATE = (6, 7, 8, 1, 4), (0, 2, 3, 5)
PLACES = EARLY + LATE


def shifted(line, by):
    rows = lax.broadcasted_iota(jnp.int32, line.shape, 0)
    if by == 1:
        return jnp.where(rows == 0, 0.0, pltpu.roll(line, 1, 0))
    return jnp.where(rows == 127, 0.0, pltpu.roll(line, 127, 0))


def joined(low, mid, high, reverse):
    if reverse:
        return shifted(low, -1) + mid + shifted(high, 1)
    return shifted(low, 1) + mid + shifted(high, -1)


class Link:
    def __init__(self, src, dst, sems, index, device, sends, receives):
        self.parts = (src, dst, sems[0].at[index], sems[1].at[index], device)
        self.sends = sends
        self.receives = receives

    def copy(self):
        src, dst, send_sem, recv_sem, device = self.parts
        return pltpu.make_async_remote_copy(
            src_ref=src, dst_ref=dst, send_sem=send_sem, recv_sem=recv_sem,
            device_id=device, device_id_type=MESH_ID,
        )

    def start(self):
        @pl.when(self.sends)
        def _():
            self.copy().start()

    def wait_recv(self):
        @pl.when(self.receives)
        def _():
            self.copy().wait_recv()

    def wait_send(self):
        @pl.when(self.sends)
        def _():
            self.copy().wait_send()


def front_kernel(
    tms, rows_count, x_hbm, g_hbm, kin_hbm, kout_hbm, sect_ref, in_ref, out_ref,
    kin_ref, kout_ref, s_load, back_ref, xp, gp, icx, icg, acc, hid, dgrad, act, gate, window, inner,
    sent_f, got_f, sum_f, got_zf, sent_b, got_b, sum_b, got_zb,
    wide_e, wide_a, act_t, icx_t, fin, fout,
    s_xp, r_xp, s_gp, r_gp, s_sf, r_sf, s_sb, r_sb, s_seg, r_seg,
    *reduce_refs,
):
    seg = lax.axis_index("segment")
    tm = lax.axis_index("tm")
    row = lax.axis_index("rows")
    encodes = seg == 0
    decodes = seg == 1
    later, earlier = tm + 1 < tms, tm > 0
    tm_later = {"tm": lax.rem(tm + 1, tms)}
    tm_earlier = {"tm": lax.rem(tm + tms - 1, tms)}
    other = {"segment": 1 - seg}
    other_next = {"segment": 1 - seg, "tm": lax.rem(tm + tms + 1 - 2 * seg, tms)}
    both = jnp.logical_and
    core, at_x, at_y = lax.rem(row, 2), lax.rem(row // 2, XS), row // (XS * CORES)

    step = 2 * core - 1
    crosses = both(row + step >= 0, row + step < rows_count)
    across = {"rows": lax.rem(row + step + rows_count, rows_count)}

    def x_at(offset):
        return lax.rem(at_x + offset, XS)

    sibling = {"rows": at_y * (XS * CORES) + at_x * 2 + 1 - core}
    across_y = {"rows": (1 - at_y) * (XS * CORES) + at_x * 2 + core}
    across_x = [{"rows": at_y * (XS * CORES) + x_at(o) * 2 + core} for o in range(1, XS)]
    in_time = [{"tm": lax.rem(tm + p, ZS)} for p in range(1, ZS)]
    load_in = pltpu.make_async_copy(kin_hbm, kin_ref, s_load.at[0])
    load_out = pltpu.make_async_copy(kout_hbm, kout_ref, s_load.at[1])
    load_in.start()
    load_out.start()

    xp[...] = jnp.zeros_like(xp)
    gp[...] = jnp.zeros_like(gp)
    got_f[...] = jnp.zeros_like(got_f)
    got_zf[...] = jnp.zeros_like(got_zf)
    got_b[...] = jnp.zeros_like(got_b)
    got_zb[...] = jnp.zeros_like(got_zb)

    load_x = pltpu.make_async_copy(x_hbm, xp.at[2:4, 1:3], s_load.at[2])
    load_g = pltpu.make_async_copy(g_hbm, gp.at[0:2, 1:3], s_load.at[3])

    @pl.when(encodes)
    def _():
        load_x.start()

    @pl.when(decodes)
    def _():
        load_g.start()

    barrier = pltpu.get_barrier_semaphore()
    partners = [across, other, other_next, sibling, across_y] + across_x + in_time
    for partner in partners:
        pl.semaphore_signal(barrier, inc=1, device_id=partner, device_id_type=MESH_ID)
    window[...] = jnp.zeros_like(window)

    @pl.when(encodes)
    def _():
        load_x.wait()

    @pl.when(decodes)
    def _():
        load_g.wait()

    pl.semaphore_wait(barrier, len(partners))

    inner_rows = (1 + core, 2 - core)
    row_devices = (across, sibling)
    edge_slots = (3 * (1 - core), 3 * core)
    outer_rows = (3 * core, 3 * (1 - core))
    row_exists = (crosses, True)

    def gather(buf, own, far, sems, to, sends, receives, arrivals, order, early, direct=None):
        edges, times, fars = [], [], []
        for k in range(2):
            device, slot = row_devices[k], edge_slots[k]
            edges.append(
                Link(buf.at[own, inner_rows[k]], buf.at[own, slot], sems, k, device, row_exists[k], row_exists[k])
            )
            times.append(
                Link(buf.at[own, inner_rows[k]], buf.at[far, inner_rows[k]], sems, 2 + k, to, sends, receives)
            )
            crossing = both(row_exists[k], receives)
            fars.append(
                Link(buf.at[far, inner_rows[k]], buf.at[far, slot], sems, 4 + k, device, crossing, crossing)
            )
        for k in order:
            if direct:
                arrivals[k]()
                edges[k].start()
                direct[k].wait_recv()
                fars[k].start()
            else:
                times[k].start()
                edges[k].start()
        if not direct:
            for k in order:
                times[k].wait_recv()
                fars[k].start()
        for link in edges:
            link.wait_recv()
        early()
        for link in fars:
            link.wait_recv()
        return edges + fars + ([] if direct else times)

    def columns(buf, dest, reverse, taps):
        for n in taps:
            t, i = n // 3, n % 3
            a, b = (2 - t, 2 - i) if reverse else (t, i)
            for f in range(2):
                for r in range(2):
                    dest[pl.ds((2 * f + r) * 128, 128), pl.ds(PLACES.index(n) * 128, 128)] = buf[a + f, b + r]

    def conv_part(taps, source, weights_of, contract, add):
        span = pl.ds(PLACES.index(taps[0]) * 128, len(taps) * 128)
        for j in range(3):
            product = lax.dot_general(
                source[:, span], weights_of(taps, j), (((1,), (contract,)), ((), ())),
                preferred_element_type=jnp.float32,
            )
            acc[j] = acc[j] + product if add else product

    def hidden_part(taps, add):
        columns(xp, icx, False, taps)
        conv_part(
            taps, icx, lambda ns, j: jnp.concatenate([kin_ref[n, j] for n in ns], axis=0), 0, add
        )

    def upstream_part(taps, add):
        columns(gp, icg, True, taps)
        conv_part(
            taps, icg, lambda ns, j: jnp.concatenate([kout_ref[n, j] for n in ns], axis=1), 1, add
        )

    def activate():
        def line(n, carry):
            at = pl.ds(pl.multiple_of(n * 128, 128), 128)
            value = joined(acc[0, at], acc[1, at], acc[2, at], False)
            hid[at] = value
            act[at] = (value / (1.0 + jnp.exp(-value))).astype(jnp.bfloat16)
            return carry

        lax.fori_loop(0, 4, line, 0)

    def keep_upstream():
        def line(n, carry):
            at = pl.ds(pl.multiple_of(n * 128, 128), 128)
            dgrad[at] = joined(acc[0, at], acc[1, at], acc[2, at], True)
            return carry

        lax.fori_loop(0, 4, line, 0)

    def gating():
        def line(n, carry):
            at = pl.ds(pl.multiple_of(n * 128, 128), 128)
            value = hid[at]
            sigmoid = 1.0 / (1.0 + jnp.exp(-value))
            gate[at] = (dgrad[at] * sigmoid * (1.0 + value * (1.0 - sigmoid))).astype(jnp.bfloat16)
            return carry

        lax.fori_loop(0, 4, line, 0)

    def scatter(source, reverse, sent, got, total, got_time, sems, to, sends, receives, finish):
        own, far = (2, 0) if reverse else (0, 2)
        first = 2 * core if reverse else 2 - 2 * core

        def products(t, i):
            n = 3 * t + i
            if reverse:
                product = lax.dot_general(
                    source[...], kin_ref[n].reshape(384, 256), (((1,), (1,)), ((), ())),
                    preferred_element_type=jnp.float32,
                )
                a, b = t, i
            else:
                weights = jnp.concatenate([kout_ref[n, j] for j in range(3)], axis=1)
                product = jnp.dot(source[...], weights, preferred_element_type=jnp.float32)
                a, b = 2 - t, 2 - i
            for f in range(2):
                for r in range(2):
                    window[a + f, b + r] += product[(2 * f + r) * 128 : (2 * f + r + 1) * 128]

        def value(f, r):
            return joined(
                window[f, r, :, 0:128], window[f, r, :, 128:256], window[f, r, :, 256:384], reverse
            )

        def send_edge(k, start, index, exists):
            for f in range(2):
                sent[k, start + f] = value(start + f, outer_rows[k]).astype(jnp.bfloat16)
            span = pl.ds(start, 2)
            goes = both(row_exists[k], exists)
            link = Link(sent.at[k, span], got.at[k, span], sems, index + k, row_devices[k], goes, goes)
            link.start()
            return link

        far_links, own_links = [], []
        for k, i in ((0, first), (1, 2 - first)):
            products(0, i)
            products(1, i)
            far_links.append(send_edge(k, far, 0, sends))
            products(2, i)
            own_links.append(send_edge(k, own, 2, True))
        for t in range(3):
            products(t, 1)
        time_links = []
        for k in (1, 0):
            far_links[k].wait_recv()
            for f in range(2):
                total[k, f] = (
                    value(far + f, inner_rows[k]) + got[k, far + f].astype(jnp.float32)
                ).astype(jnp.bfloat16)
            link = Link(total.at[k], got_time.at[k], sems, 4 + k, to, sends, receives)
            link.start()
            time_links.append(link)
        for k, link in zip((1, 0), time_links):
            for f in range(2):
                inner[k, f] = value(own + f, inner_rows[k])
            own_links[k].wait_recv()
            link.wait_recv()
            finish(
                k,
                [
                    inner[k, f] + got[k, own + f].astype(jnp.float32) + got_time[k, f].astype(jnp.float32)
                    for f in range(2)
                ],
            )
        return far_links + own_links + time_links

    own_x, far_x = pl.ds(2, 2), pl.ds(0, 2)
    own_g, far_g = pl.ds(0, 2), pl.ds(2, 2)
    seg_sems = (s_seg, r_seg)
    x_links, g_links, x_next, g_next = [], [], [], []
    for k in range(2):
        place = inner_rows[k]
        x_links.append(
            Link(sect_ref.at[:, place - 1], xp.at[own_x, place], seg_sems, k, other, encodes, decodes)
        )
        g_links.append(
            Link(back_ref.at[:, place - 1], gp.at[own_g, place], seg_sems, 2 + k, other, decodes, encodes)
        )
        x_next.append(
            Link(
                sect_ref.at[:, place - 1], xp.at[far_x, place], seg_sems, 4 + k, other_next,
                both(encodes, later), both(decodes, earlier),
            )
        )
        g_next.append(
            Link(
                back_ref.at[:, place - 1], gp.at[far_g, place], seg_sems, 6 + k, other_next,
                both(decodes, earlier), both(encodes, later),
            )
        )

    def gather_g(arrivals, order, ready, meanwhile, direct=None):
        def early():
            ready()
            upstream_part(EARLY, False)
            meanwhile()

        links = gather(
            gp, own_g, far_g, (s_gp, r_gp), tm_earlier, earlier, later, arrivals, order, early, direct
        )
        upstream_part(LATE, True)
        keep_upstream()
        for link in links:
            link.wait_send()

    def gather_x(arrivals, order, ready, direct=None):
        def early():
            ready()
            hidden_part(EARLY, False)

        links = gather(
            xp, own_x, far_x, (s_xp, r_xp), tm_later, later, earlier, arrivals, order,
            early, direct,
        )
        hidden_part(LATE, True)
        activate()
        for link in links:
            link.wait_send()

    def finish_x(k, sums):
        place = inner_rows[k]
        for f in range(2):
            sect_ref[f, place - 1] = (xp[f + 2, place].astype(jnp.float32) + sums[f]).astype(jnp.bfloat16)
        x_next[k].start()
        x_links[k].start()

    def finish_g(k, sums):
        place = inner_rows[k]
        for f in range(2):
            back_ref[f, place - 1] = (gp[f, place].astype(jnp.float32) + sums[f]).astype(jnp.bfloat16)
        g_next[k].start()
        g_links[k].start()

    def widen(source, dest, by):
        def line(n, carry):
            at = pl.ds(pl.multiple_of(n * 128, 128), 128)
            value = source[at].astype(jnp.float32)
            dest[at, 0:256] = shifted(value, by).astype(jnp.bfloat16)
            dest[at, 256:512] = source[at]
            dest[at, 512:768] = shifted(value, -by).astype(jnp.bfloat16)
            return carry

        lax.fori_loop(0, 4, line, 0)

    def prepare():
        widen(act, wide_a, 1)
        for n in range(6):
            act_t[pl.ds(n * 128, 128)] = wide_a[:, pl.ds(n * 128, 128)].T
        for n in range(9):
            icx_t[pl.ds(n * 128, 128)] = icx[:, pl.ds(n * 128, 128)].T

    def out_grad(taps):
        span = pl.ds(PLACES.index(taps[0]) * 128, len(taps) * 128)
        product = jnp.dot(act_t[...], icg[:, span], preferred_element_type=jnp.float32)
        for at, n in enumerate(taps):
            for j in range(3):
                fout[pl.ds((3 * n + j) * 256, 256)] = product[
                    j * 256 : (j + 1) * 256, at * 128 : (at + 1) * 128
                ]

    def in_grad():
        widen(gate, wide_e, -1)
        for group in range(3):
            product = jnp.dot(
                icx_t[pl.ds(group * 384, 384)], wide_e[...], preferred_element_type=jnp.float32
            )
            for i in range(3):
                for j in range(3):
                    fin[pl.ds((3 * PLACES[3 * group + i] + j) * 128, 128)] = product[
                        i * 128 : (i + 1) * 128, j * 256 : (j + 1) * 256
                    ]

    begin_reduce, end_reduce = reduce_scatter(
        fin, fout, in_ref, out_ref, tm, core, at_y, x_at, sibling, across_y, *reduce_refs
    )
    at_once = (lambda: None, lambda: None)

    def weights_there():
        load_in.wait()
        load_out.wait()

    @pl.when(encodes)
    def _():
        gather_x(at_once, (0, 1), weights_there)

    @pl.when(decodes)
    def _():
        gather_g(at_once, (0, 1), weights_there, lambda: None)
        gather_x([link.wait_recv for link in x_links], (1, 0), lambda: None, x_next)
        gating()
        back_links = scatter(
            gate, True, sent_b, got_b, sum_b, got_zb, (s_sb, r_sb), tm_earlier, earlier, later, finish_g
        )
        window[...] = jnp.zeros_like(window)
        for link in back_links:
            link.wait_send()
        prepare()
        out_grad(EARLY)
        out_grad(LATE)
        in_grad()
        begin_reduce()

    links = scatter(
        act, False, sent_f, got_f, sum_f, got_zf, (s_sf, r_sf), tm_later, later, earlier, finish_x
    )

    @pl.when(encodes)
    def _():
        prepare()
        gather_g(
            [link.wait_recv for link in g_links], (1, 0), lambda: None, lambda: out_grad(EARLY), g_next
        )
        gating()
        out_grad(LATE)
        in_grad()
        begin_reduce()

    end_reduce()
    for link in links + x_links + g_links + x_next + g_next:
        link.wait_send()


def reduce_scatter(
    fin, fout, in_ref, out_ref, tm, core, at_y, x_at, sibling, across_y,
    blocks, got_core, half_a, got_a, half_c, got_c, next_a, got_a2, next_c, got_c2,
    own_a, own_c, last, got_z,
    s_core, r_core, s_a, r_a, s_c, r_c, s_a2, r_a2, s_c2, r_c2, s_z, r_z,
):
    f32, bf16 = jnp.float32, jnp.bfloat16

    def made(src, dst, send_sem, recv_sem, device):
        return pltpu.make_async_remote_copy(
            src_ref=src, dst_ref=dst, send_sem=send_sem, recv_sem=recv_sem,
            device_id=device, device_id_type=MESH_ID,
        )

    def x_device(o):
        return {"rows": at_y * (XS * CORES) + x_at(o) * 2 + core}

    def core_copy(q):
        return pltpu.make_async_remote_copy(
            src_ref=blocks.at[q, :, :, 1 - core], dst_ref=got_core.at[q],
            send_sem=s_core.at[q], recv_sem=r_core.at[q],
            device_id=sibling, device_id_type=MESH_ID,
        )

    def pack(q, carry):
        odd = lax.rem(q, 2)
        offset = 4 + (1 - odd) * (q // 2) - odd * ((q + 1) // 2)
        z = lax.rem(tm + offset, ZS)
        ins = fin[pl.ds(pl.multiple_of(z * 432, 16), 432)]
        outs = fout[pl.ds(pl.multiple_of(z * 864, 16), 864)]
        pad = jnp.zeros((CHUNK - 108, 128), f32)
        for k in range(16):
            part = ins[27 * k : 27 * k + 27]
            block = jnp.concatenate([part[:, :128], part[:, 128:], outs[54 * k : 54 * k + 54], pad], axis=0)
            blocks[q, k // 8, k // 2 % 4, k % 2] = block.astype(bf16)
        core_copy(q).start()
        return carry

    def first_copies(h):
        copies = [
            made(half_a.at[h, o], got_a.at[h, o], s_a.at[h, o], r_a.at[h, o], x_device(o)) for o in (2, 1, 3)
        ]
        return copies + [made(half_c.at[h, 1], got_c.at[h], s_c.at[h], r_c.at[h], across_y)]

    def second_copies(h):
        copies = [made(next_a.at[h], got_a2.at[h], s_a2.at[h], r_a2.at[h], across_y)]
        return copies + [
            made(next_c.at[h, o], got_c2.at[h, o], s_c2.at[h, o], r_c2.at[h, o], x_device(o))
            for o in (2, 1, 3)
        ]

    def third_copy(q):
        offset = 4 + q // 2 if q % 2 == 0 else 4 - (q + 1) // 2
        device = {"tm": lax.rem(tm + offset, ZS)}
        return made(last.at[q], got_z.at[q], s_z.at[q], r_z.at[q], device)

    def add_core(q, carry):
        h, n = q // EACH, lax.rem(q, EACH)
        core_copy(q).wait_recv()
        for o in range(XS):
            for y in range(YS):
                x = x_at(o)
                side = lax.rem(at_y + y, 2)
                total = blocks[q, side, x, core].astype(f32) + got_core[q, side, x].astype(f32)
                half_a[h, o, n, y] = total[0:TOP].astype(bf16)
                half_c[h, y, n, o] = total[TOP:CHUNK].astype(bf16)
        return carry

    def begin():
        lax.fori_loop(0, 2 * EACH, pack, 0)
        for h in range(PIECES):
            lax.fori_loop(h * EACH, (h + 1) * EACH, add_core, 0)
            for copy in first_copies(h):
                copy.start()
            if h + 2 < PIECES:
                lax.fori_loop((h + 2) * EACH, (h + 3) * EACH, pack, 0)

    def second(h):
        for copy in first_copies(h):
            copy.wait_recv()

        def add_first(n, carry):
            for y in range(YS):
                total = half_a[h, 0, n, y].astype(f32)
                for o in range(1, XS):
                    total = total + got_a[h, o, n, y].astype(f32)
                if y == 0:
                    own_a[h, n] = total
                else:
                    next_a[h, n] = total.astype(bf16)
            for o in range(XS):
                total = half_c[h, 0, n, o].astype(f32) + got_c[h, n, o].astype(f32)
                if o == 0:
                    own_c[h, n] = total
                else:
                    next_c[h, o, n] = total.astype(bf16)
            return carry

        lax.fori_loop(0, EACH, add_first, 0)
        for copy in second_copies(h):
            copy.start()

    def third(h):
        for copy in second_copies(h):
            copy.wait_recv()
        total = None
        for n in range(EACH):
            q = EACH * h + n
            top = own_a[h, n] + got_a2[h, n].astype(f32)
            low = own_c[h, n]
            for o in range(1, XS):
                low = low + got_c2[h, o, n].astype(f32)
            total = jnp.concatenate([top, low], axis=0)
            if q < ZS - 1:
                last[q] = total.astype(bf16)
                third_copy(q).start()
        return total

    def end():
        second(0)
        for h in range(1, PIECES):
            second(h)
            third(h - 1)
        total = third(PIECES - 1)
        for q in range(ZS - 1):
            third_copy(q).wait_recv()
            total = total + got_z[q].astype(f32)
        in_ref[:, 0:128] = total[0:27]
        in_ref[:, 128:256] = total[27:54]
        out_ref[...] = total[54:108]
        for h in range(PIECES):
            for copy in first_copies(h) + second_copies(h):
                copy.wait_send()
        for q in range(ZS - 1):
            third_copy(q).wait_send()

        def drain(q, carry):
            core_copy(q).wait_send()
            return carry

        lax.fori_loop(0, ZS, drain, 0)

    return begin, end


def front(tms, rows_count, clip, cotangent, kernel_in, kernel_out):
    whole = pl.BlockSpec(memory_space=pltpu.VMEM)
    dma = pltpu.SemaphoreType.DMA
    bf16, f32 = jnp.bfloat16, jnp.float32
    vmem = pltpu.VMEM
    tile = (128, 128)
    return pl.pallas_call(
        partial(front_kernel, tms, rows_count),
        out_shape=(
            jax.ShapeDtypeStruct((2, 2) + tile, bf16),
            jax.ShapeDtypeStruct((27, 256), f32),
            jax.ShapeDtypeStruct((54, 128), f32),
        ),
        in_specs=[pl.BlockSpec(memory_space=pl.ANY)] * 4,
        out_specs=(whole, whole, whole),
        scratch_shapes=[
            vmem((9, 3, 128, 256), bf16),
            vmem((9, 3, 256, 128), bf16),
            dma((4,)),
            vmem((2, 2) + tile, bf16),
            vmem((4, 4) + tile, bf16),
            vmem((4, 4) + tile, bf16),
            vmem((512, 1152), bf16),
            vmem((512, 1152), bf16),
            vmem((3, 512, 256), f32),
            vmem((512, 256), f32),
            vmem((512, 256), f32),
            vmem((512, 256), bf16),
            vmem((512, 256), bf16),
            vmem((4, 4, 128, 384), f32),
            vmem((2, 2) + tile, f32),
        ]
        + [vmem((2, 4) + tile, bf16), vmem((2, 4) + tile, bf16), vmem((2, 2) + tile, bf16), vmem((2, 2) + tile, bf16)] * 2
        + [
            vmem((512, 768), bf16),
            vmem((512, 768), bf16),
            vmem((768, 512), bf16),
            vmem((1152, 512), bf16),
            vmem((3456, 256), f32),
            vmem((6912, 128), f32),
            dma((6,)), dma((6,)), dma((6,)), dma((6,)), dma((6,)), dma((6,)), dma((6,)), dma((6,)), dma((8,)), dma((8,)),
            vmem((ZS, YS, XS, CORES, CHUNK, 128), bf16),
            vmem((ZS, YS, XS, CHUNK, 128), bf16),
            vmem((PIECES, XS, EACH, YS, TOP, 128), bf16),
            vmem((PIECES, XS, EACH, YS, TOP, 128), bf16),
            vmem((PIECES, YS, EACH, XS, CHUNK - TOP, 128), bf16),
            vmem((PIECES, EACH, XS, CHUNK - TOP, 128), bf16),
            vmem((PIECES, EACH, TOP, 128), bf16),
            vmem((PIECES, EACH, TOP, 128), bf16),
            vmem((PIECES, XS, EACH, CHUNK - TOP, 128), bf16),
            vmem((PIECES, XS, EACH, CHUNK - TOP, 128), bf16),
            vmem((PIECES, EACH, TOP, 128), f32),
            vmem((PIECES, EACH, CHUNK - TOP, 128), f32),
            vmem((ZS, CHUNK, 128), bf16),
            vmem((ZS, CHUNK, 128), bf16),
            dma((ZS,)), dma((ZS,)), dma((PIECES, XS)), dma((PIECES, XS)), dma((PIECES,)), dma((PIECES,)),
            dma((PIECES,)), dma((PIECES,)), dma((PIECES, XS)), dma((PIECES, XS)), dma((ZS,)), dma((ZS,)),
        ],
        compiler_params=pltpu.CompilerParams(
            collective_id=1, has_side_effects=True, vmem_limit_bytes=56 << 20
        ),
    )(clip, cotangent, kernel_in, kernel_out)


def hand_over_kernel(sect_ref, in_ref, out_ref, sect_out, in_out, out_out):
    sect_out[...] = sect_ref[...]
    for k in range(27):
        in_out[:, pl.ds(256 * k, 256)] = in_ref[pl.ds(k, 1)]
    for k in range(54):
        out_out[:, pl.ds(128 * k, 128)] = out_ref[pl.ds(k, 1)]


def hand_over(sections, in_sum, out_sum):
    whole = pl.BlockSpec(memory_space=pltpu.VMEM)
    return pl.pallas_call(
        hand_over_kernel,
        out_shape=(
            jax.ShapeDtypeStruct(sections.shape, sections.dtype),
            jax.ShapeDtypeStruct((1, 6912), jnp.float32),
            jax.ShapeDtypeStruct((1, 6912), jnp.float32),
        ),
        in_specs=[whole] * 3,
        out_specs=(whole,) * 3,
    )(sections, in_sum, out_sum)


def on_device(tms, rows_count, input_clip, cotangent, kernel_in, kernel_out):
    sections, in_sum, out_sum = front(
        tms, rows_count, input_clip, cotangent,
        kernel_in.reshape(9, 3, 128, 256), kernel_out.reshape(9, 3, 256, 128),
    )
    sections, in_sum, out_sum = hand_over(sections, in_sum, out_sum)
    return (sections[None], in_sum, out_sum)


def solution(mesh):
    in_specs = (
        P("tm", "rows", None, None),
        P("tm", "rows", None, None),
        P("segment", None, None),
        P("segment", None, None),
    )
    out_specs = (
        P("segment", "tm", "rows", None, None),
        P("segment", ("tm", "rows")),
        P("segment", ("tm", "rows")),
    )
    return jax.shard_map(
        partial(on_device, mesh.shape["tm"], mesh.shape["rows"]),
        mesh=mesh, in_specs=in_specs, out_specs=out_specs, check_vma=False,
    )
```

```python
from functools import partial

import jax
import jax.numpy as jnp
from jax import lax
from jax.experimental import pallas as pl
from jax.experimental.pallas import tpu as pltpu
from jax.sharding import PartitionSpec as P

MESH_ID = pl.DeviceIdType.MESH
CORES, XS, YS, ZS = 2, 4, 2, 8
CHUNK = 112


TOP = 56
PIECES = 4
EACH = ZS // PIECES
EARLY, LATE = (6, 7, 8, 1, 4), (0, 2, 3, 5)
PLACES = EARLY + LATE


def shifted(line, by):
    rows = lax.broadcasted_iota(jnp.int32, line.shape, 0)
    if by == 1:
        return jnp.where(rows == 0, 0.0, pltpu.roll(line, 1, 0))
    return jnp.where(rows == 127, 0.0, pltpu.roll(line, 127, 0))


def joined(low, mid, high, reverse):
    if reverse:
        return shifted(low, -1) + mid + shifted(high, 1)
    return shifted(low, 1) + mid + shifted(high, -1)


class Link:
    def __init__(self, src, dst, sems, index, device, sends, receives):
        self.parts = (src, dst, sems[0].at[index], sems[1].at[index], device)
        self.sends = sends
        self.receives = receives

    def copy(self):
        src, dst, send_sem, recv_sem, device = self.parts
        return pltpu.make_async_remote_copy(
            src_ref=src, dst_ref=dst, send_sem=send_sem, recv_sem=recv_sem,
            device_id=device, device_id_type=MESH_ID,
        )

    def start(self):
        @pl.when(self.sends)
        def _():
            self.copy().start()

    def wait_recv(self):
        @pl.when(self.receives)
        def _():
            self.copy().wait_recv()

    def wait_send(self):
        @pl.when(self.sends)
        def _():
            self.copy().wait_send()


def front_kernel(
    tms, rows_count, x_hbm, g_hbm, kin_hbm, kout_hbm, sect_hbm, in_ref, out_ref,
    sect_ref, kin_ref, kout_ref, s_load, back_ref, xp, gp, icx, icg, acc, slope, dgrad, act, gate, window, inner,
    sent_f, got_f, sum_f, got_zf, sent_b, got_b, sum_b, got_zb,
    wide_e, wide_a, act_t, icx_t, fin, fout,
    s_xp, r_xp, s_gp, r_gp, s_sf, r_sf, s_sb, r_sb, s_seg, r_seg,
    *reduce_refs,
):
    seg = lax.axis_index("segment")
    tm = lax.axis_index("tm")
    row = lax.axis_index("rows")
    encodes = seg == 0
    decodes = seg == 1
    later, earlier = tm + 1 < tms, tm > 0
    tm_later = {"tm": lax.rem(tm + 1, tms)}
    tm_earlier = {"tm": lax.rem(tm + tms - 1, tms)}
    other = {"segment": 1 - seg}
    other_next = {"segment": 1 - seg, "tm": lax.rem(tm + tms + 1 - 2 * seg, tms)}
    both = jnp.logical_and
    core, at_x, at_y = lax.rem(row, 2), lax.rem(row // 2, XS), row // (XS * CORES)

    step = 2 * core - 1
    crosses = both(row + step >= 0, row + step < rows_count)
    across = {"rows": lax.rem(row + step + rows_count, rows_count)}

    def x_at(offset):
        return lax.rem(at_x + offset, XS)

    sibling = {"rows": at_y * (XS * CORES) + at_x * 2 + 1 - core}
    across_y = {"rows": (1 - at_y) * (XS * CORES) + at_x * 2 + core}
    across_x = [{"rows": at_y * (XS * CORES) + x_at(o) * 2 + core} for o in range(1, XS)]
    in_time = [{"tm": lax.rem(tm + p, ZS)} for p in range(1, ZS)]
    load_in = pltpu.make_async_copy(kin_hbm, kin_ref, s_load.at[0])
    load_out = pltpu.make_async_copy(kout_hbm, kout_ref, s_load.at[1])
    load_in.start()
    load_out.start()

    xp[...] = jnp.zeros_like(xp)
    gp[...] = jnp.zeros_like(gp)
    got_f[...] = jnp.zeros_like(got_f)
    got_zf[...] = jnp.zeros_like(got_zf)
    got_b[...] = jnp.zeros_like(got_b)
    got_zb[...] = jnp.zeros_like(got_zb)

    load_x = pltpu.make_async_copy(x_hbm, xp.at[2:4, 1:3], s_load.at[2])
    load_g = pltpu.make_async_copy(g_hbm, gp.at[0:2, 1:3], s_load.at[3])

    @pl.when(encodes)
    def _():
        load_x.start()

    @pl.when(decodes)
    def _():
        load_g.start()

    barrier = pltpu.get_barrier_semaphore()
    partners = [across, other, other_next, sibling, across_y] + across_x + in_time
    for partner in partners:
        pl.semaphore_signal(barrier, inc=1, device_id=partner, device_id_type=MESH_ID)
    window[...] = jnp.zeros_like(window)

    @pl.when(encodes)
    def _():
        load_x.wait()

    @pl.when(decodes)
    def _():
        load_g.wait()

    pl.semaphore_wait(barrier, len(partners))

    inner_rows = (1 + core, 2 - core)
    row_devices = (across, sibling)
    edge_slots = (3 * (1 - core), 3 * core)
    outer_rows = (3 * core, 3 * (1 - core))
    row_exists = (crosses, True)

    def gather(buf, own, far, sems, to, sends, receives, arrivals, early, direct=None):
        edges, times, fars = [], [], []
        for k in range(2):
            device, slot = row_devices[k], edge_slots[k]
            edges.append(
                Link(buf.at[own, inner_rows[k]], buf.at[own, slot], sems, k, device, row_exists[k], row_exists[k])
            )
            times.append(
                Link(buf.at[own, inner_rows[k]], buf.at[far, inner_rows[k]], sems, 2 + k, to, sends, receives)
            )
            crossing = both(row_exists[k], receives)
            fars.append(
                Link(buf.at[far, inner_rows[k]], buf.at[far, slot], sems, 4 + k, device, crossing, crossing)
            )
        if direct:
            arrivals[1]()
            times[1].start()
            edges[1].start()
            direct.wait_recv()
            fars[0].start()
            arrivals[0]()
            edges[0].start()
            times[1].wait_recv()
            fars[1].start()
        else:
            for k in (0, 1):
                times[k].start()
                edges[k].start()
            for k in (0, 1):
                times[k].wait_recv()
                fars[k].start()
        for link in edges:
            link.wait_recv()
        early()
        for link in fars:
            link.wait_recv()
        return edges + fars + (times[1:] if direct else times)

    def columns(buf, dest, reverse, taps):
        for n in taps:
            t, i = n // 3, n % 3
            a, b = (2 - t, 2 - i) if reverse else (t, i)
            for f in range(2):
                for r in range(2):
                    dest[pl.ds((2 * f + r) * 128, 128), pl.ds(PLACES.index(n) * 128, 128)] = buf[a + f, b + r]

    def conv_part(taps, source, weights_of, contract, add):
        span = pl.ds(PLACES.index(taps[0]) * 128, len(taps) * 128)
        for j in range(3):
            product = lax.dot_general(
                source[:, span], weights_of(taps, j), (((1,), (contract,)), ((), ())),
                preferred_element_type=jnp.float32,
            )
            acc[j] = acc[j] + product if add else product

    def hidden_part(taps, add):
        columns(xp, icx, False, taps)
        conv_part(
            taps, icx, lambda ns, j: jnp.concatenate([kin_ref[n, j] for n in ns], axis=0), 0, add
        )

    def upstream_part(taps, add):
        columns(gp, icg, True, taps)
        conv_part(
            taps, icg, lambda ns, j: jnp.concatenate([kout_ref[n, j] for n in ns], axis=1), 1, add
        )

    def activate():
        def line(n, carry):
            at = pl.ds(pl.multiple_of(n * 128, 128), 128)
            value = joined(acc[0, at], acc[1, at], acc[2, at], False)
            sigmoid = 1.0 / (1.0 + jnp.exp(-value))
            slope[at] = sigmoid * (1.0 + value * (1.0 - sigmoid))
            act[at] = (value * sigmoid).astype(jnp.bfloat16)
            return carry

        lax.fori_loop(0, 4, line, 0)

    def keep_upstream():
        def line(n, carry):
            at = pl.ds(pl.multiple_of(n * 128, 128), 128)
            dgrad[at] = joined(acc[0, at], acc[1, at], acc[2, at], True)
            return carry

        lax.fori_loop(0, 4, line, 0)

    def gating():
        def line(n, carry):
            at = pl.ds(pl.multiple_of(n * 128, 128), 128)
            gate[at] = (dgrad[at] * slope[at]).astype(jnp.bfloat16)
            return carry

        lax.fori_loop(0, 4, line, 0)

    def scatter(source, reverse, sent, got, total, got_time, sems, to, sends, receives, finish):
        own, far = (2, 0) if reverse else (0, 2)
        first = 2 * core if reverse else 2 - 2 * core

        def products(t, i):
            n = 3 * t + i
            if reverse:
                product = lax.dot_general(
                    source[...], kin_ref[n].reshape(384, 256), (((1,), (1,)), ((), ())),
                    preferred_element_type=jnp.float32,
                )
                a, b = t, i
            else:
                weights = jnp.concatenate([kout_ref[n, j] for j in range(3)], axis=1)
                product = jnp.dot(source[...], weights, preferred_element_type=jnp.float32)
                a, b = 2 - t, 2 - i
            for f in range(2):
                for r in range(2):
                    window[a + f, b + r] += product[(2 * f + r) * 128 : (2 * f + r + 1) * 128]

        def value(f, r):
            return joined(
                window[f, r, :, 0:128], window[f, r, :, 128:256], window[f, r, :, 256:384], reverse
            )

        def send_edge(k, start, index, exists):
            for f in range(2):
                sent[k, start + f] = value(start + f, outer_rows[k]).astype(jnp.bfloat16)
            span = pl.ds(start, 2)
            goes = both(row_exists[k], exists)
            link = Link(sent.at[k, span], got.at[k, span], sems, index + k, row_devices[k], goes, goes)
            link.start()
            return link

        far_links, own_links = [], []
        for k, i in ((0, first), (1, 2 - first)):
            products(0, i)
            products(1, i)
            far_links.append(send_edge(k, far, 0, sends))
            products(2, i)
            own_links.append(send_edge(k, own, 2, True))
        for t in range(3):
            products(t, 1)
        time_links = []
        for k in (1, 0):
            far_links[k].wait_recv()
            for f in range(2):
                total[k, f] = (
                    value(far + f, inner_rows[k]) + got[k, far + f].astype(jnp.float32)
                ).astype(jnp.bfloat16)
            link = Link(total.at[k], got_time.at[k], sems, 4 + k, to, sends, receives)
            link.start()
            time_links.append(link)
        for k, link in zip((1, 0), time_links):
            for f in range(2):
                inner[k, f] = value(own + f, inner_rows[k])
            own_links[k].wait_recv()
            link.wait_recv()
            finish(
                k,
                [
                    inner[k, f] + got[k, own + f].astype(jnp.float32) + got_time[k, f].astype(jnp.float32)
                    for f in range(2)
                ],
            )
        return far_links + own_links + time_links

    own_x, far_x = pl.ds(2, 2), pl.ds(0, 2)
    own_g, far_g = pl.ds(0, 2), pl.ds(2, 2)
    seg_sems = (s_seg, r_seg)
    x_links, g_links = [], []
    for k in range(2):
        place = inner_rows[k]
        x_links.append(
            Link(sect_ref.at[:, place - 1], xp.at[own_x, place], seg_sems, k, other, encodes, decodes)
        )
        g_links.append(
            Link(back_ref.at[:, place - 1], gp.at[own_g, place], seg_sems, 2 + k, other, decodes, encodes)
        )
    x_next = Link(
        sect_ref.at[:, core], xp.at[far_x, 1 + core], seg_sems, 4, other_next,
        both(encodes, later), both(decodes, earlier),
    )
    g_next = Link(
        back_ref.at[:, core], gp.at[far_g, 1 + core], seg_sems, 5, other_next,
        both(decodes, earlier), both(encodes, later),
    )

    def gather_g(arrivals, ready, meanwhile, direct=None):
        def early():
            ready()
            upstream_part(EARLY, False)
            meanwhile()

        links = gather(
            gp, own_g, far_g, (s_gp, r_gp), tm_earlier, earlier, later, arrivals, early, direct
        )
        upstream_part(LATE, True)
        keep_upstream()
        for link in links:
            link.wait_send()

    def gather_x(arrivals, ready, direct=None):
        def early():
            ready()
            hidden_part(EARLY, False)

        links = gather(
            xp, own_x, far_x, (s_xp, r_xp), tm_later, later, earlier, arrivals,
            early, direct,
        )
        hidden_part(LATE, True)
        activate()
        for link in links:
            link.wait_send()

    def finish_x(k, sums):
        place = inner_rows[k]
        for f in range(2):
            sect_ref[f, place - 1] = (xp[f + 2, place].astype(jnp.float32) + sums[f]).astype(jnp.bfloat16)
        if k == 0:
            x_next.start()
        x_links[k].start()

    def finish_g(k, sums):
        place = inner_rows[k]
        for f in range(2):
            back_ref[f, place - 1] = (gp[f, place].astype(jnp.float32) + sums[f]).astype(jnp.bfloat16)
        if k == 0:
            g_next.start()
        g_links[k].start()

    def widen(source, dest, by):
        def line(n, carry):
            at = pl.ds(pl.multiple_of(n * 128, 128), 128)
            value = source[at].astype(jnp.float32)
            dest[at, 0:256] = shifted(value, by).astype(jnp.bfloat16)
            dest[at, 256:512] = source[at]
            dest[at, 512:768] = shifted(value, -by).astype(jnp.bfloat16)
            return carry

        lax.fori_loop(0, 4, line, 0)

    def prepare():
        widen(act, wide_a, 1)
        for n in range(6):
            act_t[pl.ds(n * 128, 128)] = wide_a[:, pl.ds(n * 128, 128)].T
        for n in range(9):
            icx_t[pl.ds(n * 128, 128)] = icx[:, pl.ds(n * 128, 128)].T

    def out_grad(taps):
        span = pl.ds(PLACES.index(taps[0]) * 128, len(taps) * 128)
        product = jnp.dot(act_t[...], icg[:, span], preferred_element_type=jnp.float32)
        for at, n in enumerate(taps):
            for j in range(3):
                fout[pl.ds((3 * n + j) * 256, 256)] = product[
                    j * 256 : (j + 1) * 256, at * 128 : (at + 1) * 128
                ]

    def in_grad():
        widen(gate, wide_e, -1)
        for group in range(3):
            product = jnp.dot(
                icx_t[pl.ds(group * 384, 384)], wide_e[...], preferred_element_type=jnp.float32
            )
            for i in range(3):
                for j in range(3):
                    fin[pl.ds((3 * PLACES[3 * group + i] + j) * 128, 128)] = product[
                        i * 128 : (i + 1) * 128, j * 256 : (j + 1) * 256
                    ]

    begin_reduce, end_reduce = reduce_scatter(
        fin, fout, in_ref, out_ref, tm, core, at_y, x_at, sibling, across_y, *reduce_refs
    )

    def weights_there():
        load_in.wait()
        load_out.wait()

    @pl.when(encodes)
    def _():
        gather_x(None, weights_there)

    @pl.when(decodes)
    def _():
        gather_g(None, weights_there, lambda: None)
        gather_x([link.wait_recv for link in x_links], lambda: None, x_next)
        gating()
        back_links = scatter(
            gate, True, sent_b, got_b, sum_b, got_zb, (s_sb, r_sb), tm_earlier, earlier, later, finish_g
        )
        window[...] = jnp.zeros_like(window)
        for link in back_links:
            link.wait_send()
        prepare()
        out_grad(EARLY)
        out_grad(LATE)
        in_grad()
        begin_reduce()

    links = scatter(
        act, False, sent_f, got_f, sum_f, got_zf, (s_sf, r_sf), tm_later, later, earlier, finish_x
    )

    @pl.when(encodes)
    def _():
        prepare()
        gather_g(
            [link.wait_recv for link in g_links], lambda: None, lambda: out_grad(EARLY), g_next
        )
        gating()
        out_grad(LATE)
        in_grad()
        begin_reduce()

    store = pltpu.make_async_copy(sect_ref, sect_hbm, s_load.at[4])
    store.start()
    end_reduce()
    store.wait()
    for link in links + x_links + g_links + [x_next, g_next]:
        link.wait_send()


def reduce_scatter(
    fin, fout, in_ref, out_ref, tm, core, at_y, x_at, sibling, across_y,
    blocks, got_core, half_a, got_a, half_c, got_c, next_a, got_a2, next_c, got_c2,
    own_a, own_c, last, got_z,
    s_core, r_core, s_a, r_a, s_c, r_c, s_a2, r_a2, s_c2, r_c2, s_z, r_z,
):
    f32, bf16 = jnp.float32, jnp.bfloat16

    def made(src, dst, send_sem, recv_sem, device):
        return pltpu.make_async_remote_copy(
            src_ref=src, dst_ref=dst, send_sem=send_sem, recv_sem=recv_sem,
            device_id=device, device_id_type=MESH_ID,
        )

    def x_device(o):
        return {"rows": at_y * (XS * CORES) + x_at(o) * 2 + core}

    def core_copy(q):
        return pltpu.make_async_remote_copy(
            src_ref=blocks.at[q, :, :, 1 - core], dst_ref=got_core.at[q],
            send_sem=s_core.at[q], recv_sem=r_core.at[q],
            device_id=sibling, device_id_type=MESH_ID,
        )

    def pack(q, carry):
        odd = lax.rem(q, 2)
        offset = 4 + (1 - odd) * (q // 2) - odd * ((q + 1) // 2)
        z = lax.rem(tm + offset, ZS)
        ins = fin[pl.ds(pl.multiple_of(z * 432, 16), 432)]
        outs = fout[pl.ds(pl.multiple_of(z * 864, 16), 864)]
        pad = jnp.zeros((CHUNK - 108, 128), f32)
        for k in range(16):
            part = ins[27 * k : 27 * k + 27]
            block = jnp.concatenate([part[:, :128], part[:, 128:], outs[54 * k : 54 * k + 54], pad], axis=0)
            blocks[q, k // 8, k // 2 % 4, k % 2] = block.astype(bf16)
        core_copy(q).start()
        return carry

    def first_copies(h):
        copies = [
            made(half_a.at[h, o], got_a.at[h, o], s_a.at[h, o], r_a.at[h, o], x_device(o)) for o in (2, 1, 3)
        ]
        return copies + [made(half_c.at[h, 1], got_c.at[h], s_c.at[h], r_c.at[h], across_y)]

    def second_copies(h):
        copies = [made(next_a.at[h], got_a2.at[h], s_a2.at[h], r_a2.at[h], across_y)]
        return copies + [
            made(next_c.at[h, o], got_c2.at[h, o], s_c2.at[h, o], r_c2.at[h, o], x_device(o))
            for o in (2, 1, 3)
        ]

    def third_copy(q):
        offset = 4 + q // 2 if q % 2 == 0 else 4 - (q + 1) // 2
        device = {"tm": lax.rem(tm + offset, ZS)}
        return made(last.at[q], got_z.at[q], s_z.at[q], r_z.at[q], device)

    def add_core(q, carry):
        h, n = q // EACH, lax.rem(q, EACH)
        core_copy(q).wait_recv()
        for o in range(XS):
            for y in range(YS):
                x = x_at(o)
                side = lax.rem(at_y + y, 2)
                total = blocks[q, side, x, core].astype(f32) + got_core[q, side, x].astype(f32)
                half_a[h, o, n, y] = total[0:TOP].astype(bf16)
                half_c[h, y, n, o] = total[TOP:CHUNK].astype(bf16)
        return carry

    def begin():
        lax.fori_loop(0, 2 * EACH, pack, 0)
        for h in range(PIECES):
            lax.fori_loop(h * EACH, (h + 1) * EACH, add_core, 0)
            for copy in first_copies(h):
                copy.start()
            if h + 2 < PIECES:
                lax.fori_loop((h + 2) * EACH, (h + 3) * EACH, pack, 0)

    def second(h):
        for copy in first_copies(h):
            copy.wait_recv()

        def add_first(n, carry):
            for y in range(YS):
                total = half_a[h, 0, n, y].astype(f32)
                for o in range(1, XS):
                    total = total + got_a[h, o, n, y].astype(f32)
                if y == 0:
                    own_a[h, n] = total
                else:
                    next_a[h, n] = total.astype(bf16)
            for o in range(XS):
                total = half_c[h, 0, n, o].astype(f32) + got_c[h, n, o].astype(f32)
                if o == 0:
                    own_c[h, n] = total
                else:
                    next_c[h, o, n] = total.astype(bf16)
            return carry

        lax.fori_loop(0, EACH, add_first, 0)
        for copy in second_copies(h):
            copy.start()

    def third(h):
        for copy in second_copies(h):
            copy.wait_recv()
        total = None
        for n in range(EACH):
            q = EACH * h + n
            top = own_a[h, n] + got_a2[h, n].astype(f32)
            low = own_c[h, n]
            for o in range(1, XS):
                low = low + got_c2[h, o, n].astype(f32)
            total = jnp.concatenate([top, low], axis=0)
            if q < ZS - 1:
                last[q] = total.astype(bf16)
                third_copy(q).start()
        return total

    def end():
        second(0)
        for h in range(1, PIECES):
            second(h)
            third(h - 1)
        total = third(PIECES - 1)
        for q in range(ZS - 1):
            third_copy(q).wait_recv()
            total = total + got_z[q].astype(f32)
        in_ref[:, 0:128] = total[0:27]
        in_ref[:, 128:256] = total[27:54]
        out_ref[...] = total[54:108]
        for h in range(PIECES):
            for copy in first_copies(h) + second_copies(h):
                copy.wait_send()
        for q in range(ZS - 1):
            third_copy(q).wait_send()

        def drain(q, carry):
            core_copy(q).wait_send()
            return carry

        lax.fori_loop(0, ZS, drain, 0)

    return begin, end


def front(tms, rows_count, clip, cotangent, kernel_in, kernel_out):
    whole = pl.BlockSpec(memory_space=pltpu.VMEM)
    dma = pltpu.SemaphoreType.DMA
    bf16, f32 = jnp.bfloat16, jnp.float32
    vmem = pltpu.VMEM
    tile = (128, 128)
    return pl.pallas_call(
        partial(front_kernel, tms, rows_count),
        out_shape=(
            jax.ShapeDtypeStruct((2, 2) + tile, bf16),
            jax.ShapeDtypeStruct((27, 256), f32),
            jax.ShapeDtypeStruct((54, 128), f32),
        ),
        in_specs=[pl.BlockSpec(memory_space=pl.ANY)] * 4,
        out_specs=(pl.BlockSpec(memory_space=pl.ANY), whole, whole),
        scratch_shapes=[
            vmem((2, 2) + tile, bf16),
            vmem((9, 3, 128, 256), bf16),
            vmem((9, 3, 256, 128), bf16),
            dma((5,)),
            vmem((2, 2) + tile, bf16),
            vmem((4, 4) + tile, bf16),
            vmem((4, 4) + tile, bf16),
            vmem((512, 1152), bf16),
            vmem((512, 1152), bf16),
            vmem((3, 512, 256), f32),
            vmem((512, 256), f32),
            vmem((512, 256), f32),
            vmem((512, 256), bf16),
            vmem((512, 256), bf16),
            vmem((4, 4, 128, 384), f32),
            vmem((2, 2) + tile, f32),
        ]
        + [vmem((2, 4) + tile, bf16), vmem((2, 4) + tile, bf16), vmem((2, 2) + tile, bf16), vmem((2, 2) + tile, bf16)] * 2
        + [
            vmem((512, 768), bf16),
            vmem((512, 768), bf16),
            vmem((768, 512), bf16),
            vmem((1152, 512), bf16),
            vmem((3456, 256), f32),
            vmem((6912, 128), f32),
            dma((6,)), dma((6,)), dma((6,)), dma((6,)), dma((6,)), dma((6,)), dma((6,)), dma((6,)), dma((6,)), dma((6,)),
            vmem((ZS, YS, XS, CORES, CHUNK, 128), bf16),
            vmem((ZS, YS, XS, CHUNK, 128), bf16),
            vmem((PIECES, XS, EACH, YS, TOP, 128), bf16),
            vmem((PIECES, XS, EACH, YS, TOP, 128), bf16),
            vmem((PIECES, YS, EACH, XS, CHUNK - TOP, 128), bf16),
            vmem((PIECES, EACH, XS, CHUNK - TOP, 128), bf16),
            vmem((PIECES, EACH, TOP, 128), bf16),
            vmem((PIECES, EACH, TOP, 128), bf16),
            vmem((PIECES, XS, EACH, CHUNK - TOP, 128), bf16),
            vmem((PIECES, XS, EACH, CHUNK - TOP, 128), bf16),
            vmem((PIECES, EACH, TOP, 128), f32),
            vmem((PIECES, EACH, CHUNK - TOP, 128), f32),
            vmem((ZS, CHUNK, 128), bf16),
            vmem((ZS, CHUNK, 128), bf16),
            dma((ZS,)), dma((ZS,)), dma((PIECES, XS)), dma((PIECES, XS)), dma((PIECES,)), dma((PIECES,)),
            dma((PIECES,)), dma((PIECES,)), dma((PIECES, XS)), dma((PIECES, XS)), dma((ZS,)), dma((ZS,)),
        ],
        compiler_params=pltpu.CompilerParams(
            collective_id=1, has_side_effects=True, vmem_limit_bytes=56 << 20
        ),
    )(clip, cotangent, kernel_in, kernel_out)


def hand_over_kernel(sect_hbm, in_ref, out_ref, sect_out, in_out, out_out, sem):
    copy = pltpu.make_async_copy(sect_hbm, sect_out, sem)
    copy.start()
    for k in range(27):
        in_out[:, pl.ds(256 * k, 256)] = in_ref[pl.ds(k, 1)]
    for k in range(54):
        out_out[:, pl.ds(128 * k, 128)] = out_ref[pl.ds(k, 1)]
    copy.wait()


def hand_over(sections, in_sum, out_sum):
    whole, anywhere = pl.BlockSpec(memory_space=pltpu.VMEM), pl.BlockSpec(memory_space=pl.ANY)
    return pl.pallas_call(
        hand_over_kernel,
        out_shape=(
            jax.ShapeDtypeStruct(sections.shape, sections.dtype),
            jax.ShapeDtypeStruct((1, 6912), jnp.float32),
            jax.ShapeDtypeStruct((1, 6912), jnp.float32),
        ),
        in_specs=[anywhere, whole, whole],
        out_specs=(anywhere, whole, whole),
        scratch_shapes=[pltpu.SemaphoreType.DMA],
    )(sections, in_sum, out_sum)


def on_device(tms, rows_count, input_clip, cotangent, kernel_in, kernel_out):
    sections, in_sum, out_sum = front(
        tms, rows_count, input_clip, cotangent,
        kernel_in.reshape(9, 3, 128, 256), kernel_out.reshape(9, 3, 256, 128),
    )
    sections, in_sum, out_sum = hand_over(sections, in_sum, out_sum)
    return (sections[None], in_sum, out_sum)


def solution(mesh):
    in_specs = (
        P("tm", "rows", None, None),
        P("tm", "rows", None, None),
        P("segment", None, None),
        P("segment", None, None),
    )
    out_specs = (
        P("segment", "tm", "rows", None, None),
        P("segment", ("tm", "rows")),
        P("segment", ("tm", "rows")),
    )
    return jax.shard_map(
        partial(on_device, mesh.shape["tm"], mesh.shape["rows"]),
        mesh=mesh, in_specs=in_specs, out_specs=out_specs, check_vma=False,
    )
```

```python
from functools import partial

import jax
import jax.numpy as jnp
from jax import lax
from jax.experimental import pallas as pl
from jax.experimental.pallas import tpu as pltpu
from jax.sharding import PartitionSpec as P

MESH_ID = pl.DeviceIdType.MESH
CORES, XS, YS, ZS = 2, 4, 2, 8
CHUNK = 112


TOP = 48
PIECES = 2
EACH = ZS // PIECES
EARLY, LATE = (6, 7, 8, 1, 4), (0, 2, 3, 5)
PLACES = EARLY + LATE


def shifted(line, by):
    rows = lax.broadcasted_iota(jnp.int32, line.shape, 0)
    if by == 1:
        return jnp.where(rows == 0, 0.0, pltpu.roll(line, 1, 0))
    return jnp.where(rows == 127, 0.0, pltpu.roll(line, 127, 0))


def joined(low, mid, high, reverse):
    if reverse:
        return shifted(low, -1) + mid + shifted(high, 1)
    return shifted(low, 1) + mid + shifted(high, -1)


class Link:
    def __init__(self, src, dst, sems, index, device, sends, receives):
        self.parts = (src, dst, sems[0].at[index], sems[1].at[index], device)
        self.sends = sends
        self.receives = receives

    def copy(self):
        src, dst, send_sem, recv_sem, device = self.parts
        return pltpu.make_async_remote_copy(
            src_ref=src, dst_ref=dst, send_sem=send_sem, recv_sem=recv_sem,
            device_id=device, device_id_type=MESH_ID,
        )

    def start(self):
        @pl.when(self.sends)
        def _():
            self.copy().start()

    def wait_recv(self):
        @pl.when(self.receives)
        def _():
            self.copy().wait_recv()

    def wait_send(self):
        @pl.when(self.sends)
        def _():
            self.copy().wait_send()


def front_kernel(
    tms, rows_count, x_hbm, g_hbm, kin_hbm, kout_hbm, sect_hbm, in_ref, out_ref,
    sect_ref, kin_ref, kout_ref, s_load, back_ref, xp, gp, icx, icg, acc, slope, dgrad, act, gate, window, inner,
    sent_f, got_f, sum_f, got_zf, sent_b, got_b, sum_b, got_zb,
    wide_e, wide_a, act_t, icx_t, fin, fout,
    s_xp, r_xp, s_gp, r_gp, s_sf, r_sf, s_sb, r_sb, s_seg, r_seg,
    *reduce_refs,
):
    seg = lax.axis_index("segment")
    tm = lax.axis_index("tm")
    row = lax.axis_index("rows")
    encodes = seg == 0
    decodes = seg == 1
    later, earlier = tm + 1 < tms, tm > 0
    tm_later = {"tm": lax.rem(tm + 1, tms)}
    tm_earlier = {"tm": lax.rem(tm + tms - 1, tms)}
    other = {"segment": 1 - seg}
    other_next = {"segment": 1 - seg, "tm": lax.rem(tm + tms + 1 - 2 * seg, tms)}
    both = jnp.logical_and
    core, at_x, at_y = lax.rem(row, 2), lax.rem(row // 2, XS), row // (XS * CORES)

    step = 2 * core - 1
    crosses = both(row + step >= 0, row + step < rows_count)
    across_row = lax.rem(row + step + rows_count, rows_count)
    across = {"rows": across_row}
    border = both(crosses, at_y != across_row // (XS * CORES))
    inside = jnp.logical_not(border)
    other_across = {"segment": 1 - seg, "rows": across_row}
    other_across_next = {
        "segment": 1 - seg, "tm": lax.rem(tm + tms + 1 - 2 * seg, tms), "rows": across_row
    }

    def x_at(offset):
        return lax.rem(at_x + offset, XS)

    sibling = {"rows": at_y * (XS * CORES) + at_x * 2 + 1 - core}
    across_y = {"rows": (1 - at_y) * (XS * CORES) + at_x * 2 + core}
    across_x = [{"rows": at_y * (XS * CORES) + x_at(o) * 2 + core} for o in range(1, XS)]
    in_time = [{"tm": lax.rem(tm + p, ZS)} for p in range(1, ZS)]
    load_in = pltpu.make_async_copy(kin_hbm, kin_ref, s_load.at[0])
    load_out = pltpu.make_async_copy(kout_hbm, kout_ref, s_load.at[1])
    load_in.start()
    load_out.start()

    xp[...] = jnp.zeros_like(xp)
    gp[...] = jnp.zeros_like(gp)
    got_f[...] = jnp.zeros_like(got_f)
    got_zf[...] = jnp.zeros_like(got_zf)
    got_b[...] = jnp.zeros_like(got_b)
    got_zb[...] = jnp.zeros_like(got_zb)

    load_x = pltpu.make_async_copy(x_hbm, xp.at[2:4, 1:3], s_load.at[2])
    load_g = pltpu.make_async_copy(g_hbm, gp.at[0:2, 1:3], s_load.at[3])

    @pl.when(encodes)
    def _():
        load_x.start()

    @pl.when(decodes)
    def _():
        load_g.start()

    barrier = pltpu.get_barrier_semaphore()
    partners = [across, other, other_next, other_across, other_across_next, sibling, across_y] + across_x + in_time
    for partner in partners:
        pl.semaphore_signal(barrier, inc=1, device_id=partner, device_id_type=MESH_ID)
    window[...] = jnp.zeros_like(window)

    @pl.when(encodes)
    def _():
        load_x.wait()

    @pl.when(decodes)
    def _():
        load_g.wait()

    pl.semaphore_wait(barrier, len(partners))

    inner_rows = (1 + core, 2 - core)
    row_devices = (across, sibling)
    edge_slots = (3 * (1 - core), 3 * core)
    outer_rows = (3 * core, 3 * (1 - core))
    row_exists = (crosses, True)

    def gather(buf, own, far, sems, to, sends, receives, arrivals, early, direct=None):
        edges, times, fars = [], [], []
        for k in range(2):
            device, slot = row_devices[k], edge_slots[k]
            exists = both(row_exists[k], inside) if direct and k == 0 else row_exists[k]
            edges.append(
                Link(buf.at[own, inner_rows[k]], buf.at[own, slot], sems, k, device, exists, exists)
            )
            times.append(
                Link(buf.at[own, inner_rows[k]], buf.at[far, inner_rows[k]], sems, 2 + k, to, sends, receives)
            )
            crossing = both(exists, receives)
            fars.append(
                Link(buf.at[far, inner_rows[k]], buf.at[far, slot], sems, 4 + k, device, crossing, crossing)
            )
        if direct:
            arrivals[1]()
            times[1].start()
            edges[1].start()
            direct[0].wait_recv()
            fars[0].start()
            arrivals[0]()
            edges[0].start()
            times[1].wait_recv()
            fars[1].start()
        else:
            for k in (0, 1):
                times[k].start()
                edges[k].start()
            for k in (0, 1):
                times[k].wait_recv()
                fars[k].start()
        for link in edges + (direct[2:] if direct else []):
            link.wait_recv()
        early()
        for link in fars + (direct[1:2] if direct else []):
            link.wait_recv()
        return edges + fars + (times[1:] if direct else times)

    def columns(buf, dest, reverse, taps):
        for n in taps:
            t, i = n // 3, n % 3
            a, b = (2 - t, 2 - i) if reverse else (t, i)
            for f in range(2):
                for r in range(2):
                    dest[pl.ds((2 * f + r) * 128, 128), pl.ds(PLACES.index(n) * 128, 128)] = buf[a + f, b + r]

    def conv_part(taps, source, weights_of, contract, add):
        span = pl.ds(PLACES.index(taps[0]) * 128, len(taps) * 128)
        for j in range(3):
            product = lax.dot_general(
                source[:, span], weights_of(taps, j), (((1,), (contract,)), ((), ())),
                preferred_element_type=jnp.float32,
            )
            acc[j] = acc[j] + product if add else product

    def hidden_part(taps, add):
        columns(xp, icx, False, taps)
        conv_part(
            taps, icx, lambda ns, j: jnp.concatenate([kin_ref[n, j] for n in ns], axis=0), 0, add
        )

    def upstream_part(taps, add):
        columns(gp, icg, True, taps)
        conv_part(
            taps, icg, lambda ns, j: jnp.concatenate([kout_ref[n, j] for n in ns], axis=1), 1, add
        )

    def activate():
        def line(n, carry):
            at = pl.ds(pl.multiple_of(n * 128, 128), 128)
            value = joined(acc[0, at], acc[1, at], acc[2, at], False)
            sigmoid = 1.0 / (1.0 + jnp.exp(-value))
            slope[at] = sigmoid * (1.0 + value * (1.0 - sigmoid))
            act[at] = (value * sigmoid).astype(jnp.bfloat16)
            return carry

        lax.fori_loop(0, 4, line, 0)

    def keep_upstream():
        def line(n, carry):
            at = pl.ds(pl.multiple_of(n * 128, 128), 128)
            dgrad[at] = joined(acc[0, at], acc[1, at], acc[2, at], True)
            return carry

        lax.fori_loop(0, 4, line, 0)

    def gating():
        def line(n, carry):
            at = pl.ds(pl.multiple_of(n * 128, 128), 128)
            gate[at] = (dgrad[at] * slope[at]).astype(jnp.bfloat16)
            return carry

        lax.fori_loop(0, 4, line, 0)

    def scatter(source, reverse, sent, got, total, got_time, sems, to, sends, receives, finish):
        own, far = (2, 0) if reverse else (0, 2)
        first = 2 * core if reverse else 2 - 2 * core

        def products(t, i):
            n = 3 * t + i
            if reverse:
                product = lax.dot_general(
                    source[...], kin_ref[n].reshape(384, 256), (((1,), (1,)), ((), ())),
                    preferred_element_type=jnp.float32,
                )
                a, b = t, i
            else:
                weights = jnp.concatenate([kout_ref[n, j] for j in range(3)], axis=1)
                product = jnp.dot(source[...], weights, preferred_element_type=jnp.float32)
                a, b = 2 - t, 2 - i
            for f in range(2):
                for r in range(2):
                    window[a + f, b + r] += product[(2 * f + r) * 128 : (2 * f + r + 1) * 128]

        def value(f, r):
            return joined(
                window[f, r, :, 0:128], window[f, r, :, 128:256], window[f, r, :, 256:384], reverse
            )

        def send_edge(k, start, index, exists):
            for f in range(2):
                sent[k, start + f] = value(start + f, outer_rows[k]).astype(jnp.bfloat16)
            span = pl.ds(start, 2)
            goes = both(row_exists[k], exists)
            link = Link(sent.at[k, span], got.at[k, span], sems, index + k, row_devices[k], goes, goes)
            link.start()
            return link

        far_links, own_links = [], []
        for k, i in ((0, first), (1, 2 - first)):
            products(0, i)
            products(1, i)
            far_links.append(send_edge(k, far, 0, sends))
            products(2, i)
            own_links.append(send_edge(k, own, 2, True))
        for t in range(3):
            products(t, 1)
        time_links = []
        for k in (1, 0):
            far_links[k].wait_recv()
            for f in range(2):
                total[k, f] = (
                    value(far + f, inner_rows[k]) + got[k, far + f].astype(jnp.float32)
                ).astype(jnp.bfloat16)
            link = Link(total.at[k], got_time.at[k], sems, 4 + k, to, sends, receives)
            link.start()
            time_links.append(link)
        for k, link in zip((1, 0), time_links):
            for f in range(2):
                inner[k, f] = value(own + f, inner_rows[k])
            own_links[k].wait_recv()
            link.wait_recv()
            finish(
                k,
                [
                    inner[k, f] + got[k, own + f].astype(jnp.float32) + got_time[k, f].astype(jnp.float32)
                    for f in range(2)
                ],
            )
        return far_links + own_links + time_links

    own_x, far_x = pl.ds(2, 2), pl.ds(0, 2)
    own_g, far_g = pl.ds(0, 2), pl.ds(2, 2)
    seg_sems = (s_seg, r_seg)
    x_links, g_links = [], []
    for k in range(2):
        place = inner_rows[k]
        x_links.append(
            Link(sect_ref.at[:, place - 1], xp.at[own_x, place], seg_sems, k, other, encodes, decodes)
        )
        g_links.append(
            Link(back_ref.at[:, place - 1], gp.at[own_g, place], seg_sems, 2 + k, other, decodes, encodes)
        )
    def straight(src, buf, own, far, index, sends, receives, sends_next, receives_next):
        row_ref, place, slot = src.at[:, core], 1 + core, edge_slots[0]
        return [
            Link(row_ref, buf.at[far, place], seg_sems, index, other_next, sends_next, receives_next),
            Link(
                row_ref, buf.at[far, slot], seg_sems, index + 1, other_across_next,
                both(sends_next, border), both(receives_next, border),
            ),
            Link(
                row_ref, buf.at[own, slot], seg_sems, index + 2, other_across,
                both(sends, border), both(receives, border),
            ),
        ]

    x_next = straight(
        sect_ref, xp, own_x, far_x, 4, encodes, decodes, both(encodes, later), both(decodes, earlier)
    )
    g_next = straight(
        back_ref, gp, own_g, far_g, 7, decodes, encodes, both(decodes, earlier), both(encodes, later)
    )

    def gather_g(arrivals, ready, meanwhile, direct=None):
        def early():
            ready()
            upstream_part(EARLY, False)
            meanwhile()

        links = gather(
            gp, own_g, far_g, (s_gp, r_gp), tm_earlier, earlier, later, arrivals, early, direct
        )
        upstream_part(LATE, True)
        keep_upstream()
        for link in links:
            link.wait_send()

    def gather_x(arrivals, ready, direct=None):
        def early():
            ready()
            hidden_part(EARLY, False)

        links = gather(
            xp, own_x, far_x, (s_xp, r_xp), tm_later, later, earlier, arrivals,
            early, direct,
        )
        hidden_part(LATE, True)
        activate()
        for link in links:
            link.wait_send()

    def finish_x(k, sums):
        place = inner_rows[k]
        for f in range(2):
            sect_ref[f, place - 1] = (xp[f + 2, place].astype(jnp.float32) + sums[f]).astype(jnp.bfloat16)
        if k == 0:
            for link in x_next:
                link.start()
        x_links[k].start()

    def finish_g(k, sums):
        place = inner_rows[k]
        for f in range(2):
            back_ref[f, place - 1] = (gp[f, place].astype(jnp.float32) + sums[f]).astype(jnp.bfloat16)
        if k == 0:
            for link in g_next:
                link.start()
        g_links[k].start()

    def widen(source, dest, by):
        def line(n, carry):
            at = pl.ds(pl.multiple_of(n * 128, 128), 128)
            value = source[at].astype(jnp.float32)
            dest[at, 0:256] = shifted(value, by).astype(jnp.bfloat16)
            dest[at, 256:512] = source[at]
            dest[at, 512:768] = shifted(value, -by).astype(jnp.bfloat16)
            return carry

        lax.fori_loop(0, 4, line, 0)

    def prepare():
        widen(act, wide_a, 1)
        for n in range(6):
            act_t[pl.ds(n * 128, 128)] = wide_a[:, pl.ds(n * 128, 128)].T
        for n in range(9):
            icx_t[pl.ds(n * 128, 128)] = icx[:, pl.ds(n * 128, 128)].T

    def out_grad(taps):
        span = pl.ds(PLACES.index(taps[0]) * 128, len(taps) * 128)
        product = jnp.dot(act_t[...], icg[:, span], preferred_element_type=jnp.float32)
        for at, n in enumerate(taps):
            for j in range(3):
                fout[pl.ds((3 * n + j) * 256, 256)] = product[
                    j * 256 : (j + 1) * 256, at * 128 : (at + 1) * 128
                ]

    def in_grad():
        widen(gate, wide_e, -1)
        for group in range(3):
            product = jnp.dot(
                icx_t[pl.ds(group * 384, 384)], wide_e[...], preferred_element_type=jnp.float32
            )
            for i in range(3):
                for j in range(3):
                    fin[pl.ds((3 * PLACES[3 * group + i] + j) * 128, 128)] = product[
                        i * 128 : (i + 1) * 128, j * 256 : (j + 1) * 256
                    ]

    begin_reduce, end_reduce = reduce_scatter(
        fin, fout, in_ref, out_ref, tm, core, at_y, x_at, sibling, across_y, *reduce_refs
    )

    def weights_there():
        load_in.wait()
        load_out.wait()

    @pl.when(encodes)
    def _():
        gather_x(None, weights_there)

    @pl.when(decodes)
    def _():
        gather_g(None, weights_there, lambda: None)
        gather_x([link.wait_recv for link in x_links], lambda: None, x_next)
        gating()
        back_links = scatter(
            gate, True, sent_b, got_b, sum_b, got_zb, (s_sb, r_sb), tm_earlier, earlier, later, finish_g
        )
        window[...] = jnp.zeros_like(window)
        for link in back_links:
            link.wait_send()
        prepare()
        out_grad(EARLY)
        out_grad(LATE)
        in_grad()
        begin_reduce()

    links = scatter(
        act, False, sent_f, got_f, sum_f, got_zf, (s_sf, r_sf), tm_later, later, earlier, finish_x
    )

    @pl.when(encodes)
    def _():
        prepare()
        gather_g(
            [link.wait_recv for link in g_links], lambda: None, lambda: out_grad(EARLY), g_next
        )
        gating()
        out_grad(LATE)
        in_grad()
        begin_reduce()

    store = pltpu.make_async_copy(sect_ref, sect_hbm, s_load.at[4])
    store.start()
    end_reduce()
    store.wait()
    for link in links + x_links + g_links + x_next + g_next:
        link.wait_send()


def reduce_scatter(
    fin, fout, in_ref, out_ref, tm, core, at_y, x_at, sibling, across_y,
    blocks, got_core, half_a, got_a, half_c, got_c, next_a, got_a2, next_c, got_c2,
    own_a, own_c, last, got_z,
    s_core, r_core, s_a, r_a, s_c, r_c, s_a2, r_a2, s_c2, r_c2, s_z, r_z,
):
    f32, bf16 = jnp.float32, jnp.bfloat16

    def made(src, dst, send_sem, recv_sem, device):
        return pltpu.make_async_remote_copy(
            src_ref=src, dst_ref=dst, send_sem=send_sem, recv_sem=recv_sem,
            device_id=device, device_id_type=MESH_ID,
        )

    def x_device(o):
        return {"rows": at_y * (XS * CORES) + x_at(o) * 2 + core}

    def core_copy(q):
        return pltpu.make_async_remote_copy(
            src_ref=blocks.at[q, :, :, 1 - core], dst_ref=got_core.at[q],
            send_sem=s_core.at[q], recv_sem=r_core.at[q],
            device_id=sibling, device_id_type=MESH_ID,
        )

    def pack(q, carry):
        odd = lax.rem(q, 2)
        offset = 4 + (1 - odd) * (q // 2) - odd * ((q + 1) // 2)
        z = lax.rem(tm + offset, ZS)
        ins = fin[pl.ds(pl.multiple_of(z * 432, 16), 432)]
        outs = fout[pl.ds(pl.multiple_of(z * 864, 16), 864)]
        pad = jnp.zeros((CHUNK - 108, 128), f32)
        for k in range(16):
            part = ins[27 * k : 27 * k + 27]
            block = jnp.concatenate([part[:, :128], part[:, 128:], outs[54 * k : 54 * k + 54], pad], axis=0)
            blocks[q, k // 8, k // 2 % 4, k % 2] = block.astype(bf16)
        core_copy(q).start()
        return carry

    def first_copies(h):
        copies = [
            made(half_a.at[h, o], got_a.at[h, o], s_a.at[h, o], r_a.at[h, o], x_device(o)) for o in (2, 1, 3)
        ]
        return copies + [made(half_c.at[h, 1], got_c.at[h], s_c.at[h], r_c.at[h], across_y)]

    def second_copies(h):
        copies = [made(next_a.at[h], got_a2.at[h], s_a2.at[h], r_a2.at[h], across_y)]
        return copies + [
            made(next_c.at[h, o], got_c2.at[h, o], s_c2.at[h, o], r_c2.at[h, o], x_device(o))
            for o in (2, 1, 3)
        ]

    def third_copy(q):
        offset = 4 + q // 2 if q % 2 == 0 else 4 - (q + 1) // 2
        device = {"tm": lax.rem(tm + offset, ZS)}
        return made(last.at[q], got_z.at[q], s_z.at[q], r_z.at[q], device)

    def add_core(q, carry):
        h, n = q // EACH, lax.rem(q, EACH)
        core_copy(q).wait_recv()
        for o in range(XS):
            for y in range(YS):
                x = x_at(o)
                side = lax.rem(at_y + y, 2)
                total = blocks[q, side, x, core].astype(f32) + got_core[q, side, x].astype(f32)
                half_a[h, o, n, y] = total[0:TOP].astype(bf16)
                half_c[h, y, n, o] = total[TOP:CHUNK].astype(bf16)
        return carry

    def begin():
        lax.fori_loop(0, 2 * EACH, pack, 0)
        for h in range(PIECES):
            lax.fori_loop(h * EACH, (h + 1) * EACH, add_core, 0)
            for copy in first_copies(h):
                copy.start()
            if h + 2 < PIECES:
                lax.fori_loop((h + 2) * EACH, (h + 3) * EACH, pack, 0)

    def second(h):
        for copy in first_copies(h):
            copy.wait_recv()

        def add_first(n, carry):
            for y in range(YS):
                total = half_a[h, 0, n, y].astype(f32)
                for o in range(1, XS):
                    total = total + got_a[h, o, n, y].astype(f32)
                if y == 0:
                    own_a[h, n] = total
                else:
                    next_a[h, n] = total.astype(bf16)
            for o in range(XS):
                total = half_c[h, 0, n, o].astype(f32) + got_c[h, n, o].astype(f32)
                if o == 0:
                    own_c[h, n] = total
                else:
                    next_c[h, o, n] = total.astype(bf16)
            return carry

        lax.fori_loop(0, EACH, add_first, 0)
        for copy in second_copies(h):
            copy.start()

    def third(h):
        for copy in second_copies(h):
            copy.wait_recv()
        total = None
        for n in range(EACH):
            q = EACH * h + n
            top = own_a[h, n] + got_a2[h, n].astype(f32)
            low = own_c[h, n]
            for o in range(1, XS):
                low = low + got_c2[h, o, n].astype(f32)
            total = jnp.concatenate([top, low], axis=0)
            if q < ZS - 1:
                last[q] = total.astype(bf16)
                third_copy(q).start()
        return total

    def end():
        second(0)
        for h in range(1, PIECES):
            second(h)
            third(h - 1)
        total = third(PIECES - 1)
        for q in range(ZS - 1):
            third_copy(q).wait_recv()
            total = total + got_z[q].astype(f32)
        in_ref[:, 0:128] = total[0:27]
        in_ref[:, 128:256] = total[27:54]
        out_ref[...] = total[54:108]
        for h in range(PIECES):
            for copy in first_copies(h) + second_copies(h):
                copy.wait_send()
        for q in range(ZS - 1):
            third_copy(q).wait_send()

        def drain(q, carry):
            core_copy(q).wait_send()
            return carry

        lax.fori_loop(0, ZS, drain, 0)

    return begin, end


def front(tms, rows_count, clip, cotangent, kernel_in, kernel_out):
    whole = pl.BlockSpec(memory_space=pltpu.VMEM)
    dma = pltpu.SemaphoreType.DMA
    bf16, f32 = jnp.bfloat16, jnp.float32
    vmem = pltpu.VMEM
    tile = (128, 128)
    return pl.pallas_call(
        partial(front_kernel, tms, rows_count),
        out_shape=(
            jax.ShapeDtypeStruct((2, 2) + tile, bf16),
            jax.ShapeDtypeStruct((27, 256), f32),
            jax.ShapeDtypeStruct((54, 128), f32),
        ),
        in_specs=[pl.BlockSpec(memory_space=pl.ANY)] * 4,
        out_specs=(pl.BlockSpec(memory_space=pl.ANY), whole, whole),
        scratch_shapes=[
            vmem((2, 2) + tile, bf16),
            vmem((9, 3, 128, 256), bf16),
            vmem((9, 3, 256, 128), bf16),
            dma((5,)),
            vmem((2, 2) + tile, bf16),
            vmem((4, 4) + tile, bf16),
            vmem((4, 4) + tile, bf16),
            vmem((512, 1152), bf16),
            vmem((512, 1152), bf16),
            vmem((3, 512, 256), f32),
            vmem((512, 256), f32),
            vmem((512, 256), f32),
            vmem((512, 256), bf16),
            vmem((512, 256), bf16),
            vmem((4, 4, 128, 384), f32),
            vmem((2, 2) + tile, f32),
        ]
        + [vmem((2, 4) + tile, bf16), vmem((2, 4) + tile, bf16), vmem((2, 2) + tile, bf16), vmem((2, 2) + tile, bf16)] * 2
        + [
            vmem((512, 768), bf16),
            vmem((512, 768), bf16),
            vmem((768, 512), bf16),
            vmem((1152, 512), bf16),
            vmem((3456, 256), f32),
            vmem((6912, 128), f32),
            dma((6,)), dma((6,)), dma((6,)), dma((6,)), dma((6,)), dma((6,)), dma((6,)), dma((6,)), dma((10,)), dma((10,)),
            vmem((ZS, YS, XS, CORES, CHUNK, 128), bf16),
            vmem((ZS, YS, XS, CHUNK, 128), bf16),
            vmem((PIECES, XS, EACH, YS, TOP, 128), bf16),
            vmem((PIECES, XS, EACH, YS, TOP, 128), bf16),
            vmem((PIECES, YS, EACH, XS, CHUNK - TOP, 128), bf16),
            vmem((PIECES, EACH, XS, CHUNK - TOP, 128), bf16),
            vmem((PIECES, EACH, TOP, 128), bf16),
            vmem((PIECES, EACH, TOP, 128), bf16),
            vmem((PIECES, XS, EACH, CHUNK - TOP, 128), bf16),
            vmem((PIECES, XS, EACH, CHUNK - TOP, 128), bf16),
            vmem((PIECES, EACH, TOP, 128), f32),
            vmem((PIECES, EACH, CHUNK - TOP, 128), f32),
            vmem((ZS, CHUNK, 128), bf16),
            vmem((ZS, CHUNK, 128), bf16),
            dma((ZS,)), dma((ZS,)), dma((PIECES, XS)), dma((PIECES, XS)), dma((PIECES,)), dma((PIECES,)),
            dma((PIECES,)), dma((PIECES,)), dma((PIECES, XS)), dma((PIECES, XS)), dma((ZS,)), dma((ZS,)),
        ],
        compiler_params=pltpu.CompilerParams(
            collective_id=1, has_side_effects=True, vmem_limit_bytes=56 << 20
        ),
    )(clip, cotangent, kernel_in, kernel_out)


def hand_over_kernel(sect_ref, in_ref, out_ref, sect_out, in_out, out_out):
    sect_out[...] = sect_ref[...]
    for k in range(27):
        in_out[:, pl.ds(256 * k, 256)] = in_ref[pl.ds(k, 1)]
    for k in range(54):
        out_out[:, pl.ds(128 * k, 128)] = out_ref[pl.ds(k, 1)]


def hand_over(sections, in_sum, out_sum):
    whole = pl.BlockSpec(memory_space=pltpu.VMEM)
    return pl.pallas_call(
        hand_over_kernel,
        out_shape=(
            jax.ShapeDtypeStruct(sections.shape, sections.dtype),
            jax.ShapeDtypeStruct((1, 6912), jnp.float32),
            jax.ShapeDtypeStruct((1, 6912), jnp.float32),
        ),
        in_specs=[whole] * 3,
        out_specs=(whole,) * 3,
    )(sections, in_sum, out_sum)


def on_device(tms, rows_count, input_clip, cotangent, kernel_in, kernel_out):
    sections, in_sum, out_sum = front(
        tms, rows_count, input_clip, cotangent,
        kernel_in.reshape(9, 3, 128, 256), kernel_out.reshape(9, 3, 256, 128),
    )
    sections, in_sum, out_sum = hand_over(sections, in_sum, out_sum)
    return (sections[None], in_sum, out_sum)


def solution(mesh):
    in_specs = (
        P("tm", "rows", None, None),
        P("tm", "rows", None, None),
        P("segment", None, None),
        P("segment", None, None),
    )
    out_specs = (
        P("segment", "tm", "rows", None, None),
        P("segment", ("tm", "rows")),
        P("segment", ("tm", "rows")),
    )
    return jax.shard_map(
        partial(on_device, mesh.shape["tm"], mesh.shape["rows"]),
        mesh=mesh, in_specs=in_specs, out_specs=out_specs, check_vma=False,
    )
```

```python
from functools import partial

import jax
import jax.numpy as jnp
from jax import lax
from jax.experimental import pallas as pl
from jax.experimental.pallas import tpu as pltpu
from jax.sharding import PartitionSpec as P

MESH_ID = pl.DeviceIdType.MESH
CORES, XS, YS, ZS = 2, 4, 2, 8
CHUNK = 112


TOP = 56
PIECES = 4
EACH = ZS // PIECES
EARLY, LATE = (6, 7, 8, 1, 4), (0, 2, 3, 5)
PLACES = EARLY + LATE


def shifted(line, by):
    rows = lax.broadcasted_iota(jnp.int32, line.shape, 0)
    if by == 1:
        return jnp.where(rows == 0, 0.0, pltpu.roll(line, 1, 0))
    return jnp.where(rows == 127, 0.0, pltpu.roll(line, 127, 0))


def joined(low, mid, high, reverse):
    if reverse:
        return shifted(low, -1) + mid + shifted(high, 1)
    return shifted(low, 1) + mid + shifted(high, -1)


class Link:
    def __init__(self, src, dst, sems, index, device, sends, receives):
        self.parts = (src, dst, sems[0].at[index], sems[1].at[index], device)
        self.sends = sends
        self.receives = receives

    def copy(self):
        src, dst, send_sem, recv_sem, device = self.parts
        return pltpu.make_async_remote_copy(
            src_ref=src, dst_ref=dst, send_sem=send_sem, recv_sem=recv_sem,
            device_id=device, device_id_type=MESH_ID,
        )

    def start(self):
        @pl.when(self.sends)
        def _():
            self.copy().start()

    def wait_recv(self):
        @pl.when(self.receives)
        def _():
            self.copy().wait_recv()

    def wait_send(self):
        @pl.when(self.sends)
        def _():
            self.copy().wait_send()


def front_kernel(
    tms, rows_count, x_hbm, g_hbm, kin_hbm, kout_hbm, sect_hbm, in_ref, out_ref,
    sect_ref, corner_x, kin_ref, kout_ref, s_load, back_ref, xp, gp, icx, icg, acc, slope, dgrad, act, gate, window, inner,
    sent_f, got_f, sum_f, got_zf, sent_b, got_b, sum_b, got_zb,
    wide_e, wide_a, act_t, icx_t, fin, fout,
    s_xp, r_xp, s_gp, r_gp, s_sf, r_sf, s_sb, r_sb, s_seg, r_seg,
    *reduce_refs,
):
    seg = lax.axis_index("segment")
    tm = lax.axis_index("tm")
    row = lax.axis_index("rows")
    encodes = seg == 0
    decodes = seg == 1
    later, earlier = tm + 1 < tms, tm > 0
    tm_later = {"tm": lax.rem(tm + 1, tms)}
    tm_earlier = {"tm": lax.rem(tm + tms - 1, tms)}
    other = {"segment": 1 - seg}
    other_next = {"segment": 1 - seg, "tm": lax.rem(tm + tms + 1 - 2 * seg, tms)}
    both = jnp.logical_and
    core, at_x, at_y = lax.rem(row, 2), lax.rem(row // 2, XS), row // (XS * CORES)

    step = 2 * core - 1
    crosses = both(row + step >= 0, row + step < rows_count)
    across_row = lax.rem(row + step + rows_count, rows_count)
    across = {"rows": across_row}
    border = both(crosses, at_y != across_row // (XS * CORES))
    inside = jnp.logical_not(border)
    other_across = {"segment": 1 - seg, "rows": across_row}
    other_across_past = {
        "segment": 1 - seg, "tm": lax.rem(tm + tms + 2 * seg - 1, tms), "rows": across_row
    }
    other_across_next = {
        "segment": 1 - seg, "tm": lax.rem(tm + tms + 1 - 2 * seg, tms), "rows": across_row
    }

    def x_at(offset):
        return lax.rem(at_x + offset, XS)

    sibling = {"rows": at_y * (XS * CORES) + at_x * 2 + 1 - core}
    across_y = {"rows": (1 - at_y) * (XS * CORES) + at_x * 2 + core}
    across_x = [{"rows": at_y * (XS * CORES) + x_at(o) * 2 + core} for o in range(1, XS)]
    in_time = [{"tm": lax.rem(tm + p, ZS)} for p in range(1, ZS)]
    load_in = pltpu.make_async_copy(kin_hbm, kin_ref, s_load.at[0])
    load_out = pltpu.make_async_copy(kout_hbm, kout_ref, s_load.at[1])
    load_in.start()
    load_out.start()

    xp[...] = jnp.zeros_like(xp)
    gp[...] = jnp.zeros_like(gp)
    got_f[...] = jnp.zeros_like(got_f)
    got_zf[...] = jnp.zeros_like(got_zf)
    got_b[...] = jnp.zeros_like(got_b)
    got_zb[...] = jnp.zeros_like(got_zb)

    load_x = pltpu.make_async_copy(x_hbm, xp.at[2:4, 1:3], s_load.at[2])
    load_corner = pltpu.make_async_copy(x_hbm, corner_x, s_load.at[2])
    load_g = pltpu.make_async_copy(g_hbm, gp.at[0:2, 1:3], s_load.at[3])

    @pl.when(encodes)
    def _():
        load_x.start()

    @pl.when(decodes)
    def _():
        load_corner.start()
        load_g.start()

    barrier = pltpu.get_barrier_semaphore()
    partners = [across, other, other_next, other_across, other_across_next, other_across_past, sibling, across_y] + across_x + in_time
    for partner in partners:
        pl.semaphore_signal(barrier, inc=1, device_id=partner, device_id_type=MESH_ID)
    window[...] = jnp.zeros_like(window)

    @pl.when(encodes)
    def _():
        load_x.wait()

    @pl.when(decodes)
    def _():
        load_corner.wait()
        load_g.wait()

    pl.semaphore_wait(barrier, len(partners))

    inner_rows = (1 + core, 2 - core)
    row_devices = (across, sibling)
    edge_slots = (3 * (1 - core), 3 * core)
    outer_rows = (3 * core, 3 * (1 - core))
    row_exists = (crosses, True)

    def gather(buf, own, far, sems, to, sends, receives, arrivals, early, direct=None, corner=None):
        edges, times, fars = [], [], []
        for k in range(2):
            device, slot = row_devices[k], edge_slots[k]
            exists = both(row_exists[k], inside) if direct and k == 0 else row_exists[k]
            edges.append(
                Link(buf.at[own, inner_rows[k]], buf.at[own, slot], sems, k, device, exists, exists)
            )
            times.append(
                Link(buf.at[own, inner_rows[k]], buf.at[far, inner_rows[k]], sems, 2 + k, to, sends, receives)
            )
            crossing = both(exists, receives)
            fars.append(
                Link(buf.at[far, inner_rows[k]], buf.at[far, slot], sems, 4 + k, device, crossing, crossing)
            )
        if direct:
            arrivals[1]()
            times[1].start()
            edges[1].start()
            direct[0].wait_recv()
            fars[0].start()
            arrivals[0]()
            edges[0].start()
            times[1].wait_recv()
            fars[1].start()
        elif corner:
            for k in (1, 0):
                times[k].start()
                edges[1 - k].start()
            times[1].wait_recv()
            fars[1].start()
            times[0].wait_recv()
            fars = [corner, fars[1]]
        else:
            for k in (0, 1):
                times[k].start()
                edges[k].start()
            for k in (0, 1):
                times[k].wait_recv()
                fars[k].start()
        for link in edges + (direct[2:] if direct else []):
            link.wait_recv()
        early()
        for link in fars + (direct[1:2] if direct else []):
            link.wait_recv()
        return edges + (fars[1:] if corner else fars) + (times[1:] if direct else times)

    def columns(buf, dest, reverse, taps):
        for n in taps:
            t, i = n // 3, n % 3
            a, b = (2 - t, 2 - i) if reverse else (t, i)
            for f in range(2):
                for r in range(2):
                    dest[pl.ds((2 * f + r) * 128, 128), pl.ds(PLACES.index(n) * 128, 128)] = buf[a + f, b + r]

    def conv_part(taps, source, weights_of, contract, add):
        span = pl.ds(PLACES.index(taps[0]) * 128, len(taps) * 128)
        for j in range(3):
            product = lax.dot_general(
                source[:, span], weights_of(taps, j), (((1,), (contract,)), ((), ())),
                preferred_element_type=jnp.float32,
            )
            acc[j] = acc[j] + product if add else product

    def hidden_part(taps, add):
        columns(xp, icx, False, taps)
        conv_part(
            taps, icx, lambda ns, j: jnp.concatenate([kin_ref[n, j] for n in ns], axis=0), 0, add
        )

    def upstream_part(taps, add):
        columns(gp, icg, True, taps)
        conv_part(
            taps, icg, lambda ns, j: jnp.concatenate([kout_ref[n, j] for n in ns], axis=1), 1, add
        )

    def activate():
        def line(n, carry):
            at = pl.ds(pl.multiple_of(n * 128, 128), 128)
            value = joined(acc[0, at], acc[1, at], acc[2, at], False)
            sigmoid = 1.0 / (1.0 + jnp.exp(-value))
            slope[at] = sigmoid * (1.0 + value * (1.0 - sigmoid))
            act[at] = (value * sigmoid).astype(jnp.bfloat16)
            return carry

        lax.fori_loop(0, 4, line, 0)

    def keep_upstream():
        def line(n, carry):
            at = pl.ds(pl.multiple_of(n * 128, 128), 128)
            dgrad[at] = joined(acc[0, at], acc[1, at], acc[2, at], True)
            return carry

        lax.fori_loop(0, 4, line, 0)

    def gating():
        def line(n, carry):
            at = pl.ds(pl.multiple_of(n * 128, 128), 128)
            gate[at] = (dgrad[at] * slope[at]).astype(jnp.bfloat16)
            return carry

        lax.fori_loop(0, 4, line, 0)

    def scatter(source, reverse, sent, got, total, got_time, sems, to, sends, receives, finish):
        own, far = (2, 0) if reverse else (0, 2)
        first = 2 * core if reverse else 2 - 2 * core

        def products(t, i):
            n = 3 * t + i
            if reverse:
                product = lax.dot_general(
                    source[...], kin_ref[n].reshape(384, 256), (((1,), (1,)), ((), ())),
                    preferred_element_type=jnp.float32,
                )
                a, b = t, i
            else:
                weights = jnp.concatenate([kout_ref[n, j] for j in range(3)], axis=1)
                product = jnp.dot(source[...], weights, preferred_element_type=jnp.float32)
                a, b = 2 - t, 2 - i
            for f in range(2):
                for r in range(2):
                    window[a + f, b + r] += product[(2 * f + r) * 128 : (2 * f + r + 1) * 128]

        def value(f, r):
            return joined(
                window[f, r, :, 0:128], window[f, r, :, 128:256], window[f, r, :, 256:384], reverse
            )

        def send_edge(k, start, index, exists):
            for f in range(2):
                sent[k, start + f] = value(start + f, outer_rows[k]).astype(jnp.bfloat16)
            span = pl.ds(start, 2)
            goes = both(row_exists[k], exists)
            link = Link(sent.at[k, span], got.at[k, span], sems, index + k, row_devices[k], goes, goes)
            link.start()
            return link

        far_links, own_links = [], []
        for k, i in ((0, first), (1, 2 - first)):
            products(0, i)
            products(1, i)
            far_links.append(send_edge(k, far, 0, sends))
            products(2, i)
            own_links.append(send_edge(k, own, 2, True))
        for t in range(3):
            products(t, 1)
        time_links = []
        for k in (1, 0):
            far_links[k].wait_recv()
            for f in range(2):
                total[k, f] = (
                    value(far + f, inner_rows[k]) + got[k, far + f].astype(jnp.float32)
                ).astype(jnp.bfloat16)
            link = Link(total.at[k], got_time.at[k], sems, 4 + k, to, sends, receives)
            link.start()
            time_links.append(link)
        for k, link in zip((1, 0), time_links):
            for f in range(2):
                inner[k, f] = value(own + f, inner_rows[k])
            own_links[k].wait_recv()
            link.wait_recv()
            finish(
                k,
                [
                    inner[k, f] + got[k, own + f].astype(jnp.float32) + got_time[k, f].astype(jnp.float32)
                    for f in range(2)
                ],
            )
        return far_links + own_links + time_links

    own_x, far_x = pl.ds(2, 2), pl.ds(0, 2)
    own_g, far_g = pl.ds(0, 2), pl.ds(2, 2)
    seg_sems = (s_seg, r_seg)
    x_links, g_links = [], []
    for k in range(2):
        place = inner_rows[k]
        x_links.append(
            Link(sect_ref.at[:, place - 1], xp.at[own_x, place], seg_sems, k, other, encodes, decodes)
        )
        g_links.append(
            Link(back_ref.at[:, place - 1], gp.at[own_g, place], seg_sems, 2 + k, other, decodes, encodes)
        )
    def straight(src, buf, own, far, index, sends, receives, sends_next, receives_next):
        row_ref, place, slot = src.at[:, core], 1 + core, edge_slots[0]
        return [
            Link(row_ref, buf.at[far, place], seg_sems, index, other_next, sends_next, receives_next),
            Link(
                row_ref, buf.at[far, slot], seg_sems, index + 1, other_across_next,
                both(sends_next, border), both(receives_next, border),
            ),
            Link(
                row_ref, buf.at[own, slot], seg_sems, index + 2, other_across,
                both(sends, border), both(receives, border),
            ),
        ]

    x_next = straight(
        sect_ref, xp, own_x, far_x, 4, encodes, decodes, both(encodes, later), both(decodes, earlier)
    )
    g_next = straight(
        back_ref, gp, own_g, far_g, 7, decodes, encodes, both(decodes, earlier), both(encodes, later)
    )

    corner = Link(
        corner_x.at[:, core], xp.at[far_x, edge_slots[0]], seg_sems, 10, other_across_past,
        both(both(decodes, crosses), later), both(both(encodes, crosses), earlier),
    )

    def gather_g(arrivals, ready, meanwhile, direct=None):
        def early():
            ready()
            upstream_part(EARLY, False)
            meanwhile()

        links = gather(
            gp, own_g, far_g, (s_gp, r_gp), tm_earlier, earlier, later, arrivals, early, direct
        )
        upstream_part(LATE, True)
        keep_upstream()
        for link in links:
            link.wait_send()

    def gather_x(arrivals, ready, direct=None, corner=None):
        def early():
            ready()
            hidden_part(EARLY, False)

        links = gather(
            xp, own_x, far_x, (s_xp, r_xp), tm_later, later, earlier, arrivals,
            early, direct, corner,
        )
        hidden_part(LATE, True)
        activate()
        for link in links:
            link.wait_send()

    def finish_x(k, sums):
        place = inner_rows[k]
        for f in range(2):
            sect_ref[f, place - 1] = (xp[f + 2, place].astype(jnp.float32) + sums[f]).astype(jnp.bfloat16)
        if k == 0:
            for link in x_next:
                link.start()
        x_links[k].start()

    def finish_g(k, sums):
        place = inner_rows[k]
        for f in range(2):
            back_ref[f, place - 1] = (gp[f, place].astype(jnp.float32) + sums[f]).astype(jnp.bfloat16)
        if k == 0:
            for link in g_next:
                link.start()
        g_links[k].start()

    def widen(source, dest, by):
        def line(n, carry):
            at = pl.ds(pl.multiple_of(n * 128, 128), 128)
            value = source[at].astype(jnp.float32)
            dest[at, 0:256] = shifted(value, by).astype(jnp.bfloat16)
            dest[at, 256:512] = source[at]
            dest[at, 512:768] = shifted(value, -by).astype(jnp.bfloat16)
            return carry

        lax.fori_loop(0, 4, line, 0)

    def prepare():
        widen(act, wide_a, 1)
        for n in range(6):
            act_t[pl.ds(n * 128, 128)] = wide_a[:, pl.ds(n * 128, 128)].T
        for n in range(9):
            icx_t[pl.ds(n * 128, 128)] = icx[:, pl.ds(n * 128, 128)].T

    def out_grad(taps):
        span = pl.ds(PLACES.index(taps[0]) * 128, len(taps) * 128)
        product = jnp.dot(act_t[...], icg[:, span], preferred_element_type=jnp.float32)
        for at, n in enumerate(taps):
            for j in range(3):
                fout[pl.ds((3 * n + j) * 256, 256)] = product[
                    j * 256 : (j + 1) * 256, at * 128 : (at + 1) * 128
                ]

    def in_grad():
        widen(gate, wide_e, -1)
        for group in range(3):
            product = jnp.dot(
                icx_t[pl.ds(group * 384, 384)], wide_e[...], preferred_element_type=jnp.float32
            )
            for i in range(3):
                for j in range(3):
                    fin[pl.ds((3 * PLACES[3 * group + i] + j) * 128, 128)] = product[
                        i * 128 : (i + 1) * 128, j * 256 : (j + 1) * 256
                    ]

    begin_reduce, end_reduce = reduce_scatter(
        fin, fout, in_ref, out_ref, tm, core, at_y, x_at, sibling, across_y, *reduce_refs
    )

    def weights_there():
        load_in.wait()
        load_out.wait()

    @pl.when(encodes)
    def _():
        gather_x(None, weights_there, None, corner)

    @pl.when(decodes)
    def _():
        corner.start()
        gather_g(None, weights_there, lambda: None)
        gather_x([link.wait_recv for link in x_links], lambda: None, x_next)
        gating()
        back_links = scatter(
            gate, True, sent_b, got_b, sum_b, got_zb, (s_sb, r_sb), tm_earlier, earlier, later, finish_g
        )
        window[...] = jnp.zeros_like(window)
        for link in back_links:
            link.wait_send()
        prepare()
        out_grad(EARLY)
        out_grad(LATE)
        in_grad()
        begin_reduce()

    links = scatter(
        act, False, sent_f, got_f, sum_f, got_zf, (s_sf, r_sf), tm_later, later, earlier, finish_x
    )

    @pl.when(encodes)
    def _():
        prepare()
        gather_g(
            [link.wait_recv for link in g_links], lambda: None, lambda: out_grad(EARLY), g_next
        )
        gating()
        out_grad(LATE)
        in_grad()
        begin_reduce()

    store = pltpu.make_async_copy(sect_ref, sect_hbm, s_load.at[4])
    store.start()
    end_reduce()
    store.wait()
    for link in links + x_links + g_links + x_next + g_next + [corner]:
        link.wait_send()


def reduce_scatter(
    fin, fout, in_ref, out_ref, tm, core, at_y, x_at, sibling, across_y,
    blocks, got_core, half_a, got_a, half_c, got_c, next_a, got_a2, next_c, got_c2,
    own_a, own_c, last, got_z,
    s_core, r_core, s_a, r_a, s_c, r_c, s_a2, r_a2, s_c2, r_c2, s_z, r_z,
):
    f32, bf16 = jnp.float32, jnp.bfloat16

    def made(src, dst, send_sem, recv_sem, device):
        return pltpu.make_async_remote_copy(
            src_ref=src, dst_ref=dst, send_sem=send_sem, recv_sem=recv_sem,
            device_id=device, device_id_type=MESH_ID,
        )

    def x_device(o):
        return {"rows": at_y * (XS * CORES) + x_at(o) * 2 + core}

    def core_copy(q):
        return pltpu.make_async_remote_copy(
            src_ref=blocks.at[q, :, :, 1 - core], dst_ref=got_core.at[q],
            send_sem=s_core.at[q], recv_sem=r_core.at[q],
            device_id=sibling, device_id_type=MESH_ID,
        )

    def pack(q, carry):
        odd = lax.rem(q, 2)
        offset = 4 + (1 - odd) * (q // 2) - odd * ((q + 1) // 2)
        z = lax.rem(tm + offset, ZS)
        ins = fin[pl.ds(pl.multiple_of(z * 432, 16), 432)]
        outs = fout[pl.ds(pl.multiple_of(z * 864, 16), 864)]
        pad = jnp.zeros((CHUNK - 108, 128), f32)
        for k in range(16):
            part = ins[27 * k : 27 * k + 27]
            block = jnp.concatenate([part[:, :128], part[:, 128:], outs[54 * k : 54 * k + 54], pad], axis=0)
            blocks[q, k // 8, k // 2 % 4, k % 2] = block.astype(bf16)
        core_copy(q).start()
        return carry

    def first_copies(h):
        copies = [
            made(half_a.at[h, o], got_a.at[h, o], s_a.at[h, o], r_a.at[h, o], x_device(o)) for o in (2, 1, 3)
        ]
        return copies + [made(half_c.at[h, 1], got_c.at[h], s_c.at[h], r_c.at[h], across_y)]

    def second_copies(h):
        copies = [made(next_a.at[h], got_a2.at[h], s_a2.at[h], r_a2.at[h], across_y)]
        return copies + [
            made(next_c.at[h, o], got_c2.at[h, o], s_c2.at[h, o], r_c2.at[h, o], x_device(o))
            for o in (2, 1, 3)
        ]

    def third_copy(q):
        offset = 4 + q // 2 if q % 2 == 0 else 4 - (q + 1) // 2
        device = {"tm": lax.rem(tm + offset, ZS)}
        return made(last.at[q], got_z.at[q], s_z.at[q], r_z.at[q], device)

    def add_core(q, carry):
        h, n = q // EACH, lax.rem(q, EACH)
        core_copy(q).wait_recv()
        for o in range(XS):
            for y in range(YS):
                x = x_at(o)
                side = lax.rem(at_y + y, 2)
                total = blocks[q, side, x, core].astype(f32) + got_core[q, side, x].astype(f32)
                half_a[h, o, n, y] = total[0:TOP].astype(bf16)
                half_c[h, y, n, o] = total[TOP:CHUNK].astype(bf16)
        return carry

    def begin():
        lax.fori_loop(0, 2 * EACH, pack, 0)
        for h in range(PIECES):
            lax.fori_loop(h * EACH, (h + 1) * EACH, add_core, 0)
            for copy in first_copies(h):
                copy.start()
            if h + 2 < PIECES:
                lax.fori_loop((h + 2) * EACH, (h + 3) * EACH, pack, 0)

    def second(h):
        for copy in first_copies(h):
            copy.wait_recv()

        def add_first(n, carry):
            for y in range(YS):
                total = half_a[h, 0, n, y].astype(f32)
                for o in range(1, XS):
                    total = total + got_a[h, o, n, y].astype(f32)
                if y == 0:
                    own_a[h, n] = total
                else:
                    next_a[h, n] = total.astype(bf16)
            for o in range(XS):
                total = half_c[h, 0, n, o].astype(f32) + got_c[h, n, o].astype(f32)
                if o == 0:
                    own_c[h, n] = total
                else:
                    next_c[h, o, n] = total.astype(bf16)
            return carry

        lax.fori_loop(0, EACH, add_first, 0)
        for copy in second_copies(h):
            copy.start()

    def third(h):
        for copy in second_copies(h):
            copy.wait_recv()
        total = None
        for n in range(EACH):
            q = EACH * h + n
            top = own_a[h, n] + got_a2[h, n].astype(f32)
            low = own_c[h, n]
            for o in range(1, XS):
                low = low + got_c2[h, o, n].astype(f32)
            total = jnp.concatenate([top, low], axis=0)
            if q < ZS - 1:
                last[q] = total.astype(bf16)
                third_copy(q).start()
        return total

    def end():
        second(0)
        for h in range(1, PIECES):
            second(h)
            third(h - 1)
        total = third(PIECES - 1)
        for q in range(ZS - 1):
            third_copy(q).wait_recv()
            total = total + got_z[q].astype(f32)
        in_ref[:, 0:128] = total[0:27]
        in_ref[:, 128:256] = total[27:54]
        out_ref[...] = total[54:108]
        for h in range(PIECES):
            for copy in first_copies(h) + second_copies(h):
                copy.wait_send()
        for q in range(ZS - 1):
            third_copy(q).wait_send()

        def drain(q, carry):
            core_copy(q).wait_send()
            return carry

        lax.fori_loop(0, ZS, drain, 0)

    return begin, end


def front(tms, rows_count, clip, cotangent, kernel_in, kernel_out):
    whole = pl.BlockSpec(memory_space=pltpu.VMEM)
    dma = pltpu.SemaphoreType.DMA
    bf16, f32 = jnp.bfloat16, jnp.float32
    vmem = pltpu.VMEM
    tile = (128, 128)
    return pl.pallas_call(
        partial(front_kernel, tms, rows_count),
        out_shape=(
            jax.ShapeDtypeStruct((2, 2) + tile, bf16),
            jax.ShapeDtypeStruct((27, 256), f32),
            jax.ShapeDtypeStruct((54, 128), f32),
        ),
        in_specs=[pl.BlockSpec(memory_space=pl.ANY)] * 4,
        out_specs=(pl.BlockSpec(memory_space=pl.ANY), whole, whole),
        scratch_shapes=[
            vmem((2, 2) + tile, bf16),
            vmem((2, 2) + tile, bf16),
            vmem((9, 3, 128, 256), bf16),
            vmem((9, 3, 256, 128), bf16),
            dma((5,)),
            vmem((2, 2) + tile, bf16),
            vmem((4, 4) + tile, bf16),
            vmem((4, 4) + tile, bf16),
            vmem((512, 1152), bf16),
            vmem((512, 1152), bf16),
            vmem((3, 512, 256), f32),
            vmem((512, 256), f32),
            vmem((512, 256), f32),
            vmem((512, 256), bf16),
            vmem((512, 256), bf16),
            vmem((4, 4, 128, 384), f32),
            vmem((2, 2) + tile, f32),
        ]
        + [vmem((2, 4) + tile, bf16), vmem((2, 4) + tile, bf16), vmem((2, 2) + tile, bf16), vmem((2, 2) + tile, bf16)] * 2
        + [
            vmem((512, 768), bf16),
            vmem((512, 768), bf16),
            vmem((768, 512), bf16),
            vmem((1152, 512), bf16),
            vmem((3456, 256), f32),
            vmem((6912, 128), f32),
            dma((6,)), dma((6,)), dma((6,)), dma((6,)), dma((6,)), dma((6,)), dma((6,)), dma((6,)), dma((11,)), dma((11,)),
            vmem((ZS, YS, XS, CORES, CHUNK, 128), bf16),
            vmem((ZS, YS, XS, CHUNK, 128), bf16),
            vmem((PIECES, XS, EACH, YS, TOP, 128), bf16),
            vmem((PIECES, XS, EACH, YS, TOP, 128), bf16),
            vmem((PIECES, YS, EACH, XS, CHUNK - TOP, 128), bf16),
            vmem((PIECES, EACH, XS, CHUNK - TOP, 128), bf16),
            vmem((PIECES, EACH, TOP, 128), bf16),
            vmem((PIECES, EACH, TOP, 128), bf16),
            vmem((PIECES, XS, EACH, CHUNK - TOP, 128), bf16),
            vmem((PIECES, XS, EACH, CHUNK - TOP, 128), bf16),
            vmem((PIECES, EACH, TOP, 128), f32),
            vmem((PIECES, EACH, CHUNK - TOP, 128), f32),
            vmem((ZS, CHUNK, 128), bf16),
            vmem((ZS, CHUNK, 128), bf16),
            dma((ZS,)), dma((ZS,)), dma((PIECES, XS)), dma((PIECES, XS)), dma((PIECES,)), dma((PIECES,)),
            dma((PIECES,)), dma((PIECES,)), dma((PIECES, XS)), dma((PIECES, XS)), dma((ZS,)), dma((ZS,)),
        ],
        compiler_params=pltpu.CompilerParams(
            collective_id=1, has_side_effects=True, vmem_limit_bytes=56 << 20
        ),
    )(clip, cotangent, kernel_in, kernel_out)


def hand_over_kernel(sect_ref, in_ref, out_ref, sect_out, in_out, out_out):
    sect_out[...] = sect_ref[...]
    for k in range(27):
        in_out[:, pl.ds(256 * k, 256)] = in_ref[pl.ds(k, 1)]
    for k in range(54):
        out_out[:, pl.ds(128 * k, 128)] = out_ref[pl.ds(k, 1)]


def hand_over(sections, in_sum, out_sum):
    whole = pl.BlockSpec(memory_space=pltpu.VMEM)
    return pl.pallas_call(
        hand_over_kernel,
        out_shape=(
            jax.ShapeDtypeStruct(sections.shape, sections.dtype),
            jax.ShapeDtypeStruct((1, 6912), jnp.float32),
            jax.ShapeDtypeStruct((1, 6912), jnp.float32),
        ),
        in_specs=[whole] * 3,
        out_specs=(whole,) * 3,
    )(sections, in_sum, out_sum)


def on_device(tms, rows_count, input_clip, cotangent, kernel_in, kernel_out):
    sections, in_sum, out_sum = front(
        tms, rows_count, input_clip, cotangent,
        kernel_in.reshape(9, 3, 128, 256), kernel_out.reshape(9, 3, 256, 128),
    )
    sections, in_sum, out_sum = hand_over(sections, in_sum, out_sum)
    return (sections[None], in_sum, out_sum)


def solution(mesh):
    in_specs = (
        P("tm", "rows", None, None),
        P("tm", "rows", None, None),
        P("segment", None, None),
        P("segment", None, None),
    )
    out_specs = (
        P("segment", "tm", "rows", None, None),
        P("segment", ("tm", "rows")),
        P("segment", ("tm", "rows")),
    )
    return jax.shard_map(
        partial(on_device, mesh.shape["tm"], mesh.shape["rows"]),
        mesh=mesh, in_specs=in_specs, out_specs=out_specs, check_vma=False,
    )
```

```python
from functools import partial

import jax
import jax.numpy as jnp
from jax import lax
from jax.experimental import pallas as pl
from jax.experimental.pallas import tpu as pltpu
from jax.sharding import PartitionSpec as P

MESH_ID = pl.DeviceIdType.MESH
CORES, XS, YS, ZS = 2, 4, 2, 8
CHUNK = 112


TOP = 56
PIECES = 4
EACH = ZS // PIECES
EARLY, LATE = (6, 7, 8, 1, 4), (0, 2, 3, 5)
PLACES = EARLY + LATE


def shifted(line, by):
    rows = lax.broadcasted_iota(jnp.int32, line.shape, 0)
    if by == 1:
        return jnp.where(rows == 0, 0.0, pltpu.roll(line, 1, 0))
    return jnp.where(rows == 127, 0.0, pltpu.roll(line, 127, 0))


def joined(low, mid, high, reverse):
    if reverse:
        return shifted(low, -1) + mid + shifted(high, 1)
    return shifted(low, 1) + mid + shifted(high, -1)


class Link:
    def __init__(self, src, dst, sems, index, device, sends, receives):
        self.parts = (src, dst, sems[0].at[index], sems[1].at[index], device)
        self.sends = sends
        self.receives = receives

    def copy(self):
        src, dst, send_sem, recv_sem, device = self.parts
        return pltpu.make_async_remote_copy(
            src_ref=src, dst_ref=dst, send_sem=send_sem, recv_sem=recv_sem,
            device_id=device, device_id_type=MESH_ID,
        )

    def start(self):
        @pl.when(self.sends)
        def _():
            self.copy().start()

    def wait_recv(self):
        @pl.when(self.receives)
        def _():
            self.copy().wait_recv()

    def wait_send(self):
        @pl.when(self.sends)
        def _():
            self.copy().wait_send()


def front_kernel(
    tms, rows_count, x_hbm, g_hbm, kin_hbm, kout_hbm, sect_hbm, in_ref, out_ref,
    sect_ref, corner_x, kin_ref, kout_ref, s_load, back_ref, xp, gp, icx, icg, acc, slope, dgrad, act, gate, window, inner,
    sent_f, got_f, sum_f, got_zf, sent_b, got_b, sum_b, got_zb,
    wide_e, wide_a, act_t, icx_t, fin, fout,
    s_xp, r_xp, s_gp, r_gp, s_sf, r_sf, s_sb, r_sb, s_seg, r_seg,
    *reduce_refs,
):
    seg = lax.axis_index("segment")
    tm = lax.axis_index("tm")
    row = lax.axis_index("rows")
    encodes = seg == 0
    decodes = seg == 1
    later, earlier = tm + 1 < tms, tm > 0
    tm_later = {"tm": lax.rem(tm + 1, tms)}
    tm_earlier = {"tm": lax.rem(tm + tms - 1, tms)}
    other = {"segment": 1 - seg}
    other_next = {"segment": 1 - seg, "tm": lax.rem(tm + tms + 1 - 2 * seg, tms)}
    both = jnp.logical_and
    core, at_x, at_y = lax.rem(row, 2), lax.rem(row // 2, XS), row // (XS * CORES)

    step = 2 * core - 1
    crosses = both(row + step >= 0, row + step < rows_count)
    across_row = lax.rem(row + step + rows_count, rows_count)
    across = {"rows": across_row}
    border = both(crosses, at_y != across_row // (XS * CORES))
    inside = jnp.logical_not(border)
    other_across = {"segment": 1 - seg, "rows": across_row}
    other_across_past = {
        "segment": 1 - seg, "tm": lax.rem(tm + tms + 2 * seg - 1, tms), "rows": across_row
    }
    other_across_next = {
        "segment": 1 - seg, "tm": lax.rem(tm + tms + 1 - 2 * seg, tms), "rows": across_row
    }

    def x_at(offset):
        return lax.rem(at_x + offset, XS)

    sibling = {"rows": at_y * (XS * CORES) + at_x * 2 + 1 - core}
    across_y = {"rows": (1 - at_y) * (XS * CORES) + at_x * 2 + core}
    across_x = [{"rows": at_y * (XS * CORES) + x_at(o) * 2 + core} for o in range(1, XS)]
    in_time = [{"tm": lax.rem(tm + p, ZS)} for p in range(1, ZS)]
    load_in = pltpu.make_async_copy(kin_hbm, kin_ref, s_load.at[0])
    load_out = pltpu.make_async_copy(kout_hbm, kout_ref, s_load.at[1])
    load_in.start()
    load_out.start()

    xp[...] = jnp.zeros_like(xp)
    gp[...] = jnp.zeros_like(gp)
    got_f[...] = jnp.zeros_like(got_f)
    got_zf[...] = jnp.zeros_like(got_zf)
    got_b[...] = jnp.zeros_like(got_b)
    got_zb[...] = jnp.zeros_like(got_zb)

    load_x = pltpu.make_async_copy(x_hbm, xp.at[2:4, 1:3], s_load.at[2])
    load_corner = pltpu.make_async_copy(x_hbm, corner_x, s_load.at[2])
    load_g = pltpu.make_async_copy(g_hbm, gp.at[0:2, 1:3], s_load.at[3])

    @pl.when(encodes)
    def _():
        load_x.start()

    @pl.when(decodes)
    def _():
        load_corner.start()
        load_g.start()

    barrier = pltpu.get_barrier_semaphore()
    partners = in_time + across_x + [across_y, other_across_next, other_across_past, other_across, other_next, other, across, sibling]
    for partner in partners:
        pl.semaphore_signal(barrier, inc=1, device_id=partner, device_id_type=MESH_ID)
    window[...] = jnp.zeros_like(window)

    @pl.when(encodes)
    def _():
        load_x.wait()

    @pl.when(decodes)
    def _():
        load_corner.wait()
        load_g.wait()

    pl.semaphore_wait(barrier, len(partners))

    inner_rows = (1 + core, 2 - core)
    row_devices = (across, sibling)
    edge_slots = (3 * (1 - core), 3 * core)
    outer_rows = (3 * core, 3 * (1 - core))
    row_exists = (crosses, True)

    def gather(buf, own, far, sems, to, sends, receives, arrivals, early, direct=None, corner=None):
        edges, times, fars = [], [], []
        for k in range(2):
            device, slot = row_devices[k], edge_slots[k]
            exists = both(row_exists[k], inside) if direct and k == 0 else row_exists[k]
            edges.append(
                Link(buf.at[own, inner_rows[k]], buf.at[own, slot], sems, k, device, exists, exists)
            )
            times.append(
                Link(buf.at[own, inner_rows[k]], buf.at[far, inner_rows[k]], sems, 2 + k, to, sends, receives)
            )
            crossing = both(exists, receives)
            fars.append(
                Link(buf.at[far, inner_rows[k]], buf.at[far, slot], sems, 4 + k, device, crossing, crossing)
            )
        if direct:
            arrivals[1]()
            times[1].start()
            edges[1].start()
            direct[0].wait_recv()
            fars[0].start()
            arrivals[0]()
            edges[0].start()
            times[1].wait_recv()
            fars[1].start()
        elif corner:
            for k in (1, 0):
                times[k].start()
                edges[1 - k].start()
            times[1].wait_recv()
            fars[1].start()
            times[0].wait_recv()
            fars = [corner, fars[1]]
        else:
            for k in (0, 1):
                times[k].start()
                edges[k].start()
            for k in (0, 1):
                times[k].wait_recv()
                fars[k].start()
        for link in edges + (direct[2:] if direct else []):
            link.wait_recv()
        early()
        for link in fars + (direct[1:2] if direct else []):
            link.wait_recv()
        return edges + (fars[1:] if corner else fars) + (times[1:] if direct else times)

    def columns(buf, dest, reverse, taps):
        for n in taps:
            t, i = n // 3, n % 3
            a, b = (2 - t, 2 - i) if reverse else (t, i)
            for f in range(2):
                for r in range(2):
                    dest[pl.ds((2 * f + r) * 128, 128), pl.ds(PLACES.index(n) * 128, 128)] = buf[a + f, b + r]

    def conv_part(taps, source, weights_of, contract, add):
        span = pl.ds(PLACES.index(taps[0]) * 128, len(taps) * 128)
        for j in range(3):
            product = lax.dot_general(
                source[:, span], weights_of(taps, j), (((1,), (contract,)), ((), ())),
                preferred_element_type=jnp.float32,
            )
            acc[j] = acc[j] + product if add else product

    def hidden_part(taps, add):
        columns(xp, icx, False, taps)
        conv_part(
            taps, icx, lambda ns, j: jnp.concatenate([kin_ref[n, j] for n in ns], axis=0), 0, add
        )

    def upstream_part(taps, add):
        columns(gp, icg, True, taps)
        conv_part(
            taps, icg, lambda ns, j: jnp.concatenate([kout_ref[n, j] for n in ns], axis=1), 1, add
        )

    def activate():
        def line(n, carry):
            at = pl.ds(pl.multiple_of(n * 128, 128), 128)
            value = joined(acc[0, at], acc[1, at], acc[2, at], False)
            sigmoid = 1.0 / (1.0 + jnp.exp(-value))
            slope[at] = sigmoid * (1.0 + value * (1.0 - sigmoid))
            act[at] = (value * sigmoid).astype(jnp.bfloat16)
            return carry

        lax.fori_loop(0, 4, line, 0)

    def keep_upstream():
        def line(n, carry):
            at = pl.ds(pl.multiple_of(n * 128, 128), 128)
            dgrad[at] = joined(acc[0, at], acc[1, at], acc[2, at], True)
            return carry

        lax.fori_loop(0, 4, line, 0)

    def gating():
        def line(n, carry):
            at = pl.ds(pl.multiple_of(n * 128, 128), 128)
            gate[at] = (dgrad[at] * slope[at]).astype(jnp.bfloat16)
            return carry

        lax.fori_loop(0, 4, line, 0)

    def scatter(source, reverse, sent, got, total, got_time, sems, to, sends, receives, finish):
        own, far = (2, 0) if reverse else (0, 2)
        first = 2 * core if reverse else 2 - 2 * core

        def products(t, i):
            n = 3 * t + i
            if reverse:
                product = lax.dot_general(
                    source[...], kin_ref[n].reshape(384, 256), (((1,), (1,)), ((), ())),
                    preferred_element_type=jnp.float32,
                )
                a, b = t, i
            else:
                weights = jnp.concatenate([kout_ref[n, j] for j in range(3)], axis=1)
                product = jnp.dot(source[...], weights, preferred_element_type=jnp.float32)
                a, b = 2 - t, 2 - i
            for f in range(2):
                for r in range(2):
                    window[a + f, b + r] += product[(2 * f + r) * 128 : (2 * f + r + 1) * 128]

        def value(f, r):
            return joined(
                window[f, r, :, 0:128], window[f, r, :, 128:256], window[f, r, :, 256:384], reverse
            )

        def send_edge(k, start, index, exists):
            for f in range(2):
                sent[k, start + f] = value(start + f, outer_rows[k]).astype(jnp.bfloat16)
            span = pl.ds(start, 2)
            goes = both(row_exists[k], exists)
            link = Link(sent.at[k, span], got.at[k, span], sems, index + k, row_devices[k], goes, goes)
            link.start()
            return link

        far_links, own_links = [], []
        for k, i in ((0, first), (1, 2 - first)):
            products(0, i)
            products(1, i)
            far_links.append(send_edge(k, far, 0, sends))
        for k, i in ((0, first), (1, 2 - first)):
            products(2, i)
            own_links.append(send_edge(k, own, 2, True))
        for t in range(3):
            products(t, 1)
        time_links = []
        for k in (1, 0):
            far_links[k].wait_recv()
            for f in range(2):
                total[k, f] = (
                    value(far + f, inner_rows[k]) + got[k, far + f].astype(jnp.float32)
                ).astype(jnp.bfloat16)
            link = Link(total.at[k], got_time.at[k], sems, 4 + k, to, sends, receives)
            link.start()
            time_links.append(link)
        for k, link in zip((1, 0), time_links):
            for f in range(2):
                inner[k, f] = value(own + f, inner_rows[k])
            own_links[k].wait_recv()
            link.wait_recv()
            finish(
                k,
                [
                    inner[k, f] + got[k, own + f].astype(jnp.float32) + got_time[k, f].astype(jnp.float32)
                    for f in range(2)
                ],
            )
        return far_links + own_links + time_links

    own_x, far_x = pl.ds(2, 2), pl.ds(0, 2)
    own_g, far_g = pl.ds(0, 2), pl.ds(2, 2)
    seg_sems = (s_seg, r_seg)
    x_links, g_links = [], []
    for k in range(2):
        place = inner_rows[k]
        x_links.append(
            Link(sect_ref.at[:, place - 1], xp.at[own_x, place], seg_sems, k, other, encodes, decodes)
        )
        g_links.append(
            Link(back_ref.at[:, place - 1], gp.at[own_g, place], seg_sems, 2 + k, other, decodes, encodes)
        )
    def straight(src, buf, own, far, index, sends, receives, sends_next, receives_next):
        row_ref, place, slot = src.at[:, core], 1 + core, edge_slots[0]
        return [
            Link(row_ref, buf.at[far, place], seg_sems, index, other_next, sends_next, receives_next),
            Link(
                row_ref, buf.at[far, slot], seg_sems, index + 1, other_across_next,
                both(sends_next, border), both(receives_next, border),
            ),
            Link(
                row_ref, buf.at[own, slot], seg_sems, index + 2, other_across,
                both(sends, border), both(receives, border),
            ),
        ]

    x_next = straight(
        sect_ref, xp, own_x, far_x, 4, encodes, decodes, both(encodes, later), both(decodes, earlier)
    )
    g_next = straight(
        back_ref, gp, own_g, far_g, 7, decodes, encodes, both(decodes, earlier), both(encodes, later)
    )

    corner = Link(
        corner_x.at[:, core], xp.at[far_x, edge_slots[0]], seg_sems, 10, other_across_past,
        both(both(decodes, crosses), later), both(both(encodes, crosses), earlier),
    )

    def gather_g(arrivals, ready, meanwhile, direct=None):
        def early():
            ready()
            upstream_part(EARLY, False)
            meanwhile()

        links = gather(
            gp, own_g, far_g, (s_gp, r_gp), tm_earlier, earlier, later, arrivals, early, direct
        )
        upstream_part(LATE, True)
        keep_upstream()
        for link in links:
            link.wait_send()

    def gather_x(arrivals, ready, direct=None, corner=None):
        def early():
            ready()
            hidden_part(EARLY, False)

        links = gather(
            xp, own_x, far_x, (s_xp, r_xp), tm_later, later, earlier, arrivals,
            early, direct, corner,
        )
        hidden_part(LATE, True)
        activate()
        for link in links:
            link.wait_send()

    def finish_x(k, sums):
        place = inner_rows[k]
        for f in range(2):
            sect_ref[f, place - 1] = (xp[f + 2, place].astype(jnp.float32) + sums[f]).astype(jnp.bfloat16)
        if k == 0:
            for link in x_next:
                link.start()
        x_links[k].start()

    def finish_g(k, sums):
        place = inner_rows[k]
        for f in range(2):
            back_ref[f, place - 1] = (gp[f, place].astype(jnp.float32) + sums[f]).astype(jnp.bfloat16)
        if k == 0:
            for link in g_next:
                link.start()
        g_links[k].start()

    def widen(source, dest, by):
        def line(n, carry):
            at = pl.ds(pl.multiple_of(n * 128, 128), 128)
            value = source[at].astype(jnp.float32)
            dest[at, 0:256] = shifted(value, by).astype(jnp.bfloat16)
            dest[at, 256:512] = source[at]
            dest[at, 512:768] = shifted(value, -by).astype(jnp.bfloat16)
            return carry

        lax.fori_loop(0, 4, line, 0)

    def prepare():
        widen(act, wide_a, 1)
        for n in range(6):
            act_t[pl.ds(n * 128, 128)] = wide_a[:, pl.ds(n * 128, 128)].T
        for n in range(9):
            icx_t[pl.ds(n * 128, 128)] = icx[:, pl.ds(n * 128, 128)].T

    def out_grad(taps):
        span = pl.ds(PLACES.index(taps[0]) * 128, len(taps) * 128)
        product = jnp.dot(act_t[...], icg[:, span], preferred_element_type=jnp.float32)
        for at, n in enumerate(taps):
            for j in range(3):
                fout[pl.ds((3 * n + j) * 256, 256)] = product[
                    j * 256 : (j + 1) * 256, at * 128 : (at + 1) * 128
                ]

    def in_grad():
        widen(gate, wide_e, -1)
        for group in range(3):
            product = jnp.dot(
                icx_t[pl.ds(group * 384, 384)], wide_e[...], preferred_element_type=jnp.float32
            )
            for i in range(3):
                for j in range(3):
                    fin[pl.ds((3 * PLACES[3 * group + i] + j) * 128, 128)] = product[
                        i * 128 : (i + 1) * 128, j * 256 : (j + 1) * 256
                    ]

    begin_reduce, end_reduce = reduce_scatter(
        fin, fout, in_ref, out_ref, tm, core, at_y, x_at, sibling, across_y, *reduce_refs
    )

    def weights_there():
        load_in.wait()
        load_out.wait()

    @pl.when(encodes)
    def _():
        gather_x(None, weights_there, None, corner)

    @pl.when(decodes)
    def _():
        corner.start()
        gather_g(None, weights_there, lambda: None)
        gather_x([link.wait_recv for link in x_links], lambda: None, x_next)
        gating()
        back_links = scatter(
            gate, True, sent_b, got_b, sum_b, got_zb, (s_sb, r_sb), tm_earlier, earlier, later, finish_g
        )
        window[...] = jnp.zeros_like(window)
        for link in back_links:
            link.wait_send()
        prepare()
        out_grad(EARLY)
        out_grad(LATE)
        in_grad()
        begin_reduce()

    links = scatter(
        act, False, sent_f, got_f, sum_f, got_zf, (s_sf, r_sf), tm_later, later, earlier, finish_x
    )

    @pl.when(encodes)
    def _():
        prepare()
        gather_g(
            [link.wait_recv for link in g_links], lambda: None, lambda: out_grad(EARLY), g_next
        )
        gating()
        out_grad(LATE)
        in_grad()
        begin_reduce()

    store = pltpu.make_async_copy(sect_ref, sect_hbm, s_load.at[4])
    store.start()
    end_reduce()
    store.wait()
    for link in links + x_links + g_links + x_next + g_next + [corner]:
        link.wait_send()


def reduce_scatter(
    fin, fout, in_ref, out_ref, tm, core, at_y, x_at, sibling, across_y,
    blocks, got_core, half_a, got_a, half_c, got_c, next_a, got_a2, next_c, got_c2,
    own_a, own_c, last, got_z,
    s_core, r_core, s_a, r_a, s_c, r_c, s_a2, r_a2, s_c2, r_c2, s_z, r_z,
):
    f32, bf16 = jnp.float32, jnp.bfloat16

    def made(src, dst, send_sem, recv_sem, device):
        return pltpu.make_async_remote_copy(
            src_ref=src, dst_ref=dst, send_sem=send_sem, recv_sem=recv_sem,
            device_id=device, device_id_type=MESH_ID,
        )

    def x_device(o):
        return {"rows": at_y * (XS * CORES) + x_at(o) * 2 + core}

    def core_copy(q):
        return pltpu.make_async_remote_copy(
            src_ref=blocks.at[q, :, :, 1 - core], dst_ref=got_core.at[q],
            send_sem=s_core.at[q], recv_sem=r_core.at[q],
            device_id=sibling, device_id_type=MESH_ID,
        )

    def pack(q, carry):
        odd = lax.rem(q, 2)
        offset = 4 + (1 - odd) * (q // 2) - odd * ((q + 1) // 2)
        z = lax.rem(tm + offset, ZS)
        ins = fin[pl.ds(pl.multiple_of(z * 432, 16), 432)]
        outs = fout[pl.ds(pl.multiple_of(z * 864, 16), 864)]
        pad = jnp.zeros((CHUNK - 108, 128), f32)
        for k in range(16):
            part = ins[27 * k : 27 * k + 27]
            block = jnp.concatenate([part[:, :128], part[:, 128:], outs[54 * k : 54 * k + 54], pad], axis=0)
            blocks[q, k // 8, k // 2 % 4, k % 2] = block.astype(bf16)
        core_copy(q).start()
        return carry

    def first_copies(h):
        copies = [made(half_c.at[h, 1], got_c.at[h], s_c.at[h], r_c.at[h], across_y)]
        return copies + [
            made(half_a.at[h, o], got_a.at[h, o], s_a.at[h, o], r_a.at[h, o], x_device(o)) for o in (2, 1, 3)
        ]

    def second_copies(h):
        copies = [made(next_a.at[h], got_a2.at[h], s_a2.at[h], r_a2.at[h], across_y)]
        return copies + [
            made(next_c.at[h, o], got_c2.at[h, o], s_c2.at[h, o], r_c2.at[h, o], x_device(o))
            for o in (2, 1, 3)
        ]

    def third_copy(q):
        offset = 4 + q // 2 if q % 2 == 0 else 4 - (q + 1) // 2
        device = {"tm": lax.rem(tm + offset, ZS)}
        return made(last.at[q], got_z.at[q], s_z.at[q], r_z.at[q], device)

    def add_core(q, carry):
        h, n = q // EACH, lax.rem(q, EACH)
        core_copy(q).wait_recv()
        for o in range(XS):
            for y in range(YS):
                x = x_at(o)
                side = lax.rem(at_y + y, 2)
                total = blocks[q, side, x, core].astype(f32) + got_core[q, side, x].astype(f32)
                half_a[h, o, n, y] = total[0:TOP].astype(bf16)
                half_c[h, y, n, o] = total[TOP:CHUNK].astype(bf16)
        return carry

    def begin():
        lax.fori_loop(0, 2 * EACH, pack, 0)
        for h in range(PIECES):
            lax.fori_loop(h * EACH, (h + 1) * EACH, add_core, 0)
            for copy in first_copies(h):
                copy.start()
            if h + 2 < PIECES:
                lax.fori_loop((h + 2) * EACH, (h + 3) * EACH, pack, 0)

    def second(h):
        for copy in first_copies(h):
            copy.wait_recv()

        def add_first(n, carry):
            for y in range(YS):
                total = half_a[h, 0, n, y].astype(f32)
                for o in range(1, XS):
                    total = total + got_a[h, o, n, y].astype(f32)
                if y == 0:
                    own_a[h, n] = total
                else:
                    next_a[h, n] = total.astype(bf16)
            for o in range(XS):
                total = half_c[h, 0, n, o].astype(f32) + got_c[h, n, o].astype(f32)
                if o == 0:
                    own_c[h, n] = total
                else:
                    next_c[h, o, n] = total.astype(bf16)
            return carry

        lax.fori_loop(0, EACH, add_first, 0)
        for copy in second_copies(h):
            copy.start()

    def third(h):
        for copy in second_copies(h):
            copy.wait_recv()
        total = None
        for n in range(EACH):
            q = EACH * h + n
            top = own_a[h, n] + got_a2[h, n].astype(f32)
            low = own_c[h, n]
            for o in range(1, XS):
                low = low + got_c2[h, o, n].astype(f32)
            total = jnp.concatenate([top, low], axis=0)
            if q < ZS - 1:
                last[q] = total.astype(bf16)
                third_copy(q).start()
        return total

    def end():
        second(0)
        for h in range(1, PIECES):
            second(h)
            third(h - 1)
        total = third(PIECES - 1)
        for q in range(ZS - 1):
            third_copy(q).wait_recv()
            total = total + got_z[q].astype(f32)
        in_ref[:, 0:128] = total[0:27]
        in_ref[:, 128:256] = total[27:54]
        out_ref[...] = total[54:108]
        for h in range(PIECES):
            for copy in first_copies(h) + second_copies(h):
                copy.wait_send()
        for q in range(ZS - 1):
            third_copy(q).wait_send()

        def drain(q, carry):
            core_copy(q).wait_send()
            return carry

        lax.fori_loop(0, ZS, drain, 0)

    return begin, end


def front(tms, rows_count, clip, cotangent, kernel_in, kernel_out):
    whole = pl.BlockSpec(memory_space=pltpu.VMEM)
    dma = pltpu.SemaphoreType.DMA
    bf16, f32 = jnp.bfloat16, jnp.float32
    vmem = pltpu.VMEM
    tile = (128, 128)
    return pl.pallas_call(
        partial(front_kernel, tms, rows_count),
        out_shape=(
            jax.ShapeDtypeStruct((2, 2) + tile, bf16),
            jax.ShapeDtypeStruct((27, 256), f32),
            jax.ShapeDtypeStruct((54, 128), f32),
        ),
        in_specs=[pl.BlockSpec(memory_space=pl.ANY)] * 4,
        out_specs=(pl.BlockSpec(memory_space=pl.ANY), whole, whole),
        scratch_shapes=[
            vmem((2, 2) + tile, bf16),
            vmem((2, 2) + tile, bf16),
            vmem((9, 3, 128, 256), bf16),
            vmem((9, 3, 256, 128), bf16),
            dma((5,)),
            vmem((2, 2) + tile, bf16),
            vmem((4, 4) + tile, bf16),
            vmem((4, 4) + tile, bf16),
            vmem((512, 1152), bf16),
            vmem((512, 1152), bf16),
            vmem((3, 512, 256), f32),
            vmem((512, 256), f32),
            vmem((512, 256), f32),
            vmem((512, 256), bf16),
            vmem((512, 256), bf16),
            vmem((4, 4, 128, 384), f32),
            vmem((2, 2) + tile, f32),
        ]
        + [vmem((2, 4) + tile, bf16), vmem((2, 4) + tile, bf16), vmem((2, 2) + tile, bf16), vmem((2, 2) + tile, bf16)] * 2
        + [
            vmem((512, 768), bf16),
            vmem((512, 768), bf16),
            vmem((768, 512), bf16),
            vmem((1152, 512), bf16),
            vmem((3456, 256), f32),
            vmem((6912, 128), f32),
            dma((6,)), dma((6,)), dma((6,)), dma((6,)), dma((6,)), dma((6,)), dma((6,)), dma((6,)), dma((11,)), dma((11,)),
            vmem((ZS, YS, XS, CORES, CHUNK, 128), bf16),
            vmem((ZS, YS, XS, CHUNK, 128), bf16),
            vmem((PIECES, XS, EACH, YS, TOP, 128), bf16),
            vmem((PIECES, XS, EACH, YS, TOP, 128), bf16),
            vmem((PIECES, YS, EACH, XS, CHUNK - TOP, 128), bf16),
            vmem((PIECES, EACH, XS, CHUNK - TOP, 128), bf16),
            vmem((PIECES, EACH, TOP, 128), bf16),
            vmem((PIECES, EACH, TOP, 128), bf16),
            vmem((PIECES, XS, EACH, CHUNK - TOP, 128), bf16),
            vmem((PIECES, XS, EACH, CHUNK - TOP, 128), bf16),
            vmem((PIECES, EACH, TOP, 128), f32),
            vmem((PIECES, EACH, CHUNK - TOP, 128), f32),
            vmem((ZS, CHUNK, 128), bf16),
            vmem((ZS, CHUNK, 128), bf16),
            dma((ZS,)), dma((ZS,)), dma((PIECES, XS)), dma((PIECES, XS)), dma((PIECES,)), dma((PIECES,)),
            dma((PIECES,)), dma((PIECES,)), dma((PIECES, XS)), dma((PIECES, XS)), dma((ZS,)), dma((ZS,)),
        ],
        compiler_params=pltpu.CompilerParams(
            collective_id=1, has_side_effects=True, vmem_limit_bytes=56 << 20
        ),
    )(clip, cotangent, kernel_in, kernel_out)


def hand_over_kernel(sect_ref, in_ref, out_ref, sect_out, in_out, out_out):
    sect_out[...] = sect_ref[...]
    for k in range(27):
        in_out[:, pl.ds(256 * k, 256)] = in_ref[pl.ds(k, 1)]
    for k in range(54):
        out_out[:, pl.ds(128 * k, 128)] = out_ref[pl.ds(k, 1)]


def hand_over(sections, in_sum, out_sum):
    whole = pl.BlockSpec(memory_space=pltpu.VMEM)
    return pl.pallas_call(
        hand_over_kernel,
        out_shape=(
            jax.ShapeDtypeStruct(sections.shape, sections.dtype),
            jax.ShapeDtypeStruct((1, 6912), jnp.float32),
            jax.ShapeDtypeStruct((1, 6912), jnp.float32),
        ),
        in_specs=[whole] * 3,
        out_specs=(whole,) * 3,
    )(sections, in_sum, out_sum)


def on_device(tms, rows_count, input_clip, cotangent, kernel_in, kernel_out):
    sections, in_sum, out_sum = front(
        tms, rows_count, input_clip, cotangent,
        kernel_in.reshape(9, 3, 128, 256), kernel_out.reshape(9, 3, 256, 128),
    )
    sections, in_sum, out_sum = hand_over(sections, in_sum, out_sum)
    return (sections[None], in_sum, out_sum)


def solution(mesh):
    in_specs = (
        P("tm", "rows", None, None),
        P("tm", "rows", None, None),
        P("segment", None, None),
        P("segment", None, None),
    )
    out_specs = (
        P("segment", "tm", "rows", None, None),
        P("segment", ("tm", "rows")),
        P("segment", ("tm", "rows")),
    )
    return jax.shard_map(
        partial(on_device, mesh.shape["tm"], mesh.shape["rows"]),
        mesh=mesh, in_specs=in_specs, out_specs=out_specs, check_vma=False,
    )
```
